128 devices in a mesh: row: 16 (over z, y), proto: 8 (over x, core).
Axes of the slice: x: 4, y: 4, z: 4, core: 2. Of those that a mesh axis runs over, the one named last changes fastest.
Arguments:
- embeddings: bfloat16 [4096, 256], P('row')
- queue_feats: bfloat16 [8192, 256], P('row')
- prototypes: bfloat16 [256, 65536], P('row', 'proto')
- crop_image: int32 [4096], P('row'), may hold values from 0 to 511, as said below
- fill_count: int32 [1], replicated, may hold values from 4096 to 8192
Outputs:
- grad_embed: float32 [4096, 256], P('row')
- grad_proto: float32 [256, 65536], P('row', 'proto')
- loss: float32 [1], replicated
The draws below stay inside these ranges and needn't reach their ends.
Inputs may be any that keep to these rules, and one draw needn't show every extreme that they name: `crop_image`: each image index is named by exactly 8 crops, all within one aligned block of 256 rows (the rows of one device); block b holds images b * 32 to (b + 1) * 32 - 1.
All inputs are finite; a program needn't handle non-finite values.
Results may differ from the reference program's by a relative error of at most 0.002.
Values may be sent and summed in bfloat16 or wider, within the bound.
A program may use at most 64 MiB of HBM per device.

```python
import math
import jax
import jax.numpy as jnp
from jax import lax

D = 256
PROTOS = 65536
CROPS = 8
ITERS = 3
BATCH_DEV = 256
BATCH = 4096
QUEUE = 8192
IMAGES = 512


def common_direction(key):
    return jax.random.normal(jax.random.fold_in(key, 7), (D,), jnp.float32) / math.sqrt(D)


def banded_loading(key, count, first):
    position = jnp.arange(count, dtype=jnp.float32)
    jitter = jax.random.uniform(jax.random.fold_in(key, first), (count,), jnp.float32, 0.0, 1.0)
    return -1.5 + 3.0 * (position + jitter) / count


def drawn_rows(key, count, first, second):
    direction = common_direction(key)
    along = banded_loading(key, count, first)
    noise = jax.random.normal(jax.random.fold_in(key, second), (count, D), jnp.float32)
    values = along[:, None] * math.sqrt(D) * direction[None, :] + noise
    return values.astype(jnp.bfloat16)


def draw_embeddings(key, part):
    return drawn_rows(key, BATCH, 10, 11)


def draw_queue_feats(key, part):
    return drawn_rows(key, QUEUE, 12, 13)


def draw_prototypes(key, part):
    direction = common_direction(key)
    loading = jax.random.uniform(jax.random.fold_in(key, 8), (PROTOS,), jnp.float32, -0.6, 0.6)
    noise = jax.random.normal(jax.random.fold_in(key, 9), (D, PROTOS), jnp.float32) / math.sqrt(D)
    return (direction[:, None] * loading[None, :] + noise).astype(jnp.bfloat16)


def draw_crop_image(key, part):
    block_total = BATCH // BATCH_DEV
    block_keys = jax.random.split(jax.random.fold_in(key, 21), block_total)
    local_ids = jax.vmap(lambda single: jax.random.permutation(single, BATCH_DEV))(block_keys) // CROPS
    offsets = (jnp.arange(block_total, dtype=jnp.int32) * (BATCH_DEV // CROPS))[:, None]
    return (local_ids.astype(jnp.int32) + offsets).reshape(BATCH).astype(jnp.int32)


def setup_inputs(seed: int = 0) -> dict:
    key_of = jax.random.split(jax.random.key(seed), 6)
    embeddings = draw_embeddings(jax.random.fold_in(key_of[5], 71), 0)
    queue_feats = draw_queue_feats(jax.random.fold_in(key_of[5], 71), 0)
    prototypes = draw_prototypes(jax.random.fold_in(key_of[5], 71), 0)
    crop_image = draw_crop_image(jax.random.fold_in(key_of[5], 71), 0)
    fill_count = jax.random.randint(key_of[4], (1,), QUEUE // 2, QUEUE + 1).astype(jnp.int32)
    return {"embeddings": embeddings, "queue_feats": queue_feats, "prototypes": prototypes, "crop_image": crop_image, "fill_count": fill_count}


ENTROPY_SMOOTHER = 0.05
SOFTMAX_TEMPER = 0.1

def unit_rows(raw):
    values = raw.astype(jnp.float32)
    inverse = lax.rsqrt(lax.optimization_barrier(jnp.sum(values * values, axis=1, keepdims=True)) + 1e-06)
    return (values * inverse, inverse)

def reference(embeddings, queue_feats, prototypes, crop_image, fill_count):
    normed_exact, inverse = unit_rows(embeddings)
    normed = normed_exact.astype(jnp.bfloat16)
    queue_normed = unit_rows(queue_feats)[0].astype(jnp.bfloat16)
    rows_all = jnp.concatenate([normed, queue_normed], axis=0)
    queue_live = (jnp.arange(QUEUE, dtype=jnp.int32) < fill_count[0]).astype(jnp.float32)
    live = jnp.concatenate([jnp.ones((BATCH,), jnp.float32), queue_live])
    block_cols = min(PROTOS, 4096)
    block_count = PROTOS // block_cols
    blocks = prototypes.reshape(D, block_count, block_cols).transpose(1, 0, 2)

    def column_totals(centroid_matrix):

        def column_block(proto_block):
            centroid_similarity = jnp.dot(rows_all, proto_block, preferred_element_type=jnp.float32)
            return lax.optimization_barrier(jnp.sum(jnp.exp(centroid_similarity / ENTROPY_SMOOTHER) * centroid_matrix[:, None], axis=0))
        return lax.map(column_block, blocks).reshape(PROTOS)

    def row_totals(column):

        def row_block(cumulative_accumulator, inputs_pair):
            proto_block, cluster_rescaling = inputs_pair
            centroid_similarity = jnp.dot(rows_all, proto_block, preferred_element_type=jnp.float32)
            return (cumulative_accumulator + lax.optimization_barrier(jnp.sum(jnp.exp(centroid_similarity / ENTROPY_SMOOTHER) * cluster_rescaling[None, :], axis=1)), None)
        row_total, _ = lax.scan(row_block, jnp.zeros((BATCH + QUEUE,), jnp.float32), (blocks, column.reshape(block_count, block_cols)))
        return row_total
    centroid_matrix = live
    column = jnp.zeros((PROTOS,), jnp.float32)
    for sweep_index in range(ITERS):
        column = 1.0 / column_totals(centroid_matrix)
        if sweep_index + 1 < ITERS:
            centroid_matrix = live / row_totals(column)
    column_blocks = column.reshape(block_count, block_cols)

    def totals(cumulative_accumulator, inputs_pair):
        proto_block, cluster_rescaling = inputs_pair
        centroid_similarity = jnp.dot(normed, proto_block, preferred_element_type=jnp.float32)
        allotment_share = lax.optimization_barrier(jnp.sum(jnp.exp(centroid_similarity / ENTROPY_SMOOTHER) * cluster_rescaling[None, :], axis=1))
        softmax_portion = lax.optimization_barrier(jnp.sum(jnp.exp(centroid_similarity / SOFTMAX_TEMPER), axis=1))
        return ((cumulative_accumulator[0] + allotment_share, cumulative_accumulator[1] + softmax_portion), None)
    zeros_batch = jnp.zeros((BATCH,), jnp.float32)
    (overall_mass_sum, softmax_total), _ = lax.scan(totals, (zeros_batch, zeros_batch), (blocks, column_blocks))
    log_grand_total = jnp.log(softmax_total)

    def gradients(cumulative_accumulator, inputs_pair):
        proto_block, cluster_rescaling = inputs_pair
        centroid_similarity = jnp.dot(normed, proto_block, preferred_element_type=jnp.float32)
        cluster_allotment = jnp.exp(centroid_similarity / ENTROPY_SMOOTHER) * cluster_rescaling[None, :] / overall_mass_sum[:, None]
        grouped = jax.ops.segment_sum(cluster_allotment, crop_image, num_segments=IMAGES)
        target_codes = (grouped[crop_image] - cluster_allotment) / (CROPS - 1)
        predicted_probs = jnp.exp(centroid_similarity / SOFTMAX_TEMPER) / softmax_total[:, None]
        logit_gradient = ((predicted_probs - target_codes) / SOFTMAX_TEMPER).astype(jnp.bfloat16)
        loss_portion = jnp.sum(target_codes * (log_grand_total[:, None] - centroid_similarity / SOFTMAX_TEMPER))
        grad_block = lax.dot_general(normed, logit_gradient, (((0,), (0,)), ((), ())), preferred_element_type=jnp.float32)
        normed_part = lax.dot_general(logit_gradient, proto_block, (((1,), (1,)), ((), ())), preferred_element_type=jnp.float32)
        return ((cumulative_accumulator[0] + normed_part, cumulative_accumulator[1] + loss_portion), grad_block)
    (normed_grad, loss_total), grad_blocks = lax.scan(gradients, (jnp.zeros((BATCH, D), jnp.float32), jnp.zeros((), jnp.float32)), (blocks, column_blocks))
    grad_proto = grad_blocks.transpose(1, 0, 2).reshape(D, PROTOS)
    grad_embed = inverse * (normed_grad - normed_exact * lax.optimization_barrier(jnp.sum(normed_exact * normed_grad, axis=1, keepdims=True)))
    loss = (loss_total / BATCH).reshape(1)
    return (grad_embed, grad_proto, loss)
```

```python
import functools
import math

import jax
import jax.numpy as jnp
from jax import lax
from jax.experimental import pallas as pl
from jax.experimental.pallas import tpu as pltpu
from jax.sharding import PartitionSpec as P

MESH = pl.DeviceIdType.MESH
F32 = jnp.float32
BF16 = jnp.bfloat16

CROPS = 8
ITERS = 3
SIDE = 4
LANES = 8
SCALE = 10.0 * math.log2(math.e)

B = 256
Q = 512
R = B + Q
D = 256
TILE = 256
NT = (((1,), (1,)), ((), ()))


def iota(shape, dim):
    return lax.broadcasted_iota(jnp.int32, shape, dim)


def split3(v):
    hi = v.astype(BF16).astype(F32)
    rest = v - hi
    mid = rest.astype(BF16).astype(F32)
    return hi, mid, rest - mid


def stack16(v):
    hi, mid, low = split3(v)
    rid = iota((16, v.shape[1]), 0)
    out = jnp.where(rid == 0, hi, jnp.where(rid == 1, mid, jnp.where(rid == 2, low, 0.0)))
    return out.astype(BF16)


def unit_rows(raw):
    values = raw.astype(F32)
    inverse = lax.rsqrt(jnp.sum(values * values, axis=1, keepdims=True) + 1e-06)
    return values * inverse, inverse


def kernel(
    fill_ref, emb_ref, queue_ref, proto_ref, image_ref,
    ge_ref, gp_ref, loss_ref,
    rows, protos, mass, score, grad, turned, soft_acc, row16, col16, colb,
    col_part, row_part, row_mid, col_in, rowx_in, rowy_in,
    row_soft, row_code, row_log,
    gp_out, gp_in, ng_out, ng_in, ng_all, lx_in, lz_in,
    a_send, a_recv, z_send, z_recv, r_send, r_recv,
    c_send, c_recv, x_send, x_recv, y_send, y_recv,
    g_send, g_recv, n_send, n_recv, h_send, h_recv, lx_send, lx_recv, lz_send, lz_recv,
):
    row = lax.axis_index("row")
    me = lax.axis_index("proto")
    z = row // SIDE
    y = lax.rem(row, SIDE)
    width = protos.shape[1]
    tiles = width // TILE

    def y_peer(d):
        return lax.rem(y + d, SIDE)

    def z_peer(d):
        return lax.rem(z + d, SIDE)

    def p_peer(d):
        return lax.rem(me + d, LANES)

    def remote(src, dst, send, recv, device):
        copy = pltpu.make_async_remote_copy(
            src_ref=src, dst_ref=dst, send_sem=send, recv_sem=recv,
            device_id=device, device_id_type=MESH,
        )
        copy.start()
        return copy

    barrier = pltpu.get_barrier_semaphore()
    count = 0
    for dz in range(SIDE):
        for dy in range(SIDE):
            if dz or dy:
                pl.semaphore_signal(
                    barrier, inc=1, device_id=(z_peer(dz) * SIDE + y_peer(dy), me), device_id_type=MESH
                )
                count += 1
    for dy in range(SIDE):
        for dp in range(1, LANES):
            pl.semaphore_signal(
                barrier, inc=1, device_id=(z * SIDE + y_peer(dy), p_peer(dp)), device_id_type=MESH
            )
            count += 1

    image = image_ref[...].astype(F32)
    wide = jnp.broadcast_to(image, (B, B))
    rid, cid = iota((B, B), 0), iota((B, B), 1)
    tall = jnp.sum(jnp.where(rid == cid, wide, 0.0), axis=1, keepdims=True)
    same = jnp.where(wide == tall, 1.0, 0.0)
    base = (row * (B // CROPS)).astype(F32)
    place = jnp.sum(jnp.where(rid < cid, same, 0.0), axis=0, keepdims=True) * (B // CROPS) + (image - base)
    forward = jnp.where(rid.astype(F32) == place, 1.0, 0.0).astype(BF16)
    exact, _ = unit_rows(emb_ref[...])
    ordered = jnp.dot(forward, exact.astype(BF16), preferred_element_type=F32).astype(BF16)
    rows[y, 0:B, :] = ordered
    rows[y, B:R, :] = unit_rows(queue_ref[...])[0].astype(BF16)
    dims = pl.ds(pl.multiple_of(row * 16, 16), 16)
    protos[dims, :] = proto_ref[:, pl.ds(pl.multiple_of(y * width, width), width)]

    pl.semaphore_wait(barrier, count)

    first = []
    for d in (1, 3, 2):
        first.append(
            remote(
                proto_ref.at[:, pl.ds(pl.multiple_of(y_peer(d) * width, width), width)],
                protos.at[dims, :], a_send.at[d], a_recv.at[d], (z * SIDE + y_peer(d), me),
            )
        )
    row_copies = {}
    for d in (1, 3, 2):
        row_copies[d] = remote(
            rows.at[y], rows.at[y], r_send.at[d], r_recv.at[d], (z * SIDE + y_peer(d), me)
        )
    for copy in first:
        copy.wait()
    second = []
    plane = pl.ds(pl.multiple_of(z * 64, 64), 64)
    for d in (1, 3, 2):
        second.append(
            remote(
                protos.at[plane, :], protos.at[plane, :], z_send.at[d], z_recv.at[d],
                (z_peer(d) * SIDE + y, me),
            )
        )
    soft_acc[...] = jnp.zeros_like(soft_acc)
    col_part[...] = jnp.zeros_like(col_part)
    fill = fill_ref[0]
    for copy in second:
        copy.wait()

    for d in (0, 1, 3, 2):
        if d:
            row_copies[d].wait()
        slot = lax.rem(y + SIDE - d, SIDE)
        lane = iota((16, R), 1)
        first_queue = (z * SIDE + slot) * Q - B
        alive = jnp.logical_or(lane < B, lane + first_queue < fill)
        live16 = jnp.where(jnp.logical_and(alive, iota((16, R), 0) == 0), 1.0, 0.0).astype(BF16)

        def score_tile(j, carry, slot=slot, live16=live16):
            cols = pl.ds(pl.multiple_of(j * TILE, TILE), TILE)
            total = jnp.dot(rows[slot], protos[:, cols], preferred_element_type=F32)
            crop = total[0:B]
            score[slot, :, cols] = crop
            soft = jnp.exp2(crop * SCALE)
            soft_acc[slot] += soft[:, 0:128] + soft[:, 128:256]
            mass[slot, 0:B, cols] = (soft * soft).astype(BF16)
            mass[slot, B:R, cols] = jnp.exp2(total[B:R] * (2.0 * SCALE)).astype(BF16)
            part = jnp.dot(live16, mass[slot, :, cols], preferred_element_type=F32)
            col_part[0, pl.ds(j, 1), :] += part[0:1, :]
            return carry

        lax.fori_loop(0, tiles, score_tile, 0)

    def column_exchange(t):
        copies = []
        for d in (2, 1, 3):
            copies.append(
                remote(
                    col_part.at[t], col_in.at[t, z], c_send.at[t, d], c_recv.at[t, d],
                    (z_peer(d) * SIDE + y, me),
                )
            )
        col_in[t, z] = col_part[t]
        for copy in copies:
            copy.wait()
        column = 1.0 / (col_in[t, 0] + col_in[t, 1] + col_in[t, 2] + col_in[t, 3])
        for j in range(tiles):
            col16[:, j * TILE:(j + 1) * TILE] = stack16(column[j:j + 1, :])
            if t == ITERS - 1:
                colb[:, j * TILE:(j + 1) * TILE] = jnp.broadcast_to(column[j:j + 1, :], (8, TILE))

    def row_exchange(t):
        copies = []
        for d in (4, 3, 5, 2, 6, 1, 7):
            copies.append(
                remote(
                    row_part.at[t], rowx_in.at[t, me], x_send.at[t, d], x_recv.at[t, d],
                    (row, p_peer(d)),
                )
            )
        rowx_in[t, me] = row_part[t]
        for copy in copies:
            copy.wait()
        total = rowx_in[t, 0]
        for k in range(1, LANES):
            total = total + rowx_in[t, k]
        row_mid[t] = total
        copies = []
        for d in (2, 1, 3):
            copies.append(
                remote(
                    row_mid.at[t], rowy_in.at[t, y], y_send.at[t, d], y_recv.at[t, d],
                    (z * SIDE + y_peer(d), me),
                )
            )
        rowy_in[t, y] = total
        for copy in copies:
            copy.wait()
        return rowy_in[t, 0] + rowy_in[t, 1] + rowy_in[t, 2] + rowy_in[t, 3]

    half = R // 2
    rid8, lane8 = iota((8, half), 0), iota((8, half), 1)
    spot = lax.rem(rid8, 2) * half + lane8
    queue_row = (z * SIDE + rid8 // 2) * Q + spot - B
    live = jnp.where(jnp.logical_or(spot < B, queue_row < fill), 1.0, 0.0)

    for t in range(ITERS):
        column_exchange(t)
        if t + 1 == ITERS:
            break

        for slot in range(SIDE):
            part = lax.dot_general(col16[...], mass[slot], NT, preferred_element_type=F32)
            part = jnp.sum(part, axis=0, keepdims=True)
            row_part[t, 2 * slot:2 * slot + 1, :] = part[:, 0:half]
            row_part[t, 2 * slot + 1:2 * slot + 2, :] = part[:, half:R]
        weight = live / row_exchange(t)
        for slot in range(SIDE):
            vector = jnp.concatenate(
                [weight[2 * slot:2 * slot + 1, :], weight[2 * slot + 1:2 * slot + 2, :]], axis=1
            )
            row16[slot] = stack16(vector)

        def column_tile(j, carry, t=t):
            cols = pl.ds(pl.multiple_of(j * TILE, TILE), TILE)
            part = jnp.dot(row16[0], mass[0, :, cols], preferred_element_type=F32)
            for slot in range(1, SIDE):
                part = part + jnp.dot(row16[slot], mass[slot, :, cols], preferred_element_type=F32)
            col_part[t + 1, pl.ds(j, 1), :] = jnp.sum(part, axis=0, keepdims=True)
            return carry

        lax.fori_loop(0, tiles, column_tile, 0)

    last = ITERS - 1
    for slot in range(SIDE):
        part = lax.dot_general(col16[...], mass[slot, 0:B, :], NT, preferred_element_type=F32)
        row_part[last, 2 * slot:2 * slot + 1, 0:B] = jnp.sum(part, axis=0, keepdims=True)
        row_part[last, 2 * slot + 1:2 * slot + 2, 0:B] = jnp.concatenate(
            [
                jnp.sum(soft_acc[slot, 0:128, :].T, axis=0, keepdims=True),
                jnp.sum(soft_acc[slot, 128:256, :].T, axis=0, keepdims=True),
            ],
            axis=1,
        )
        row_part[last, 2 * slot:2 * slot + 2, B:half] = jnp.ones((2, half - B), F32)
        eye = jnp.where(rid == cid, 1.0, 0.0).astype(BF16)
        turned[:, slot * B:(slot + 1) * B] = lax.dot_general(
            eye, rows[slot, 0:B, :], NT, preferred_element_type=F32
        ).astype(BF16)
    sums = row_exchange(last)
    for slot in range(SIDE):
        code = sums[2 * slot:2 * slot + 1, 0:B]
        soft = sums[2 * slot + 1:2 * slot + 2, 0:B]
        for target, value in (
            (row_code, (10.0 / (CROPS - 1)) / code),
            (row_soft, 10.0 / soft),
            (row_log, 0.1 * jnp.log(soft)),
        ):
            for h in range(2):
                target[slot, h * 128:(h + 1) * 128, :] = jnp.broadcast_to(
                    value[:, h * 128:(h + 1) * 128], (128, 128)
                ).T

    images = B // CROPS

    def slope_tile(j, lost):
        cols = pl.ds(pl.multiple_of(j * TILE, TILE), TILE)
        for slot in range(SIDE):
            for h in range(TILE // 128):
                lanes = pl.ds(pl.multiple_of(j * TILE + h * 128, 128), 128)
                column = colb[:, lanes]
                for i in range(images // 8):
                    softs, parts, scores = [], [], []
                    for c in range(CROPS):
                        at = slice(c * images + i * 8, c * images + i * 8 + 8)
                        s = score[slot, at, lanes]
                        e = jnp.exp2(s * SCALE)
                        parts.append(e * e * column * row_code[slot, at, :])
                        softs.append(e * row_soft[slot, at, :])
                        scores.append(row_log[slot, at, :] - s)
                    total = parts[0]
                    for c in range(1, CROPS):
                        total = total + parts[c]
                    for c in range(0, CROPS):
                        at = slice(slot * B + c * images + i * 8, slot * B + c * images + i * 8 + 8)
                        goal = total - parts[c]
                        lost = lost + goal * scores[c]
                        grad[at, lanes] = (softs[c] - goal).astype(BF16)
        gp_out[:, cols] = jnp.dot(turned[...], grad[:, cols], preferred_element_type=F32).astype(BF16)
        return lost

    lost = jnp.zeros((8, 128), F32)
    gp_copies = []
    halves = gp_out.shape[1] // gp_in.shape[-1]
    span = width // halves
    for h in range(halves):
        lost = lax.fori_loop(h * tiles // halves, (h + 1) * tiles // halves, slope_tile, lost)
        n = 0
        for dz, dy in (
            (2, 2), (2, 1), (2, 3), (1, 2), (3, 2), (1, 1), (1, 3), (3, 1), (3, 3),
            (2, 0), (0, 2), (1, 0), (3, 0), (0, 1), (0, 3),
        ):
            peer = z_peer(dz) * SIDE + y_peer(dy)
            gp_copies.append(
                remote(
                    gp_out.at[pl.ds(pl.multiple_of(peer * 16, 16), 16), h * span:(h + 1) * span],
                    gp_in.at[z, y, h], g_send.at[h, n], g_recv.at[h, n], (peer, me),
                )
            )
            n += 1

    lx_in[me] = lost
    loss_copies = []
    for d in range(1, LANES):
        loss_copies.append(
            remote(lx_in.at[me], lx_in.at[me], lx_send.at[d], lx_recv.at[d], (row, p_peer(d)))
        )

    def normed_block(slot, carry):
        block = pl.ds(pl.multiple_of(slot * B, B), B)
        ng_out[slot] = lax.dot_general(grad[block, :], protos[...], NT, preferred_element_type=F32)
        return carry

    lax.fori_loop(0, SIDE, normed_block, 0)
    slab = B // LANES
    ng_copies = []
    n = 0
    for dy in (2, 1, 3, 0):
        for dp in (4, 3, 5, 2, 6, 1, 7, 0):
            if dy == 0 and dp == 0:
                continue
            to_y, to_p = y_peer(dy), p_peer(dp)
            ng_copies.append(
                remote(
                    ng_out.at[to_y, pl.ds(pl.multiple_of(to_p * slab, slab), slab), :],
                    ng_in.at[y * LANES + me], n_send.at[n], n_recv.at[n], (z * SIDE + to_y, to_p),
                )
            )
            n += 1
    ng_in[y * LANES + me] = ng_out[y, pl.ds(pl.multiple_of(me * slab, slab), slab), :]
    for copy in loss_copies:
        copy.wait()
    lost = lx_in[0]
    for k in range(1, LANES):
        lost = lost + lx_in[k]
    lz_in[row] = lost
    loss_copies = []
    n = 0
    for dz in range(SIDE):
        for dy in range(SIDE):
            if dz or dy:
                loss_copies.append(
                    remote(
                        lz_in.at[row], lz_in.at[row], lz_send.at[n], lz_recv.at[n],
                        (z_peer(dz) * SIDE + y_peer(dy), me),
                    )
                )
                n += 1
    for copy in ng_copies:
        copy.wait()
    total = ng_in[0]
    for k in range(1, SIDE * LANES):
        total = total + ng_in[k]
    ng_all[me] = total
    all_copies = []
    for d in (4, 3, 5, 2, 6, 1, 7):
        all_copies.append(
            remote(ng_all.at[me], ng_all.at[me], h_send.at[d], h_recv.at[d], (row, p_peer(d)))
        )

    for copy in loss_copies:
        copy.wait()
    lost = lz_in[0]
    for k in range(1, SIDE * SIDE):
        lost = lost + lz_in[k]
    loss_ref[0] = jnp.sum(lost) * (1.0 / (B * SIDE * SIDE))

    for h in range(halves):
        gp_in[z, y, h] = gp_out[dims, h * span:(h + 1) * span]
    for copy in gp_copies:
        copy.wait()
    for k in range(SIDE):
        for h in range(halves):
            start = k * width + h * span
            gp_ref[:, start:start + span] = (
                gp_in[0, k, h].astype(F32) + gp_in[1, k, h].astype(F32)
                + gp_in[2, k, h].astype(F32) + gp_in[3, k, h].astype(F32)
            )

    for copy in all_copies:
        copy.wait()
    wide = jnp.broadcast_to(image_ref[...].astype(F32), (B, B))
    rid, cid = iota((B, B), 0), iota((B, B), 1)
    tall = jnp.sum(jnp.where(rid == cid, wide, 0.0), axis=1, keepdims=True)
    same = jnp.where(wide == tall, 1.0, 0.0)
    place = jnp.sum(jnp.where(cid < rid, same, 0.0), axis=1, keepdims=True) * (B // CROPS) + (tall - base)
    back = jnp.where(cid.astype(F32) == place, 1.0, 0.0).astype(BF16)
    gathered = ng_all[...].reshape(B, D)
    normed_grad = jnp.zeros((B, D), F32)
    for term in split3(gathered):
        normed_grad = normed_grad + jnp.dot(back, term.astype(BF16), preferred_element_type=F32)
    exact, inverse = unit_rows(emb_ref[...])
    along = jnp.sum(exact * normed_grad, axis=1, keepdims=True)
    ge_ref[...] = inverse * (normed_grad - exact * along)


def body(embeddings, queue_feats, prototypes, crop_image, fill_count):
    width = prototypes.shape[1] // SIDE
    half = R // 2
    halves = 2
    vmem = pl.BlockSpec(memory_space=pltpu.VMEM)
    smem = pl.BlockSpec(memory_space=pltpu.SMEM)
    dma = pltpu.SemaphoreType.DMA
    slab = B // LANES
    scratch = [
        pltpu.VMEM((SIDE, R, D), BF16),
        pltpu.VMEM((D, width), BF16),
        pltpu.VMEM((SIDE, R, width), BF16),
        pltpu.VMEM((SIDE, B, width), F32),
        pltpu.VMEM((SIDE * B, width), BF16),
        pltpu.VMEM((D, SIDE * B), BF16),
        pltpu.VMEM((SIDE, B, 128), F32),
        pltpu.VMEM((SIDE, 16, R), BF16),
        pltpu.VMEM((16, width), BF16),
        pltpu.VMEM((8, width), F32),
        pltpu.VMEM((ITERS, 8, width // 8), F32),
        pltpu.VMEM((ITERS, 8, half), F32),
        pltpu.VMEM((ITERS, 8, half), F32),
        pltpu.VMEM((ITERS, SIDE, 8, width // 8), F32),
        pltpu.VMEM((ITERS, LANES, 8, half), F32),
        pltpu.VMEM((ITERS, SIDE, 8, half), F32),
        pltpu.VMEM((SIDE, B, 128), F32),
        pltpu.VMEM((SIDE, B, 128), F32),
        pltpu.VMEM((SIDE, B, 128), F32),
        pltpu.VMEM((D, width), BF16),
        pltpu.VMEM((SIDE, SIDE, halves, 16, width // halves), BF16),
        pltpu.VMEM((SIDE, B, D), F32),
        pltpu.VMEM((SIDE * LANES, slab, D), F32),
        pltpu.VMEM((LANES, slab, D), F32),
        pltpu.VMEM((LANES, 8, 128), F32),
        pltpu.VMEM((SIDE * SIDE, 8, 128), F32),
        dma((SIDE,)), dma((SIDE,)), dma((SIDE,)), dma((SIDE,)), dma((SIDE,)), dma((SIDE,)),
        dma((ITERS, SIDE)), dma((ITERS, SIDE)), dma((ITERS, LANES)), dma((ITERS, LANES)),
        dma((ITERS, SIDE)), dma((ITERS, SIDE)),
        dma((halves, 15)), dma((halves, 15)), dma((31,)), dma((31,)), dma((LANES,)), dma((LANES,)),
        dma((LANES,)), dma((LANES,)), dma((15,)), dma((15,)),
    ]
    return pl.pallas_call(
        kernel,
        name="swav",
        out_shape=(
            jax.ShapeDtypeStruct((B, D), F32),
            jax.ShapeDtypeStruct((prototypes.shape[0], prototypes.shape[1]), F32),
            jax.ShapeDtypeStruct((1,), F32),
        ),
        in_specs=[smem, vmem, vmem, vmem, vmem],
        out_specs=(vmem, vmem, smem),
        scratch_shapes=scratch,
        compiler_params=pltpu.CompilerParams(
            collective_id=0, has_side_effects=True, vmem_limit_bytes=60 * 1024 * 1024
        ),
    )(fill_count, embeddings, queue_feats, prototypes, crop_image.reshape(1, B))


def solution(mesh):
    placed = (P("row", None), P("row", None), P("row", "proto"), P("row"), P())
    return jax.shard_map(
        body,
        mesh=mesh,
        in_specs=placed,
        out_specs=(P("row", None), P("row", "proto"), P()),
        check_vma=False,
    )
```

```python
import functools
import math

import jax
import jax.numpy as jnp
from jax import lax
from jax.experimental import pallas as pl
from jax.experimental.pallas import tpu as pltpu
from jax.sharding import PartitionSpec as P

MESH = pl.DeviceIdType.MESH
F32 = jnp.float32
BF16 = jnp.bfloat16

CROPS = 8
ITERS = 3
SIDE = 4
LANES = 8
SCALE = 10.0 * math.log2(math.e)

B = 256
Q = 512
R = B + Q
D = 256
TILE = 256
NT = (((1,), (1,)), ((), ()))


def iota(shape, dim):
    return lax.broadcasted_iota(jnp.int32, shape, dim)


def split3(v):
    hi = v.astype(BF16).astype(F32)
    rest = v - hi
    mid = rest.astype(BF16).astype(F32)
    return hi, mid, rest - mid


def stack16(v):
    hi, mid, low = split3(v)
    rid = iota((16, v.shape[1]), 0)
    out = jnp.where(rid == 0, hi, jnp.where(rid == 1, mid, jnp.where(rid == 2, low, 0.0)))
    return out.astype(BF16)


def unit_rows(raw):
    values = raw.astype(F32)
    inverse = lax.rsqrt(jnp.sum(values * values, axis=1, keepdims=True) + 1e-06)
    return values * inverse, inverse


def kernel(
    fill_ref, emb_ref, queue_ref, proto_ref, image_ref,
    ge_ref, gp_ref, loss_ref,
    rows, protos, mass, score, grad, turned, soft_acc, col_acc, alive, row16, col16, colb,
    col_part, row_part, row_pair, row_mid, col_in, rowc_in, rowx_in, rowy_in,
    row_soft, row_code, unit, factor, back,
    gp_out, gp_in, ng_out, ng_in, ng_sum, ngy_in, ng_all, lx_in, lz_in,
    a_send, a_recv, z_send, z_recv, r_send, r_recv, f_send, f_recv,
    c_send, c_recv, s_send, s_recv, x_send, x_recv, y_send, y_recv,
    g_send, g_recv, n_send, n_recv, m_send, m_recv, h_send, h_recv, lx_send, lx_recv, lz_send, lz_recv,
):
    row = lax.axis_index("row")
    me = lax.axis_index("proto")
    z = row // SIDE
    y = lax.rem(row, SIDE)
    core = lax.rem(me, 2)
    chip = me // 2
    sibling = chip * 2 + (1 - core)
    width = protos.shape[1]
    tiles = width // TILE
    chunks = gp_in.shape[2]
    span = width // chunks

    def y_peer(d):
        return lax.rem(y + d, SIDE)

    def z_peer(d):
        return lax.rem(z + d, SIDE)

    def p_peer(d):
        return lax.rem(me + d, LANES)

    def remote(src, dst, send, recv, device):
        copy = pltpu.make_async_remote_copy(
            src_ref=src, dst_ref=dst, send_sem=send, recv_sem=recv,
            device_id=device, device_id_type=MESH,
        )
        copy.start()
        return copy

    barrier = pltpu.get_barrier_semaphore()
    count = 0
    for dz in range(SIDE):
        for dy in range(SIDE):
            if dz or dy:
                pl.semaphore_signal(
                    barrier, inc=1, device_id=(z_peer(dz) * SIDE + y_peer(dy), me), device_id_type=MESH
                )
                count += 1
    for dp in range(1, LANES):
        pl.semaphore_signal(barrier, inc=1, device_id=(row, p_peer(dp)), device_id_type=MESH)
        count += 1
    for dy in range(1, SIDE):
        pl.semaphore_signal(
            barrier, inc=1, device_id=(z * SIDE + y_peer(dy), sibling), device_id_type=MESH
        )
        count += 1

    image = image_ref[...].astype(F32)
    wide = jnp.broadcast_to(image, (B, B))
    rid, cid = iota((B, B), 0), iota((B, B), 1)
    tall = jnp.sum(jnp.where(rid == cid, wide, 0.0), axis=1, keepdims=True)
    same = jnp.where(wide == tall, 1.0, 0.0)
    base = (row * (B // CROPS)).astype(F32)
    place = jnp.sum(jnp.where(rid < cid, same, 0.0), axis=0, keepdims=True) * (B // CROPS) + (image - base)
    forward = jnp.where(rid.astype(F32) == place, 1.0, 0.0).astype(BF16)
    exact, _ = unit_rows(emb_ref[...])
    ordered = jnp.dot(forward, exact.astype(BF16), preferred_element_type=F32).astype(BF16)
    rows[y, 0:B, :] = ordered
    rows[y, B:R, :] = unit_rows(queue_ref[...])[0].astype(BF16)
    dims = pl.ds(pl.multiple_of(row * 16, 16), 16)
    protos[dims, :] = proto_ref[:, pl.ds(pl.multiple_of(y * width, width), width)]

    pl.semaphore_wait(barrier, count)

    first = {}
    for k in range(chunks):
        for d in (1, 3, 2):
            first[k, d] = remote(
                proto_ref.at[:, pl.ds(pl.multiple_of(y_peer(d) * width + k * span, span), span)],
                protos.at[dims, k * span:(k + 1) * span], a_send.at[k, d], a_recv.at[k, d],
                (z * SIDE + y_peer(d), me),
            )
    shared = pl.ds(pl.multiple_of(core * (R // 2), R // 2), R // 2)
    row_copies = {}
    for d in (1, 3, 2):
        row_copies[d] = remote(
            rows.at[y, shared, :], rows.at[y, shared, :], r_send.at[d], r_recv.at[d],
            (z * SIDE + y_peer(d), me),
        )
    second = {}
    plane = pl.ds(pl.multiple_of(z * 64, 64), 64)
    for k in range(chunks):
        for d in (1, 3, 2):
            first[k, d].wait()
        for d in (1, 3, 2):
            part = protos.at[plane, k * span:(k + 1) * span]
            second[k, d] = remote(
                part, part, z_send.at[k, d], z_recv.at[k, d], (z_peer(d) * SIDE + y, me)
            )

    soft_acc[...] = jnp.zeros_like(soft_acc)
    col_acc[...] = jnp.zeros_like(col_acc)
    fill = fill_ref[0]
    for slot in range(SIDE):
        place = (z * SIDE + slot) * Q + iota((Q, 128), 0)
        alive[slot] = jnp.where(place < fill, 1.0, 0.0)
    place = jnp.sum(jnp.where(cid < rid, same, 0.0), axis=1, keepdims=True) * (B // CROPS) + (tall - base)
    back[...] = jnp.where(cid.astype(F32) == place, 1.0, 0.0).astype(BF16)
    exact, inverse = unit_rows(emb_ref[...])
    unit[...] = exact
    factor[...] = jnp.broadcast_to(inverse, (B, 128))

    def score_chunk(slot, k):
        for h in range(span // TILE):
            cols = pl.ds(pl.multiple_of(k * span + h * TILE, TILE), TILE)
            total = jnp.dot(rows[slot], protos[:, cols], preferred_element_type=F32)
            crop = total[0:B] * SCALE
            score[slot, :, cols] = crop
            soft = jnp.exp2(crop)
            soft_acc[slot] += soft[:, 0:128] + soft[:, 128:256]
            code = soft * soft
            mass[slot, 0:B, cols] = code.astype(BF16)
            rest = jnp.exp2(total[B:R] * (2.0 * SCALE))
            mass[slot, B:R, cols] = rest.astype(BF16)
            live = alive[slot]
            for g in range(TILE // 128):
                lanes = slice(g * 128, (g + 1) * 128)
                part = jnp.sum(code[:, lanes].reshape(B // 8, 8, 128), axis=0)
                part = part + jnp.sum((rest[:, lanes] * live).reshape(Q // 8, 8, 128), axis=0)
                at = pl.ds(pl.multiple_of(k * span + h * TILE + g * 128, 128), 128)
                col_acc[:, at] += part

    def score_many(first_slot, slots, first_chunk, many):
        def step(i, carry):
            n = first_slot + i // many
            score_chunk(lax.rem(y + n + n // 2, SIDE), first_chunk + lax.rem(i, many))
            return carry

        lax.fori_loop(0, slots * many, step, 0)

    def z_arrived(k):
        for d in (1, 3, 2):
            second[k, d].wait()

    def score_far(first_chunk, many):
        def step(i, carry):
            score_chunk(y_peer(2), first_chunk + i)
            return carry

        lax.fori_loop(0, many, step, 0)

    def hand_over(d):
        row_copies[d].wait()
        slot = lax.rem(y + SIDE - d, SIDE)
        part = rows.at[slot, shared, :]
        return remote(part, part, f_send.at[d], f_recv.at[d], (row, sibling))

    z_arrived(0)
    score_chunk(y, 0)
    near = [hand_over(1), hand_over(3)]
    z_arrived(1)
    score_chunk(y, 1)
    for copy in near:
        copy.wait()
    score_many(1, 2, 0, 2)
    far = hand_over(2)
    z_arrived(2)
    score_many(0, 3, 2, 1)
    far.wait()
    score_far(0, 3)
    z_arrived(3)
    score_many(0, 3, 3, 1)
    score_far(3, 1)
    for j in range(tiles):
        col_part[0, j:j + 1, :] = jnp.sum(col_acc[:, j * TILE:(j + 1) * TILE], axis=0, keepdims=True)

    def column_exchange(t):
        copies = []
        for d in (2, 1, 3):
            copies.append(
                remote(
                    col_part.at[t], col_in.at[t, z], c_send.at[t, d], c_recv.at[t, d],
                    (z_peer(d) * SIDE + y, me),
                )
            )
        col_in[t, z] = col_part[t]
        for copy in copies:
            copy.wait()
        column = 1.0 / (col_in[t, 0] + col_in[t, 1] + col_in[t, 2] + col_in[t, 3])
        for j in range(tiles):
            col16[:, j * TILE:(j + 1) * TILE] = stack16(column[j:j + 1, :])
            if t == ITERS - 1:
                colb[:, j * TILE:(j + 1) * TILE] = jnp.broadcast_to(column[j:j + 1, :], (8, TILE))

    def row_exchange(t):
        def to_sum(d, c):
            return pltpu.make_async_remote_copy(
                src_ref=row_mid.at[t], dst_ref=rowy_in.at[t, y],
                send_sem=y_send.at[t, d, c], recv_sem=y_recv.at[t, d],
                device_id=(z * SIDE + y_peer(d), chip * 2 + c), device_id_type=MESH,
            )

        to_odd = pltpu.make_async_remote_copy(
            src_ref=row_part.at[t], dst_ref=rowc_in.at[t], send_sem=s_send.at[t], recv_sem=s_recv.at[t],
            device_id=(row, sibling), device_id_type=MESH,
        )

        @pl.when(core == 0)
        def _():
            to_odd.start()
            to_odd.wait_send()
            for d in (0, 1, 3, 2):
                to_sum(d, 0).wait_recv()

        @pl.when(core == 1)
        def _():
            to_odd.wait_recv()
            pair = row_part[t] + rowc_in[t]
            row_pair[t] = pair
            copies = []
            for d in (2, 1, 3):
                copies.append(
                    remote(
                        row_pair.at[t], rowx_in.at[t, chip], x_send.at[t, d], x_recv.at[t, d],
                        (row, lax.rem(chip + d, SIDE) * 2 + core),
                    )
                )
            rowx_in[t, chip] = pair
            for copy in copies:
                copy.wait()
            total = rowx_in[t, 0] + rowx_in[t, 1] + rowx_in[t, 2] + rowx_in[t, 3]
            row_mid[t] = total
            copies = [to_sum(d, c) for d in (2, 1, 3) for c in (0, 1)] + [to_sum(0, 0)]
            for copy in copies:
                copy.start()
            rowy_in[t, y] = total
            for copy in copies:
                copy.wait_send()
            for d in (1, 3, 2):
                to_sum(d, 1).wait_recv()

        return rowy_in[t, 0] + rowy_in[t, 1] + rowy_in[t, 2] + rowy_in[t, 3]

    half = R // 2
    rid8, lane8 = iota((8, half), 0), iota((8, half), 1)
    spot = lax.rem(rid8, 2) * half + lane8
    queue_row = (z * SIDE + rid8 // 2) * Q + spot - B
    live = jnp.where(jnp.logical_or(spot < B, queue_row < fill), 1.0, 0.0)

    for t in range(ITERS):
        column_exchange(t)
        if t + 1 == ITERS:
            break

        for slot in range(SIDE):
            part = lax.dot_general(col16[...], mass[slot], NT, preferred_element_type=F32)
            part = jnp.sum(part, axis=0, keepdims=True)
            row_part[t, 2 * slot:2 * slot + 1, :] = part[:, 0:half]
            row_part[t, 2 * slot + 1:2 * slot + 2, :] = part[:, half:R]
        weight = live / row_exchange(t)
        for slot in range(SIDE):
            vector = jnp.concatenate(
                [weight[2 * slot:2 * slot + 1, :], weight[2 * slot + 1:2 * slot + 2, :]], axis=1
            )
            row16[slot] = stack16(vector)

        def column_tile(j, carry, t=t):
            cols = pl.ds(pl.multiple_of(j * TILE, TILE), TILE)
            part = jnp.dot(row16[0], mass[0, :, cols], preferred_element_type=F32)
            for slot in range(1, SIDE):
                part = part + jnp.dot(row16[slot], mass[slot, :, cols], preferred_element_type=F32)
            col_part[t + 1, pl.ds(j, 1), :] = jnp.sum(part, axis=0, keepdims=True)
            return carry

        lax.fori_loop(0, tiles, column_tile, 0)

    last = ITERS - 1
    for slot in range(SIDE):
        part = lax.dot_general(col16[...], mass[slot, 0:B, :], NT, preferred_element_type=F32)
        row_part[last, 2 * slot:2 * slot + 1, 0:B] = jnp.sum(part, axis=0, keepdims=True)
        row_part[last, 2 * slot + 1:2 * slot + 2, 0:B] = jnp.concatenate(
            [
                jnp.sum(soft_acc[slot, 0:128, :].T, axis=0, keepdims=True),
                jnp.sum(soft_acc[slot, 128:256, :].T, axis=0, keepdims=True),
            ],
            axis=1,
        )
        row_part[last, 2 * slot:2 * slot + 2, B:half] = jnp.ones((2, half - B), F32)
        eye = jnp.where(rid == cid, 1.0, 0.0).astype(BF16)
        turned[:, slot * B:(slot + 1) * B] = lax.dot_general(
            eye, rows[slot, 0:B, :], NT, preferred_element_type=F32
        ).astype(BF16)
    sums = row_exchange(last)
    for slot in range(SIDE):
        code = sums[2 * slot:2 * slot + 1, 0:B]
        soft = sums[2 * slot + 1:2 * slot + 2, 0:B]
        for target, value in ((row_code, (10.0 / (CROPS - 1)) / code), (row_soft, 10.0 / soft)):
            for h in range(2):
                target[slot, h * 128:(h + 1) * 128, :] = jnp.broadcast_to(
                    value[:, h * 128:(h + 1) * 128], (128, 128)
                ).T
    sublane = iota((8, B), 0)
    logs = jnp.log(sums[:, 0:B])
    mine = jnp.logical_and(sublane == 2 * y + 1, me == 0)
    logs = jnp.where(mine, logs, 0.0)
    logs = logs[:, 0:128] + logs[:, 128:256]

    images = B // CROPS
    slab = B // LANES

    def slope_chunk(slot, k, lost):
        for h in range(span // 128):
            lanes = pl.ds(pl.multiple_of(k * span + h * 128, 128), 128)
            column = colb[:, lanes]
            for i in range(images // 8):
                softs, parts, scores = [], [], []
                for c in range(CROPS):
                    at = slice(c * images + i * 8, c * images + i * 8 + 8)
                    s = score[slot, at, lanes]
                    e = jnp.exp2(s)
                    parts.append(e * e * column * row_code[slot, at, :])
                    softs.append(e * row_soft[slot, at, :])
                    scores.append(s)
                total = parts[0]
                for c in range(1, CROPS):
                    total = total + parts[c]
                for c in range(CROPS):
                    at = slice(c * images + i * 8, c * images + i * 8 + 8)
                    goal = total - parts[c]
                    lost = lost + goal * scores[c]
                    grad[slot, at, lanes] = (softs[c] - goal).astype(BF16)
        return lost

    def send_normed(n, slot):
        ng_out[n] = lax.dot_general(grad[slot], protos[...], NT, preferred_element_type=F32)
        copies = []
        for d in (4, 3, 5, 2, 6, 1, 7):
            to_p = p_peer(d)
            copies.append(
                remote(
                    ng_out.at[n, pl.ds(pl.multiple_of(to_p * slab, slab), slab), :],
                    ng_in.at[n, me], n_send.at[n, d], n_recv.at[n, d], (row, to_p),
                )
            )
        ng_in[n, me] = ng_out[n, pl.ds(pl.multiple_of(me * slab, slab), slab), :]
        return copies

    def sum_normed(n, copies):
        for copy in copies:
            copy.wait()
        total = ng_in[n, 0]
        for k in range(1, LANES):
            total = total + ng_in[n, k]
        return total

    def send_protos(k):
        for h in range(span // TILE):
            cols = slice(k * span + h * TILE, k * span + (h + 1) * TILE)
            part = jnp.dot(turned[:, 0:B], grad[0, :, cols], preferred_element_type=F32)
            for other in range(1, SIDE):
                part = part + jnp.dot(
                    turned[:, other * B:(other + 1) * B], grad[other, :, cols],
                    preferred_element_type=F32,
                )
            gp_out[:, cols] = part.astype(BF16)
        copies = []
        for dz, dy in (
            (2, 2), (2, 1), (2, 3), (1, 2), (3, 2), (1, 1), (1, 3), (3, 1), (3, 3),
            (2, 0), (0, 2), (1, 0), (3, 0), (0, 1), (0, 3),
        ):
            peer = z_peer(dz) * SIDE + y_peer(dy)
            m = len(copies)
            copies.append(
                remote(
                    gp_out.at[pl.ds(pl.multiple_of(peer * 16, 16), 16), k * span:(k + 1) * span],
                    gp_in.at[z, y, k], g_send.at[k, m], g_recv.at[k, m], (peer, me),
                )
            )
        return copies

    def pass_normed(n):
        ng_sum[n] = sum_normed(n, waiting[n])
        d = order[n]
        return remote(
            ng_sum.at[n], ngy_in.at[d], m_send.at[d], m_recv.at[d], (z * SIDE + y_peer(d), me)
        )

    order = (2, 1, 3, 0)
    lost = jnp.zeros((8, 128), F32)
    waiting, passing, gp_copies = [], [], []
    for n in range(SIDE):
        slot = y_peer(order[n])
        lost = lax.fori_loop(0, chunks, lambda k, lost, slot=slot: slope_chunk(slot, k, lost), lost)
        waiting.append(send_normed(n, slot))
    lx_in[me] = logs - lost * (math.log(2.0) / 10.0)
    loss_copies = []
    for d in range(1, LANES):
        loss_copies.append(
            remote(lx_in.at[me], lx_in.at[me], lx_send.at[d], lx_recv.at[d], (row, p_peer(d)))
        )
    gp_copies += send_protos(0)
    passing.append(pass_normed(0))
    gp_copies += send_protos(1)
    passing.append(pass_normed(1))
    for copy in loss_copies:
        copy.wait()
    lost = lx_in[0]
    for k in range(1, LANES):
        lost = lost + lx_in[k]
    lz_in[row] = lost
    loss_copies = []
    for dz in range(SIDE):
        for dy in range(SIDE):
            if dz or dy:
                m = len(loss_copies)
                loss_copies.append(
                    remote(
                        lz_in.at[row], lz_in.at[row], lz_send.at[m], lz_recv.at[m],
                        (z_peer(dz) * SIDE + y_peer(dy), me),
                    )
                )
    passing.append(pass_normed(2))
    gp_copies += send_protos(2)
    gp_copies += send_protos(3)
    total = sum_normed(3, waiting[3])
    for copy in passing:
        copy.wait()
    ng_all[me] = total + ngy_in[1] + ngy_in[2] + ngy_in[3]
    all_copies = []
    for d in (4, 3, 5, 2, 6, 1, 7):
        all_copies.append(
            remote(ng_all.at[me], ng_all.at[me], h_send.at[d], h_recv.at[d], (row, p_peer(d)))
        )

    for copy in all_copies:
        copy.wait()
    gathered = ng_all[...].reshape(B, D)
    normed_grad = jnp.zeros((B, D), F32)
    for term in split3(gathered):
        normed_grad = normed_grad + jnp.dot(back[...], term.astype(BF16), preferred_element_type=F32)
    along = jnp.sum(unit[...] * normed_grad, axis=1, keepdims=True)
    rest = normed_grad - unit[...] * along
    for h in range(D // 128):
        ge_ref[:, h * 128:(h + 1) * 128] = factor[...] * rest[:, h * 128:(h + 1) * 128]

    for copy in loss_copies:
        copy.wait()
    lost = lz_in[0]
    for k in range(1, SIDE * SIDE):
        lost = lost + lz_in[k]
    loss_ref[0] = jnp.sum(lost) * (1.0 / (B * SIDE * SIDE))

    for k in range(chunks):
        gp_in[z, y, k] = gp_out[dims, k * span:(k + 1) * span]
    for copy in gp_copies:
        copy.wait()
    for n in range(SIDE):
        for k in range(chunks):
            start = n * width + k * span
            gp_ref[:, start:start + span] = (
                gp_in[0, n, k].astype(F32) + gp_in[1, n, k].astype(F32)
                + gp_in[2, n, k].astype(F32) + gp_in[3, n, k].astype(F32)
            )


def body(embeddings, queue_feats, prototypes, crop_image, fill_count):
    width = prototypes.shape[1] // SIDE
    half = R // 2
    chunks = 4
    vmem = pl.BlockSpec(memory_space=pltpu.VMEM)
    smem = pl.BlockSpec(memory_space=pltpu.SMEM)
    dma = pltpu.SemaphoreType.DMA
    slab = B // LANES

    def pair(*shape):
        return [dma(shape), dma(shape)]

    scratch = [
        pltpu.VMEM((SIDE, R, D), BF16),
        pltpu.VMEM((D, width), BF16),
        pltpu.VMEM((SIDE, R, width), BF16),
        pltpu.VMEM((SIDE, B, width), F32),
        pltpu.VMEM((SIDE, B, width), BF16),
        pltpu.VMEM((D, SIDE * B), BF16),
        pltpu.VMEM((SIDE, B, 128), F32),
        pltpu.VMEM((8, width), F32),
        pltpu.VMEM((SIDE, Q, 128), F32),
        pltpu.VMEM((SIDE, 16, R), BF16),
        pltpu.VMEM((16, width), BF16),
        pltpu.VMEM((8, width), F32),
        pltpu.VMEM((ITERS, 8, width // 8), F32),
        pltpu.VMEM((ITERS, 8, half), F32),
        pltpu.VMEM((ITERS, 8, half), F32),
        pltpu.VMEM((ITERS, 8, half), F32),
        pltpu.VMEM((ITERS, SIDE, 8, width // 8), F32),
        pltpu.VMEM((ITERS, 8, half), F32),
        pltpu.VMEM((ITERS, SIDE, 8, half), F32),
        pltpu.VMEM((ITERS, SIDE, 8, half), F32),
        pltpu.VMEM((SIDE, B, 128), F32),
        pltpu.VMEM((SIDE, B, 128), F32),
        pltpu.VMEM((B, D), F32),
        pltpu.VMEM((B, 128), F32),
        pltpu.VMEM((B, B), BF16),
        pltpu.VMEM((D, width), BF16),
        pltpu.VMEM((SIDE, SIDE, chunks, 16, width // chunks), BF16),
        pltpu.VMEM((SIDE, B, D), F32),
        pltpu.VMEM((SIDE, LANES, slab, D), F32),
        pltpu.VMEM((SIDE, slab, D), F32),
        pltpu.VMEM((SIDE, slab, D), F32),
        pltpu.VMEM((LANES, slab, D), F32),
        pltpu.VMEM((LANES, 8, 128), F32),
        pltpu.VMEM((SIDE * SIDE, 8, 128), F32),
        *pair(chunks, SIDE), *pair(chunks, SIDE), *pair(SIDE), *pair(SIDE),
        *pair(ITERS, SIDE), *pair(ITERS), *pair(ITERS, SIDE),
        dma((ITERS, SIDE, 2)), dma((ITERS, SIDE)),
        *pair(chunks, 15), *pair(SIDE, LANES), *pair(SIDE), *pair(LANES),
        *pair(LANES), *pair(15),
    ]
    return pl.pallas_call(
        kernel,
        name="swav",
        out_shape=(
            pltpu.VMEM((B, D), F32),
            pltpu.VMEM((prototypes.shape[0], prototypes.shape[1]), F32),
            jax.ShapeDtypeStruct((1,), F32),
        ),
        in_specs=[smem, vmem, vmem, vmem, vmem],
        out_specs=(vmem, vmem, smem),
        scratch_shapes=scratch,
        compiler_params=pltpu.CompilerParams(
            collective_id=0, has_side_effects=True, vmem_limit_bytes=60 * 1024 * 1024
        ),
    )(fill_count, embeddings, queue_feats, prototypes, crop_image.reshape(1, B))


def solution(mesh):
    placed = (P("row", None), P("row", None), P("row", "proto"), P("row"), P())
    return jax.shard_map(
        body,
        mesh=mesh,
        in_specs=placed,
        out_specs=(P("row", None), P("row", "proto"), P()),
        check_vma=False,
    )
```

```python
import functools
import math

import jax
import jax.numpy as jnp
from jax import lax
from jax.experimental import pallas as pl
from jax.experimental.pallas import tpu as pltpu
from jax.sharding import PartitionSpec as P

MESH = pl.DeviceIdType.MESH
F32 = jnp.float32
BF16 = jnp.bfloat16

CROPS = 8
ITERS = 3
SIDE = 4
LANES = 8
SCALE = 10.0 * math.log2(math.e)

B = 256
Q = 512
R = B + Q
V = 512
D = 256
TILE = 256
NT = (((1,), (1,)), ((), ()))


def iota(shape, dim):
    return lax.broadcasted_iota(jnp.int32, shape, dim)


def split3(v):
    hi = v.astype(BF16).astype(F32)
    rest = v - hi
    mid = rest.astype(BF16).astype(F32)
    return hi, mid, rest - mid


def stack16(v):
    hi, mid, low = split3(v)
    rid = iota((16, v.shape[1]), 0)
    out = jnp.where(rid == 0, hi, jnp.where(rid == 1, mid, jnp.where(rid == 2, low, 0.0)))
    return out.astype(BF16)


def unit_rows(raw):
    values = raw.astype(F32)
    inverse = lax.rsqrt(jnp.sum(values * values, axis=1, keepdims=True) + 1e-06)
    return values * inverse, inverse


def kernel(
    fill_ref, emb_hbm, queue_hbm, proto_hbm, image_ref,
    ge_ref, gp_ref, loss_ref,
    emb_ref, queue_ref, proto_ref, rows, protos, massf, massb, row_acc, row_wide, score, grad, turned, soft_acc, col_acc, alive, row16, col16, colb,
    col_part, row_part, row_pair, row_mid, col_in, rowc_in, rowx_in, rowy_in,
    row_soft, row_code, unit, factor, back,
    gp_out, gp_in, ng_out, ng_in, ng_sum, ngy_in, ng_all, lx_in, lz_in,
    a_send, a_recv, z_send, z_recv, r_send, r_recv, f_send, f_recv,
    c_send, c_recv, s_send, s_recv, x_send, x_recv, y_send, y_recv,
    g_send, g_recv, n_send, n_recv, m_send, m_recv, h_send, h_recv, lx_send, lx_recv, lz_send, lz_recv, in_sem,
):
    row = lax.axis_index("row")
    me = lax.axis_index("proto")
    z = row // SIDE
    y = lax.rem(row, SIDE)
    core = lax.rem(me, 2)
    chip = me // 2
    sibling = chip * 2 + (1 - core)
    width = protos.shape[1]
    tiles = width // TILE
    chunks = gp_in.shape[2]
    span = width // chunks

    def y_peer(d):
        return lax.rem(y + d, SIDE)

    def z_peer(d):
        return lax.rem(z + d, SIDE)

    def p_peer(d):
        return lax.rem(me + d, LANES)

    def remote(src, dst, send, recv, device):
        copy = pltpu.make_async_remote_copy(
            src_ref=src, dst_ref=dst, send_sem=send, recv_sem=recv,
            device_id=device, device_id_type=MESH,
        )
        copy.start()
        return copy

    loads = []
    for n, (source, target) in enumerate(
        ((emb_hbm, emb_ref), (queue_hbm, queue_ref), (proto_hbm, proto_ref))
    ):
        loads.append(pltpu.make_async_copy(source, target, in_sem.at[n]))
        loads[-1].start()
    barrier = pltpu.get_barrier_semaphore()
    count = 0
    for dz in range(SIDE):
        for dy in range(SIDE):
            if dz or dy:
                pl.semaphore_signal(
                    barrier, inc=1, device_id=(z_peer(dz) * SIDE + y_peer(dy), me), device_id_type=MESH
                )
                count += 1
    for dp in range(1, LANES):
        pl.semaphore_signal(barrier, inc=1, device_id=(row, p_peer(dp)), device_id_type=MESH)
        count += 1
    for dy in range(1, SIDE):
        pl.semaphore_signal(
            barrier, inc=1, device_id=(z * SIDE + y_peer(dy), sibling), device_id_type=MESH
        )
        count += 1

    image = image_ref[...].astype(F32)
    wide = jnp.broadcast_to(image, (B, B))
    rid, cid = iota((B, B), 0), iota((B, B), 1)
    tall = jnp.sum(jnp.where(rid == cid, wide, 0.0), axis=1, keepdims=True)
    same = jnp.where(wide == tall, 1.0, 0.0)
    base = (row * (B // CROPS)).astype(F32)
    place = jnp.sum(jnp.where(rid < cid, same, 0.0), axis=0, keepdims=True) * (B // CROPS) + (image - base)
    forward = jnp.where(rid.astype(F32) == place, 1.0, 0.0).astype(BF16)
    for copy in loads:
        copy.wait()
    exact, _ = unit_rows(emb_ref[...])
    ordered = jnp.dot(forward, exact.astype(BF16), preferred_element_type=F32).astype(BF16)
    rows[y, 0:B, :] = ordered
    rows[y, B:R, :] = unit_rows(queue_ref[...])[0].astype(BF16)
    dims = pl.ds(pl.multiple_of(row * 16, 16), 16)
    protos[dims, :] = proto_ref[:, pl.ds(pl.multiple_of(y * width, width), width)]

    pl.semaphore_wait(barrier, count)

    first = {}
    for k in range(chunks):
        for d in (1, 3, 2):
            first[k, d] = remote(
                proto_ref.at[:, pl.ds(pl.multiple_of(y_peer(d) * width + k * span, span), span)],
                protos.at[dims, k * span:(k + 1) * span], a_send.at[k, d], a_recv.at[k, d],
                (z * SIDE + y_peer(d), me),
            )
    shared = pl.ds(pl.multiple_of(core * (R // 2), R // 2), R // 2)
    row_copies = {}
    for d in (1, 3, 2):
        row_copies[d] = remote(
            rows.at[y, shared, :], rows.at[y, shared, :], r_send.at[d], r_recv.at[d],
            (z * SIDE + y_peer(d), me),
        )
    second = {}

    def to_z(k, source):
        slot = lax.rem(y + SIDE - source, SIDE)
        part = protos.at[pl.ds(pl.multiple_of((z * SIDE + slot) * 16, 16), 16), k * span:(k + 1) * span]
        for d in (1, 3, 2):
            second[k, source, d] = remote(
                part, part, z_send.at[k, source, d], z_recv.at[k, source, d], (z_peer(d) * SIDE + y, me)
            )

    for k in range(chunks):
        to_z(k, 0)
    for k in range(chunks):
        for source in (1, 3, 2):
            first[k, source].wait()
            to_z(k, source)

    soft_acc[...] = jnp.zeros_like(soft_acc)
    col_acc[...] = jnp.zeros_like(col_acc)
    fill = fill_ref[0]
    for slot in range(SIDE):
        place = (z * SIDE + slot) * Q + iota((Q, 128), 0)
        alive[slot] = jnp.where(place < fill, 1.0, 0.0)
    place = jnp.sum(jnp.where(cid < rid, same, 0.0), axis=1, keepdims=True) * (B // CROPS) + (tall - base)
    back[...] = jnp.where(cid.astype(F32) == place, 1.0, 0.0).astype(BF16)
    exact, inverse = unit_rows(emb_ref[...])
    unit[...] = exact
    factor[...] = jnp.broadcast_to(inverse, (B, 128))

    def score_chunk(slot, k):
        for h in range(span // TILE):
            cols = pl.ds(pl.multiple_of(k * span + h * TILE, TILE), TILE)
            total = jnp.dot(rows[slot], protos[:, cols], preferred_element_type=F32)
            crop = total[0:B] * SCALE
            score[slot, :, cols] = crop
            soft = jnp.exp2(crop)
            soft_acc[slot] += soft[:, 0:128] + soft[:, 128:256]
            code = soft * soft
            massf[slot, 0:B, cols] = code
            rest = jnp.exp2(total[B:R] * (2.0 * SCALE))
            massf[slot, B:V, cols] = rest[0:V - B]
            massb[slot, :, cols] = rest[V - B:].astype(BF16)
            live = alive[slot]
            for g in range(TILE // 128):
                lanes = slice(g * 128, (g + 1) * 128)
                part = jnp.sum(code[:, lanes].reshape(B // 8, 8, 128), axis=0)
                part = part + jnp.sum((rest[:, lanes] * live).reshape(Q // 8, 8, 128), axis=0)
                at = pl.ds(pl.multiple_of(k * span + h * TILE + g * 128, 128), 128)
                col_acc[:, at] += part

    def score_many(first_slot, slots, first_chunk, many):
        def step(i, carry):
            n = first_slot + i // many
            score_chunk(lax.rem(y + n + n // 2, SIDE), first_chunk + lax.rem(i, many))
            return carry

        lax.fori_loop(0, slots * many, step, 0)

    def z_arrived(k):
        for source in range(SIDE):
            for d in (1, 3, 2):
                second[k, source, d].wait()

    def score_far(first_chunk, many):
        def step(i, carry):
            score_chunk(y_peer(2), first_chunk + i)
            return carry

        lax.fori_loop(0, many, step, 0)

    def hand_over(d):
        row_copies[d].wait()
        slot = lax.rem(y + SIDE - d, SIDE)
        part = rows.at[slot, shared, :]
        return remote(part, part, f_send.at[d], f_recv.at[d], (row, sibling))

    z_arrived(0)
    score_chunk(y, 0)
    near = [hand_over(1), hand_over(3)]
    z_arrived(1)
    score_chunk(y, 1)
    for copy in near:
        copy.wait()
    score_many(1, 2, 0, 2)
    far = hand_over(2)
    z_arrived(2)
    score_many(0, 3, 2, 1)
    far.wait()
    score_far(0, 3)
    z_arrived(3)
    score_many(0, 3, 3, 1)
    score_far(3, 1)
    for j in range(tiles):
        col_part[0, j:j + 1, :] = jnp.sum(col_acc[:, j * TILE:(j + 1) * TILE], axis=0, keepdims=True)

    def column_exchange(t):
        copies = []
        for d in (2, 1, 3):
            copies.append(
                remote(
                    col_part.at[t], col_in.at[t, z], c_send.at[t, d], c_recv.at[t, d],
                    (z_peer(d) * SIDE + y, me),
                )
            )
        col_in[t, z] = col_part[t]
        for copy in copies:
            copy.wait()
        column = 1.0 / (col_in[t, 0] + col_in[t, 1] + col_in[t, 2] + col_in[t, 3])
        for j in range(tiles):
            col16[:, j * TILE:(j + 1) * TILE] = stack16(column[j:j + 1, :])
            colb[:, j * TILE:(j + 1) * TILE] = jnp.broadcast_to(column[j:j + 1, :], (8, TILE))

    def row_exchange(t):
        def to_sum(d, c):
            return pltpu.make_async_remote_copy(
                src_ref=row_mid.at[t], dst_ref=rowy_in.at[t, y],
                send_sem=y_send.at[t, d, c], recv_sem=y_recv.at[t, d],
                device_id=(z * SIDE + y_peer(d), chip * 2 + c), device_id_type=MESH,
            )

        to_odd = pltpu.make_async_remote_copy(
            src_ref=row_part.at[t], dst_ref=rowc_in.at[t], send_sem=s_send.at[t], recv_sem=s_recv.at[t],
            device_id=(row, sibling), device_id_type=MESH,
        )

        @pl.when(core == 0)
        def _():
            to_odd.start()
            to_odd.wait_send()
            for d in (0, 1, 3, 2):
                to_sum(d, 0).wait_recv()

        @pl.when(core == 1)
        def _():
            to_odd.wait_recv()
            pair = row_part[t] + rowc_in[t]
            row_pair[t] = pair
            copies = []
            for d in (2, 1, 3):
                copies.append(
                    remote(
                        row_pair.at[t], rowx_in.at[t, chip], x_send.at[t, d], x_recv.at[t, d],
                        (row, lax.rem(chip + d, SIDE) * 2 + core),
                    )
                )
            rowx_in[t, chip] = pair
            for copy in copies:
                copy.wait()
            total = rowx_in[t, 0] + rowx_in[t, 1] + rowx_in[t, 2] + rowx_in[t, 3]
            row_mid[t] = total
            copies = [to_sum(d, c) for d in (2, 1, 3) for c in (0, 1)] + [to_sum(0, 0)]
            for copy in copies:
                copy.start()
            rowy_in[t, y] = total
            for copy in copies:
                copy.wait_send()
            for d in (1, 3, 2):
                to_sum(d, 1).wait_recv()

        return rowy_in[t, 0] + rowy_in[t, 1] + rowy_in[t, 2] + rowy_in[t, 3]

    def row_sums(slot, many):
        for g in range(many // 8):
            at = slice(g * 8, g * 8 + 8)
            sums = [None, None]
            for n in range(width // 128):
                lanes = slice(n * 128, (n + 1) * 128)
                term = massf[slot, at, lanes] * colb[:, lanes]
                sums[n % 2] = term if sums[n % 2] is None else sums[n % 2] + term
            row_acc[slot, at, :] = sums[0] + sums[1]

    def turn(slot, b):
        return jnp.sum(row_acc[slot, b * 128:(b + 1) * 128, :].T, axis=0, keepdims=True)

    half = R // 2
    rid8, lane8 = iota((8, half), 0), iota((8, half), 1)
    spot = lax.rem(rid8, 2) * half + lane8
    queue_row = (z * SIDE + rid8 // 2) * Q + spot - B
    live = jnp.where(jnp.logical_or(spot < B, queue_row < fill), 1.0, 0.0)

    for t in range(ITERS):
        column_exchange(t)
        if t + 1 == ITERS:
            break

        def row_block(slot, carry, t=t):
            row_sums(slot, V)
            rest = lax.dot_general(col16[...], massb[slot], NT, preferred_element_type=F32)
            rest = jnp.sum(rest, axis=0, keepdims=True)
            parts = [turn(slot, b) for b in range(V // 128)] + [rest[:, 0:128], rest[:, 128:256]]
            for h in range(2):
                row_part[t, pl.ds(2 * slot + h, 1), :] = jnp.concatenate(parts[3 * h:3 * h + 3], axis=1)
            return carry

        lax.fori_loop(0, SIDE, row_block, 0)
        weight = live / row_exchange(t)
        for slot in range(SIDE):
            row16[slot] = stack16(weight[2 * slot + 1:2 * slot + 2, 128:half])
            for b in range(V // 128):
                at = slice((b % 3) * 128, (b % 3 + 1) * 128)
                line = weight[2 * slot + b // 3:2 * slot + b // 3 + 1, at]
                row_wide[slot, b * 128:(b + 1) * 128, :] = jnp.broadcast_to(line, (128, 128)).T

        def column_block(slot, sums):
            rest = jnp.dot(row16[slot], massb[slot], preferred_element_type=F32)
            sums = list(sums)
            for g in range(V // 8):
                at = slice(g * 8, g * 8 + 8)
                scale = row_wide[slot, at, :]
                for n in range(width // 128):
                    sums[n] = sums[n] + massf[slot, at, n * 128:(n + 1) * 128] * scale
            return tuple(sums[n] + rest[0:8, n * 128:(n + 1) * 128] for n in range(width // 128))

        sums = lax.fori_loop(
            0, SIDE, column_block, tuple(jnp.zeros((8, 128), F32) for _ in range(width // 128))
        )
        for n in range(width // 128):
            at = slice((n % 2) * 128, (n % 2 + 1) * 128)
            col_part[t + 1, n // 2:n // 2 + 1, at] = jnp.sum(sums[n], axis=0, keepdims=True)

    last = ITERS - 1
    for slot in range(SIDE):
        row_sums(slot, B)
        for b in range(B // 128):
            row_part[last, 2 * slot:2 * slot + 1, b * 128:(b + 1) * 128] = turn(slot, b)
        row_part[last, 2 * slot + 1:2 * slot + 2, 0:B] = jnp.concatenate(
            [
                jnp.sum(soft_acc[slot, 0:128, :].T, axis=0, keepdims=True),
                jnp.sum(soft_acc[slot, 128:256, :].T, axis=0, keepdims=True),
            ],
            axis=1,
        )
        row_part[last, 2 * slot:2 * slot + 2, B:half] = jnp.ones((2, half - B), F32)
        eye = jnp.where(rid == cid, 1.0, 0.0).astype(BF16)
        turned[:, slot * B:(slot + 1) * B] = lax.dot_general(
            eye, rows[slot, 0:B, :], NT, preferred_element_type=F32
        ).astype(BF16)
    sums = row_exchange(last)
    for slot in range(SIDE):
        code = sums[2 * slot:2 * slot + 1, 0:B]
        soft = sums[2 * slot + 1:2 * slot + 2, 0:B]
        for target, value in ((row_code, (10.0 / (CROPS - 1)) / code), (row_soft, 10.0 / soft)):
            for h in range(2):
                target[slot, h * 128:(h + 1) * 128, :] = jnp.broadcast_to(
                    value[:, h * 128:(h + 1) * 128], (128, 128)
                ).T
    sublane = iota((8, B), 0)
    logs = jnp.log(sums[:, 0:B])
    mine = jnp.logical_and(sublane == 2 * y + 1, me == 0)
    logs = jnp.where(mine, logs, 0.0)
    logs = logs[:, 0:128] + logs[:, 128:256]

    images = B // CROPS
    slab = B // LANES

    def slope_chunk(slot, k, lost):
        for h in range(span // 128):
            lanes = pl.ds(pl.multiple_of(k * span + h * 128, 128), 128)
            column = colb[:, lanes]
            for i in range(images // 8):
                softs, parts, scores = [], [], []
                for c in range(CROPS):
                    at = slice(c * images + i * 8, c * images + i * 8 + 8)
                    s = score[slot, at, lanes]
                    e = jnp.exp2(s)
                    parts.append(e * e * column * row_code[slot, at, :])
                    softs.append(e * row_soft[slot, at, :])
                    scores.append(s)
                total = parts[0]
                for c in range(1, CROPS):
                    total = total + parts[c]
                for c in range(CROPS):
                    at = slice(c * images + i * 8, c * images + i * 8 + 8)
                    goal = total - parts[c]
                    lost = lost + goal * scores[c]
                    grad[slot, at, lanes] = (softs[c] - goal).astype(BF16)
        return lost

    def send_normed(n, slot):
        ng_out[n] = lax.dot_general(grad[slot], protos[...], NT, preferred_element_type=F32)
        copies = []
        for d in (4, 3, 5, 2, 6, 1, 7):
            to_p = p_peer(d)
            copies.append(
                remote(
                    ng_out.at[n, pl.ds(pl.multiple_of(to_p * slab, slab), slab), :],
                    ng_in.at[n, me], n_send.at[n, d], n_recv.at[n, d], (row, to_p),
                )
            )
        ng_in[n, me] = ng_out[n, pl.ds(pl.multiple_of(me * slab, slab), slab), :]
        return copies

    def sum_normed(n, copies):
        for copy in copies:
            copy.wait()
        total = ng_in[n, 0]
        for k in range(1, LANES):
            total = total + ng_in[n, k]
        return total

    def send_protos(k):
        for h in range(span // TILE):
            cols = slice(k * span + h * TILE, k * span + (h + 1) * TILE)
            part = jnp.dot(turned[:, 0:B], grad[0, :, cols], preferred_element_type=F32)
            for other in range(1, SIDE):
                part = part + jnp.dot(
                    turned[:, other * B:(other + 1) * B], grad[other, :, cols],
                    preferred_element_type=F32,
                )
            gp_out[:, cols] = part.astype(BF16)
        copies = []
        for dz, dy in (
            (2, 2), (2, 1), (2, 3), (1, 2), (3, 2), (1, 1), (1, 3), (3, 1), (3, 3),
            (2, 0), (0, 2), (1, 0), (3, 0), (0, 1), (0, 3),
        ):
            peer = z_peer(dz) * SIDE + y_peer(dy)
            m = len(copies)
            copies.append(
                remote(
                    gp_out.at[pl.ds(pl.multiple_of(peer * 16, 16), 16), k * span:(k + 1) * span],
                    gp_in.at[z, y, k], g_send.at[k, m], g_recv.at[k, m], (peer, me),
                )
            )
        return copies

    def pass_normed(n):
        ng_sum[n] = sum_normed(n, waiting[n])
        d = order[n]
        return remote(
            ng_sum.at[n], ngy_in.at[d], m_send.at[d], m_recv.at[d], (z * SIDE + y_peer(d), me)
        )

    order = (2, 1, 3, 0)
    lost = jnp.zeros((8, 128), F32)
    waiting, passing, gp_copies = [], [], []
    for n in range(SIDE):
        slot = y_peer(order[n])
        lost = lax.fori_loop(0, chunks, lambda k, lost, slot=slot: slope_chunk(slot, k, lost), lost)
        waiting.append(send_normed(n, slot))
    lx_in[me] = logs - lost * (math.log(2.0) / 10.0)
    loss_copies = []
    for d in range(1, LANES):
        loss_copies.append(
            remote(lx_in.at[me], lx_in.at[me], lx_send.at[d], lx_recv.at[d], (row, p_peer(d)))
        )
    gp_copies += send_protos(0)
    passing.append(pass_normed(0))
    gp_copies += send_protos(1)
    passing.append(pass_normed(1))
    passing.append(pass_normed(2))
    gp_copies += send_protos(2)
    gp_copies += send_protos(3)
    for copy in loss_copies:
        copy.wait()
    lost = lx_in[0]
    for k in range(1, LANES):
        lost = lost + lx_in[k]
    lz_in[row] = lost
    loss_copies = []
    for dz in range(SIDE):
        for dy in range(SIDE):
            if dz or dy:
                m = len(loss_copies)
                loss_copies.append(
                    remote(
                        lz_in.at[row], lz_in.at[row], lz_send.at[m], lz_recv.at[m],
                        (z_peer(dz) * SIDE + y_peer(dy), me),
                    )
                )
    total = sum_normed(3, waiting[3])
    for copy in passing:
        copy.wait()
    ng_all[me] = total + ngy_in[1] + ngy_in[2] + ngy_in[3]
    all_copies = []
    for d in (4, 3, 5, 2, 6, 1, 7):
        all_copies.append(
            remote(ng_all.at[me], ng_all.at[me], h_send.at[d], h_recv.at[d], (row, p_peer(d)))
        )

    for copy in all_copies:
        copy.wait()
    gathered = ng_all[...].reshape(B, D)
    normed_grad = jnp.zeros((B, D), F32)
    for term in split3(gathered):
        normed_grad = normed_grad + jnp.dot(back[...], term.astype(BF16), preferred_element_type=F32)
    along = jnp.sum(unit[...] * normed_grad, axis=1, keepdims=True)
    rest = normed_grad - unit[...] * along
    for h in range(D // 128):
        ge_ref[:, h * 128:(h + 1) * 128] = factor[...] * rest[:, h * 128:(h + 1) * 128]

    for copy in loss_copies:
        copy.wait()
    lost = lz_in[0]
    for k in range(1, SIDE * SIDE):
        lost = lost + lz_in[k]
    loss_ref[0] = jnp.sum(lost) * (1.0 / (B * SIDE * SIDE))

    for k in range(chunks):
        gp_in[z, y, k] = gp_out[dims, k * span:(k + 1) * span]
    for copy in gp_copies:
        copy.wait()
    for n in range(SIDE):
        for k in range(chunks):
            start = n * width + k * span
            gp_ref[:, start:start + span] = (
                gp_in[0, n, k].astype(F32) + gp_in[1, n, k].astype(F32)
                + gp_in[2, n, k].astype(F32) + gp_in[3, n, k].astype(F32)
            )


def body(embeddings, queue_feats, prototypes, crop_image, fill_count):
    width = prototypes.shape[1] // SIDE
    half = R // 2
    chunks = 4
    vmem = pl.BlockSpec(memory_space=pltpu.VMEM)
    smem = pl.BlockSpec(memory_space=pltpu.SMEM)
    hbm = pl.BlockSpec(memory_space=pl.ANY)
    dma = pltpu.SemaphoreType.DMA
    slab = B // LANES

    def pair(*shape):
        return [dma(shape), dma(shape)]

    scratch = [
        pltpu.VMEM((B, D), BF16),
        pltpu.VMEM((Q, D), BF16),
        pltpu.VMEM(prototypes.shape, BF16),
        pltpu.VMEM((SIDE, R, D), BF16),
        pltpu.VMEM((D, width), BF16),
        pltpu.VMEM((SIDE, V, width), F32),
        pltpu.VMEM((SIDE, R - V, width), BF16),
        pltpu.VMEM((SIDE, V, 128), F32),
        pltpu.VMEM((SIDE, V, 128), F32),
        pltpu.VMEM((SIDE, B, width), F32),
        pltpu.VMEM((SIDE, B, width), BF16),
        pltpu.VMEM((D, SIDE * B), BF16),
        pltpu.VMEM((SIDE, B, 128), F32),
        pltpu.VMEM((8, width), F32),
        pltpu.VMEM((SIDE, Q, 128), F32),
        pltpu.VMEM((SIDE, 16, R - V), BF16),
        pltpu.VMEM((16, width), BF16),
        pltpu.VMEM((8, width), F32),
        pltpu.VMEM((ITERS, 8, width // 8), F32),
        pltpu.VMEM((ITERS, 8, half), F32),
        pltpu.VMEM((ITERS, 8, half), F32),
        pltpu.VMEM((ITERS, 8, half), F32),
        pltpu.VMEM((ITERS, SIDE, 8, width // 8), F32),
        pltpu.VMEM((ITERS, 8, half), F32),
        pltpu.VMEM((ITERS, SIDE, 8, half), F32),
        pltpu.VMEM((ITERS, SIDE, 8, half), F32),
        pltpu.VMEM((SIDE, B, 128), F32),
        pltpu.VMEM((SIDE, B, 128), F32),
        pltpu.VMEM((B, D), F32),
        pltpu.VMEM((B, 128), F32),
        pltpu.VMEM((B, B), BF16),
        pltpu.VMEM((D, width), BF16),
        pltpu.VMEM((SIDE, SIDE, chunks, 16, width // chunks), BF16),
        pltpu.VMEM((SIDE, B, D), F32),
        pltpu.VMEM((SIDE, LANES, slab, D), F32),
        pltpu.VMEM((SIDE, slab, D), F32),
        pltpu.VMEM((SIDE, slab, D), F32),
        pltpu.VMEM((LANES, slab, D), F32),
        pltpu.VMEM((LANES, 8, 128), F32),
        pltpu.VMEM((SIDE * SIDE, 8, 128), F32),
        *pair(chunks, SIDE), *pair(chunks, SIDE, SIDE), *pair(SIDE), *pair(SIDE),
        *pair(ITERS, SIDE), *pair(ITERS), *pair(ITERS, SIDE),
        dma((ITERS, SIDE, 2)), dma((ITERS, SIDE)),
        *pair(chunks, 15), *pair(SIDE, LANES), *pair(SIDE), *pair(LANES),
        *pair(LANES), *pair(15), dma((3,)),
    ]
    return pl.pallas_call(
        kernel,
        name="swav",
        out_shape=(
            pltpu.VMEM((B, D), F32),
            pltpu.VMEM((prototypes.shape[0], prototypes.shape[1]), F32),
            jax.ShapeDtypeStruct((1,), F32),
        ),
        in_specs=[smem, hbm, hbm, hbm, vmem],
        out_specs=(vmem, vmem, smem),
        scratch_shapes=scratch,
        compiler_params=pltpu.CompilerParams(
            collective_id=0, has_side_effects=True, vmem_limit_bytes=60 * 1024 * 1024
        ),
    )(fill_count, embeddings, queue_feats, prototypes, crop_image.reshape(1, B))


def solution(mesh):
    placed = (P("row", None), P("row", None), P("row", "proto"), P("row"), P())
    return jax.shard_map(
        body,
        mesh=mesh,
        in_specs=placed,
        out_specs=(P("row", None), P("row", "proto"), P()),
        check_vma=False,
    )
```

```python
import functools
import math

import jax
import jax.numpy as jnp
from jax import lax
from jax.experimental import pallas as pl
from jax.experimental.pallas import tpu as pltpu
from jax.sharding import PartitionSpec as P

MESH = pl.DeviceIdType.MESH
F32 = jnp.float32
BF16 = jnp.bfloat16

CROPS = 8
ITERS = 3
SIDE = 4
LANES = 8
SCALE = 10.0 * math.log2(math.e)

B = 256
Q = 512
R = B + Q
V = 512
D = 256
TILE = 256
NT = (((1,), (1,)), ((), ()))


def iota(shape, dim):
    return lax.broadcasted_iota(jnp.int32, shape, dim)


def split3(v):
    hi = v.astype(BF16).astype(F32)
    rest = v - hi
    mid = rest.astype(BF16).astype(F32)
    return hi, mid, rest - mid


def stack16(v):
    hi, mid, low = split3(v)
    rid = iota((16, v.shape[1]), 0)
    out = jnp.where(rid == 0, hi, jnp.where(rid == 1, mid, jnp.where(rid == 2, low, 0.0)))
    return out.astype(BF16)


def unit_rows(raw):
    values = raw.astype(F32)
    inverse = lax.rsqrt(jnp.sum(values * values, axis=1, keepdims=True) + 1e-06)
    return values * inverse, inverse


def kernel(
    fill_ref, emb_hbm, queue_hbm, proto_hbm, image_ref,
    ge_ref, gp_ref, loss_ref,
    emb_ref, queue_ref, proto_ref, rows, protos, massf, massb, row_acc, row_wide, score, grad, turned, soft_acc, col_acc, alive, row16, col16, colb,
    col_part, row_part, row_mid, col_in, rowx_in, rowy_in,
    row_soft, row_code, unit, factor, back,
    gp_out, gp_in, ng_out, ng_in, ng_sum, ngy_in, ng_all, lx_in, lz_in,
    a_send, a_recv, z_send, z_recv, r_send, r_recv, f_send, f_recv,
    c_send, c_recv, x_send, x_recv, y_send, y_recv,
    g_send, g_recv, n_send, n_recv, m_send, m_recv, h_send, h_recv, lx_send, lx_recv, lz_send, lz_recv, in_sem,
):
    row = lax.axis_index("row")
    me = lax.axis_index("proto")
    z = row // SIDE
    y = lax.rem(row, SIDE)
    core = lax.rem(me, 2)
    chip = me // 2
    sibling = chip * 2 + (1 - core)
    width = protos.shape[1]
    tiles = width // TILE
    chunks = gp_in.shape[2]
    span = width // chunks

    def y_peer(d):
        return lax.rem(y + d, SIDE)

    def z_peer(d):
        return lax.rem(z + d, SIDE)

    def p_peer(d):
        return lax.rem(me + d, LANES)

    def remote(src, dst, send, recv, device):
        copy = pltpu.make_async_remote_copy(
            src_ref=src, dst_ref=dst, send_sem=send, recv_sem=recv,
            device_id=device, device_id_type=MESH,
        )
        copy.start()
        return copy

    def landed(ref, recv):
        pltpu.make_async_remote_copy(
            src_ref=ref, dst_ref=ref, send_sem=recv, recv_sem=recv,
            device_id=(row, sibling), device_id_type=MESH,
        ).wait_recv()

    def left(ref, send):
        pltpu.make_async_remote_copy(
            src_ref=ref, dst_ref=ref, send_sem=send, recv_sem=send,
            device_id=(row, sibling), device_id_type=MESH,
        ).wait_send()

    loads = []
    for n, (source, target) in enumerate(
        ((emb_hbm, emb_ref), (queue_hbm, queue_ref), (proto_hbm, proto_ref))
    ):
        loads.append(pltpu.make_async_copy(source, target, in_sem.at[n]))
        loads[-1].start()
    barrier = pltpu.get_barrier_semaphore()
    count = 0
    for dz in range(SIDE):
        for dy in range(SIDE):
            if dz or dy:
                pl.semaphore_signal(
                    barrier, inc=1, device_id=(z_peer(dz) * SIDE + y_peer(dy), me), device_id_type=MESH
                )
                count += 1
    for dp in range(1, LANES):
        pl.semaphore_signal(barrier, inc=1, device_id=(row, p_peer(dp)), device_id_type=MESH)
        count += 1
    for dy in range(1, SIDE):
        pl.semaphore_signal(
            barrier, inc=1, device_id=(z * SIDE + y_peer(dy), sibling), device_id_type=MESH
        )
        count += 1

    image = image_ref[...].astype(F32)
    wide = jnp.broadcast_to(image, (B, B))
    rid, cid = iota((B, B), 0), iota((B, B), 1)
    tall = jnp.sum(jnp.where(rid == cid, wide, 0.0), axis=1, keepdims=True)
    same = jnp.where(wide == tall, 1.0, 0.0)
    base = (row * (B // CROPS)).astype(F32)
    place = jnp.sum(jnp.where(rid < cid, same, 0.0), axis=0, keepdims=True) * (B // CROPS) + (image - base)
    forward = jnp.where(rid.astype(F32) == place, 1.0, 0.0).astype(BF16)
    for copy in loads:
        copy.wait()
    exact, _ = unit_rows(emb_ref[...])
    ordered = jnp.dot(forward, exact.astype(BF16), preferred_element_type=F32).astype(BF16)
    rows[y, 0:B, :] = ordered
    rows[y, B:R, :] = unit_rows(queue_ref[...])[0].astype(BF16)
    dims = pl.ds(pl.multiple_of(row * 16, 16), 16)
    protos[dims, :] = proto_ref[:, pl.ds(pl.multiple_of(y * width, width), width)]

    pl.semaphore_wait(barrier, count)

    def from_y(k, d):
        return pltpu.make_async_remote_copy(
            src_ref=protos.at[dims, k * span:(k + 1) * span],
            dst_ref=protos.at[dims, k * span:(k + 1) * span],
            send_sem=a_send, recv_sem=a_recv.at[k, d], device_id=(row, sibling), device_id_type=MESH,
        )

    for k in range(chunks):
        for d in (1, 3, 2):
            remote(
                proto_ref.at[:, pl.ds(pl.multiple_of(y_peer(d) * width + k * span, span), span)],
                protos.at[dims, k * span:(k + 1) * span], a_send, a_recv.at[k, d],
                (z * SIDE + y_peer(d), me),
            )
    shared = pl.ds(pl.multiple_of(core * (R // 2), R // 2), R // 2)
    for d in (1, 3, 2):
        remote(
            rows.at[y, shared, :], rows.at[y, shared, :], r_send, r_recv.at[d],
            (z * SIDE + y_peer(d), me),
        )
    def to_z(k, source):
        slot = lax.rem(y + SIDE - source, SIDE)
        part = protos.at[pl.ds(pl.multiple_of((z * SIDE + slot) * 16, 16), 16), k * span:(k + 1) * span]
        for d in (1, 3, 2):
            remote(part, part, z_send, z_recv.at[k], (z_peer(d) * SIDE + y, me))

    for k in range(chunks):
        to_z(k, 0)
    for k in range(chunks):
        for source in (1, 3, 2):
            from_y(k, source).wait_recv()
            to_z(k, source)

    soft_acc[...] = jnp.zeros_like(soft_acc)
    col_acc[...] = jnp.zeros_like(col_acc)
    fill = fill_ref[0]
    for slot in range(SIDE):
        place = (z * SIDE + slot) * Q + iota((Q, 128), 0)
        alive[slot] = jnp.where(place < fill, 1.0, 0.0)
    place = jnp.sum(jnp.where(cid < rid, same, 0.0), axis=1, keepdims=True) * (B // CROPS) + (tall - base)
    back[...] = jnp.where(cid.astype(F32) == place, 1.0, 0.0).astype(BF16)
    exact, inverse = unit_rows(emb_ref[...])
    unit[...] = exact
    factor[...] = jnp.broadcast_to(inverse, (B, 128))

    def score_chunk(slot, k):
        for h in range(span // TILE):
            cols = pl.ds(pl.multiple_of(k * span + h * TILE, TILE), TILE)
            total = jnp.dot(rows[slot], protos[:, cols], preferred_element_type=F32)
            crop = total[0:B] * SCALE
            score[slot, :, cols] = crop
            soft = jnp.exp2(crop)
            soft_acc[slot] += soft[:, 0:128] + soft[:, 128:256]
            code = soft * soft
            massf[slot, 0:B, cols] = code
            rest = jnp.exp2(total[B:R] * (2.0 * SCALE))
            massf[slot, B:V, cols] = rest[0:V - B]
            massb[slot, :, cols] = rest[V - B:].astype(BF16)
            live = alive[slot]
            for g in range(TILE // 128):
                lanes = slice(g * 128, (g + 1) * 128)
                part = jnp.sum(code[:, lanes].reshape(B // 8, 8, 128), axis=0)
                part = part + jnp.sum((rest[:, lanes] * live).reshape(Q // 8, 8, 128), axis=0)
                at = pl.ds(pl.multiple_of(k * span + h * TILE + g * 128, 128), 128)
                col_acc[:, at] += part

    def score_many(first_slot, slots, first_chunk, many):
        def step(i, carry):
            n = first_slot + i // many
            score_chunk(lax.rem(y + n + n // 2, SIDE), first_chunk + lax.rem(i, many))
            return carry

        lax.fori_loop(0, slots * many, step, 0)

    def z_arrived(k):
        landed(protos.at[0:192, 0:span], z_recv.at[k])

    def score_far(first_chunk, many):
        def step(i, carry):
            score_chunk(y_peer(2), first_chunk + i)
            return carry

        lax.fori_loop(0, many, step, 0)

    def hand_over(d):
        landed(rows.at[0, 0:R // 2, :], r_recv.at[d])
        slot = lax.rem(y + SIDE - d, SIDE)
        part = rows.at[slot, shared, :]
        remote(part, part, f_send, f_recv.at[d], (row, sibling))

    z_arrived(0)
    score_chunk(y, 0)
    hand_over(1)
    hand_over(3)
    z_arrived(1)
    score_chunk(y, 1)
    landed(rows.at[0, 0:R // 2, :], f_recv.at[1])
    landed(rows.at[0, 0:R // 2, :], f_recv.at[3])
    score_many(1, 2, 0, 2)
    hand_over(2)
    z_arrived(2)
    score_many(0, 3, 2, 1)
    landed(rows.at[0, 0:R // 2, :], f_recv.at[2])
    score_far(0, 3)
    z_arrived(3)
    score_many(0, 3, 3, 1)
    score_far(3, 1)
    for j in range(tiles):
        col_part[0, j:j + 1, :] = jnp.sum(col_acc[:, j * TILE:(j + 1) * TILE], axis=0, keepdims=True)

    def column_exchange(t):
        for d in (2, 1, 3):
            remote(
                col_part.at[t], col_in.at[t, z], c_send, c_recv.at[t], (z_peer(d) * SIDE + y, me)
            )
        col_in[t, z] = col_part[t]
        landed(col_in.at[t, 0:SIDE - 1], c_recv.at[t])
        column = 1.0 / (col_in[t, 0] + col_in[t, 1] + col_in[t, 2] + col_in[t, 3])
        for j in range(tiles):
            col16[:, j * TILE:(j + 1) * TILE] = stack16(column[j:j + 1, :])
            colb[:, j * TILE:(j + 1) * TILE] = jnp.broadcast_to(column[j:j + 1, :], (8, TILE))

    def row_exchange(t):
        for d in (2, 1, 3):
            remote(
                row_part.at[t], rowx_in.at[t, me], x_send, x_recv.at[t],
                (row, lax.rem(chip + d, SIDE) * 2 + 1),
            )

        @pl.when(core == 0)
        def _():
            remote(row_part.at[t], rowx_in.at[t, me], x_send, x_recv.at[t], (row, sibling))
            landed(rowy_in.at[t], y_recv.at[t])

        @pl.when(core == 1)
        def _():
            rowx_in[t, me] = row_part[t]
            landed(rowx_in.at[t, 0:LANES - 1], x_recv.at[t])
            total = rowx_in[t, 0]
            for k in range(1, LANES):
                total = total + rowx_in[t, k]
            row_mid[t] = total
            for d, c in ((2, 0), (2, 1), (1, 0), (1, 1), (3, 0), (3, 1), (0, 0)):
                remote(
                    row_mid.at[t], rowy_in.at[t, y], y_send, y_recv.at[t],
                    (z * SIDE + y_peer(d), chip * 2 + c),
                )
            rowy_in[t, y] = total
            landed(rowy_in.at[t, 0:SIDE - 1], y_recv.at[t])

        return rowy_in[t, 0] + rowy_in[t, 1] + rowy_in[t, 2] + rowy_in[t, 3]

    def row_sums(slot, many):
        for g in range(many // 8):
            at = slice(g * 8, g * 8 + 8)
            sums = [None, None]
            for n in range(width // 128):
                lanes = slice(n * 128, (n + 1) * 128)
                term = massf[slot, at, lanes] * colb[:, lanes]
                sums[n % 2] = term if sums[n % 2] is None else sums[n % 2] + term
            row_acc[slot, at, :] = sums[0] + sums[1]

    def turn(slot, b):
        return jnp.sum(row_acc[slot, b * 128:(b + 1) * 128, :].T, axis=0, keepdims=True)

    half = R // 2
    rid8, lane8 = iota((8, half), 0), iota((8, half), 1)
    spot = lax.rem(rid8, 2) * half + lane8
    queue_row = (z * SIDE + rid8 // 2) * Q + spot - B
    live = jnp.where(jnp.logical_or(spot < B, queue_row < fill), 1.0, 0.0)

    for t in range(ITERS):
        column_exchange(t)
        if t + 1 == ITERS:
            break

        def row_block(slot, carry, t=t):
            row_sums(slot, V)
            rest = lax.dot_general(col16[...], massb[slot], NT, preferred_element_type=F32)
            rest = jnp.sum(rest, axis=0, keepdims=True)
            parts = [turn(slot, b) for b in range(V // 128)] + [rest[:, 0:128], rest[:, 128:256]]
            for h in range(2):
                row_part[t, pl.ds(2 * slot + h, 1), :] = jnp.concatenate(parts[3 * h:3 * h + 3], axis=1)
            return carry

        lax.fori_loop(0, SIDE, row_block, 0)
        weight = live / row_exchange(t)
        for slot in range(SIDE):
            row16[slot] = stack16(weight[2 * slot + 1:2 * slot + 2, 128:half])
            for b in range(V // 128):
                at = slice((b % 3) * 128, (b % 3 + 1) * 128)
                line = weight[2 * slot + b // 3:2 * slot + b // 3 + 1, at]
                row_wide[slot, b * 128:(b + 1) * 128, :] = jnp.broadcast_to(line, (128, 128)).T

        def column_block(slot, sums):
            rest = jnp.dot(row16[slot], massb[slot], preferred_element_type=F32)
            sums = list(sums)
            for g in range(V // 8):
                at = slice(g * 8, g * 8 + 8)
                scale = row_wide[slot, at, :]
                for n in range(width // 128):
                    sums[n] = sums[n] + massf[slot, at, n * 128:(n + 1) * 128] * scale
            return tuple(sums[n] + rest[0:8, n * 128:(n + 1) * 128] for n in range(width // 128))

        sums = lax.fori_loop(
            0, SIDE, column_block, tuple(jnp.zeros((8, 128), F32) for _ in range(width // 128))
        )
        for n in range(width // 128):
            at = slice((n % 2) * 128, (n % 2 + 1) * 128)
            col_part[t + 1, n // 2:n // 2 + 1, at] = jnp.sum(sums[n], axis=0, keepdims=True)

    last = ITERS - 1
    for slot in range(SIDE):
        row_sums(slot, B)
        for b in range(B // 128):
            row_part[last, 2 * slot:2 * slot + 1, b * 128:(b + 1) * 128] = turn(slot, b)
        row_part[last, 2 * slot + 1:2 * slot + 2, 0:B] = jnp.concatenate(
            [
                jnp.sum(soft_acc[slot, 0:128, :].T, axis=0, keepdims=True),
                jnp.sum(soft_acc[slot, 128:256, :].T, axis=0, keepdims=True),
            ],
            axis=1,
        )
        row_part[last, 2 * slot:2 * slot + 2, B:half] = jnp.ones((2, half - B), F32)
        eye = jnp.where(rid == cid, 1.0, 0.0).astype(BF16)
        turned[:, slot * B:(slot + 1) * B] = lax.dot_general(
            eye, rows[slot, 0:B, :], NT, preferred_element_type=F32
        ).astype(BF16)
    sums = row_exchange(last)
    for slot in range(SIDE):
        code = sums[2 * slot:2 * slot + 1, 0:B]
        soft = sums[2 * slot + 1:2 * slot + 2, 0:B]
        for target, value in ((row_code, (10.0 / (CROPS - 1)) / code), (row_soft, 10.0 / soft)):
            for h in range(2):
                target[slot, h * 128:(h + 1) * 128, :] = jnp.broadcast_to(
                    value[:, h * 128:(h + 1) * 128], (128, 128)
                ).T
    sublane = iota((8, B), 0)
    logs = jnp.log(sums[:, 0:B])
    mine = jnp.logical_and(sublane == 2 * y + 1, me == 0)
    logs = jnp.where(mine, logs, 0.0)
    logs = logs[:, 0:128] + logs[:, 128:256]

    images = B // CROPS
    slab = B // LANES

    def slope_chunk(slot, k, lost):
        for h in range(span // 128):
            lanes = pl.ds(pl.multiple_of(k * span + h * 128, 128), 128)
            column = colb[:, lanes]
            for i in range(images // 8):
                softs, parts, scores = [], [], []
                for c in range(CROPS):
                    at = slice(c * images + i * 8, c * images + i * 8 + 8)
                    s = score[slot, at, lanes]
                    e = jnp.exp2(s)
                    parts.append(e * e * column * row_code[slot, at, :])
                    softs.append(e * row_soft[slot, at, :])
                    scores.append(s)
                total = parts[0]
                for c in range(1, CROPS):
                    total = total + parts[c]
                for c in range(CROPS):
                    at = slice(c * images + i * 8, c * images + i * 8 + 8)
                    goal = total - parts[c]
                    lost = lost + goal * scores[c]
                    grad[slot, at, lanes] = (softs[c] - goal).astype(BF16)
        return lost

    def send_normed(n, slot):
        ng_out[n] = lax.dot_general(grad[slot], protos[...], NT, preferred_element_type=F32)
        for d in (4, 3, 5, 2, 6, 1, 7):
            to_p = p_peer(d)
            remote(
                ng_out.at[n, pl.ds(pl.multiple_of(to_p * slab, slab), slab), :],
                ng_in.at[n, me], n_send, n_recv.at[n], (row, to_p),
            )
        ng_in[n, me] = ng_out[n, pl.ds(pl.multiple_of(me * slab, slab), slab), :]

    def sum_normed(n):
        landed(ng_in.at[n, 0:LANES - 1], n_recv.at[n])
        total = ng_in[n, 0]
        for k in range(1, LANES):
            total = total + ng_in[n, k]
        return total

    def send_protos(k):
        for h in range(span // TILE):
            cols = slice(k * span + h * TILE, k * span + (h + 1) * TILE)
            part = jnp.dot(turned[:, 0:B], grad[0, :, cols], preferred_element_type=F32)
            for other in range(1, SIDE):
                part = part + jnp.dot(
                    turned[:, other * B:(other + 1) * B], grad[other, :, cols],
                    preferred_element_type=F32,
                )
            gp_out[:, cols] = part.astype(BF16)
        for dz, dy in (
            (2, 2), (2, 1), (2, 3), (1, 2), (3, 2), (1, 1), (1, 3), (3, 1), (3, 3),
            (2, 0), (0, 2), (1, 0), (3, 0), (0, 1), (0, 3),
        ):
            peer = z_peer(dz) * SIDE + y_peer(dy)
            remote(
                gp_out.at[pl.ds(pl.multiple_of(peer * 16, 16), 16), k * span:(k + 1) * span],
                gp_in.at[z, y, k], g_send, g_recv, (peer, me),
            )

    def pass_normed(n):
        ng_sum[n] = sum_normed(n)
        d = order[n]
        remote(ng_sum.at[n], ngy_in.at[d], m_send, m_recv, (z * SIDE + y_peer(d), me))

    order = (2, 1, 3, 0)
    lost = jnp.zeros((8, 128), F32)
    for n in range(SIDE):
        slot = y_peer(order[n])
        lost = lax.fori_loop(0, chunks, lambda k, lost, slot=slot: slope_chunk(slot, k, lost), lost)
        if n == SIDE - 1:
            lx_in[me] = logs - lost * (math.log(2.0) / 10.0)
            for d in range(1, LANES):
                remote(lx_in.at[me], lx_in.at[me], lx_send, lx_recv, (row, p_peer(d)))
        send_normed(n, slot)
    send_protos(0)
    pass_normed(0)
    send_protos(1)
    pass_normed(1)
    pass_normed(2)
    landed(lx_in.at[0:LANES - 1], lx_recv)
    lost = lx_in[0]
    for k in range(1, LANES):
        lost = lost + lx_in[k]
    lz_in[row] = lost
    for dz in range(SIDE):
        for dy in range(SIDE):
            if dz or dy:
                remote(
                    lz_in.at[row], lz_in.at[row], lz_send, lz_recv, (z_peer(dz) * SIDE + y_peer(dy), me)
                )
    send_protos(2)
    send_protos(3)
    total = sum_normed(3)
    landed(ngy_in.at[0:SIDE - 1], m_recv)
    ng_all[me] = total + ngy_in[1] + ngy_in[2] + ngy_in[3]
    for d in (4, 3, 5, 2, 6, 1, 7):
        remote(ng_all.at[me], ng_all.at[me], h_send, h_recv, (row, p_peer(d)))

    landed(ng_all.at[0:LANES - 1], h_recv)
    gathered = ng_all[...].reshape(B, D)
    normed_grad = jnp.zeros((B, D), F32)
    for term in split3(gathered):
        normed_grad = normed_grad + jnp.dot(back[...], term.astype(BF16), preferred_element_type=F32)
    along = jnp.sum(unit[...] * normed_grad, axis=1, keepdims=True)
    rest = normed_grad - unit[...] * along
    for h in range(D // 128):
        ge_ref[:, h * 128:(h + 1) * 128] = factor[...] * rest[:, h * 128:(h + 1) * 128]

    landed(lz_in.at[0:SIDE * SIDE - 1], lz_recv)
    lost = lz_in[0]
    for k in range(1, SIDE * SIDE):
        lost = lost + lz_in[k]
    loss_ref[0] = jnp.sum(lost) * (1.0 / (B * SIDE * SIDE))

    for k in range(chunks):
        gp_in[z, y, k] = gp_out[dims, k * span:(k + 1) * span]
    landed(gp_out.at[0:240, :], g_recv)
    for n in range(SIDE):
        for k in range(chunks):
            start = n * width + k * span
            gp_ref[:, start:start + span] = (
                gp_in[0, n, k].astype(F32) + gp_in[1, n, k].astype(F32)
                + gp_in[2, n, k].astype(F32) + gp_in[3, n, k].astype(F32)
            )
    left(protos.at[0:192, 0:span], a_send)
    left(protos.at[0:192, :], z_send)
    left(rows.at[0:3, 0:R // 2, :], r_send)
    left(rows.at[0:3, 0:R // 2, :], f_send)
    left(col_in.at[:, 0:SIDE - 1], c_send)
    left(gp_out.at[0:240, :], g_send)
    left(ng_in.at[:, 0:LANES - 1], n_send)
    left(ngy_in.at[0:SIDE - 1], m_send)
    left(ng_all.at[0:LANES - 1], h_send)
    left(lx_in.at[0:LANES - 1], lx_send)
    left(lz_in.at[0:SIDE * SIDE - 1], lz_send)

    @pl.when(core == 0)
    def _():
        left(rowx_in.at[:, 0:SIDE], x_send)

    @pl.when(core == 1)
    def _():
        left(rowx_in.at[:, 0:SIDE - 1], x_send)
        left(rowx_in.at[:, 0:LANES - 1], y_send)


def body(embeddings, queue_feats, prototypes, crop_image, fill_count):
    width = prototypes.shape[1] // SIDE
    half = R // 2
    chunks = 4
    vmem = pl.BlockSpec(memory_space=pltpu.VMEM)
    smem = pl.BlockSpec(memory_space=pltpu.SMEM)
    hbm = pl.BlockSpec(memory_space=pl.ANY)
    dma = pltpu.SemaphoreType.DMA
    slab = B // LANES

    def group(*shape):
        return [dma, dma(shape) if shape else dma]

    scratch = [
        pltpu.VMEM((B, D), BF16),
        pltpu.VMEM((Q, D), BF16),
        pltpu.VMEM(prototypes.shape, BF16),
        pltpu.VMEM((SIDE, R, D), BF16),
        pltpu.VMEM((D, width), BF16),
        pltpu.VMEM((SIDE, V, width), F32),
        pltpu.VMEM((SIDE, R - V, width), BF16),
        pltpu.VMEM((SIDE, V, 128), F32),
        pltpu.VMEM((SIDE, V, 128), F32),
        pltpu.VMEM((SIDE, B, width), F32),
        pltpu.VMEM((SIDE, B, width), BF16),
        pltpu.VMEM((D, SIDE * B), BF16),
        pltpu.VMEM((SIDE, B, 128), F32),
        pltpu.VMEM((8, width), F32),
        pltpu.VMEM((SIDE, Q, 128), F32),
        pltpu.VMEM((SIDE, 16, R - V), BF16),
        pltpu.VMEM((16, width), BF16),
        pltpu.VMEM((8, width), F32),
        pltpu.VMEM((ITERS, 8, width // 8), F32),
        pltpu.VMEM((ITERS, 8, half), F32),
        pltpu.VMEM((ITERS, 8, half), F32),
        pltpu.VMEM((ITERS, SIDE, 8, width // 8), F32),
        pltpu.VMEM((ITERS, LANES, 8, half), F32),
        pltpu.VMEM((ITERS, SIDE, 8, half), F32),
        pltpu.VMEM((SIDE, B, 128), F32),
        pltpu.VMEM((SIDE, B, 128), F32),
        pltpu.VMEM((B, D), F32),
        pltpu.VMEM((B, 128), F32),
        pltpu.VMEM((B, B), BF16),
        pltpu.VMEM((D, width), BF16),
        pltpu.VMEM((SIDE, SIDE, chunks, 16, width // chunks), BF16),
        pltpu.VMEM((SIDE, B, D), F32),
        pltpu.VMEM((SIDE, LANES, slab, D), F32),
        pltpu.VMEM((SIDE, slab, D), F32),
        pltpu.VMEM((SIDE, slab, D), F32),
        pltpu.VMEM((LANES, slab, D), F32),
        pltpu.VMEM((LANES, 8, 128), F32),
        pltpu.VMEM((SIDE * SIDE, 8, 128), F32),
        *group(chunks, SIDE), *group(chunks), *group(SIDE), *group(SIDE),
        *group(ITERS), *group(ITERS), *group(ITERS),
        *group(), *group(SIDE), *group(), *group(), *group(), *group(), dma((3,)),
    ]
    return pl.pallas_call(
        kernel,
        name="swav",
        out_shape=(
            pltpu.VMEM((B, D), F32),
            pltpu.VMEM((prototypes.shape[0], prototypes.shape[1]), F32),
            jax.ShapeDtypeStruct((1,), F32),
        ),
        in_specs=[smem, hbm, hbm, hbm, vmem],
        out_specs=(vmem, vmem, smem),
        scratch_shapes=scratch,
        compiler_params=pltpu.CompilerParams(
            collective_id=0, has_side_effects=True, vmem_limit_bytes=60 * 1024 * 1024
        ),
    )(fill_count, embeddings, queue_feats, prototypes, crop_image.reshape(1, B))


def solution(mesh):
    placed = (P("row", None), P("row", None), P("row", "proto"), P("row"), P())
    return jax.shard_map(
        body,
        mesh=mesh,
        in_specs=placed,
        out_specs=(P("row", None), P("row", "proto"), P()),
        check_vma=False,
    )
```

```python
import functools
import math

import jax
import jax.numpy as jnp
from jax import lax
from jax.experimental import pallas as pl
from jax.experimental.pallas import tpu as pltpu
from jax.sharding import PartitionSpec as P

MESH = pl.DeviceIdType.MESH
F32 = jnp.float32
BF16 = jnp.bfloat16

CROPS = 8
ITERS = 3
SIDE = 4
LANES = 8
SCALE = 10.0 * math.log2(math.e)

B = 256
Q = 512
R = B + Q
V = 512
D = 256
TILE = 256
NT = (((1,), (1,)), ((), ()))


def iota(shape, dim):
    return lax.broadcasted_iota(jnp.int32, shape, dim)


def split3(v):
    hi = v.astype(BF16).astype(F32)
    rest = v - hi
    mid = rest.astype(BF16).astype(F32)
    return hi, mid, rest - mid


def stack16(v):
    hi, mid, low = split3(v)
    rid = iota((16, v.shape[1]), 0)
    out = jnp.where(rid == 0, hi, jnp.where(rid == 1, mid, jnp.where(rid == 2, low, 0.0)))
    return out.astype(BF16)


def unit_rows(raw):
    values = raw.astype(F32)
    inverse = lax.rsqrt(jnp.sum(values * values, axis=1, keepdims=True) + 1e-06)
    return values * inverse, inverse


def kernel(
    fill_ref, emb_hbm, queue_hbm, proto_hbm, image_ref,
    ge_ref, gp_ref, loss_ref,
    emb_ref, queue_ref, proto_ref, rows, protos, massf, massb, row_acc, row_wide, score, grad, turned, soft_acc, col_acc, alive, row16, col16, colb,
    col_part, row_part, row_mid, col_in, rowx_in, rowy_in,
    row_soft, row_code, unit, factor, back,
    gp_out, gp_in, ng_out, ngc_in, ng_pair, ng_in, ng_sum, ngy_in, ng_all, lx_in, lz_in,
    a_send, a_recv, z_send, z_recv, r_send, r_recv, f_send, f_recv,
    c_send, c_recv, x_send, x_recv, y_send, y_recv,
    g_send, g_recv, e_send, e_recv, n_send, n_recv, m_send, m_recv, h_send, h_recv, lx_send, lx_recv, lz_send, lz_recv, in_sem,
):
    row = lax.axis_index("row")
    me = lax.axis_index("proto")
    z = row // SIDE
    y = lax.rem(row, SIDE)
    core = lax.rem(me, 2)
    chip = me // 2
    sibling = chip * 2 + (1 - core)
    width = protos.shape[1]
    tiles = width // TILE
    chunks = gp_in.shape[2]
    span = width // chunks

    def y_peer(d):
        return lax.rem(y + d, SIDE)

    def z_peer(d):
        return lax.rem(z + d, SIDE)

    def p_peer(d):
        return lax.rem(me + d, LANES)

    def remote(src, dst, send, recv, device):
        copy = pltpu.make_async_remote_copy(
            src_ref=src, dst_ref=dst, send_sem=send, recv_sem=recv,
            device_id=device, device_id_type=MESH,
        )
        copy.start()
        return copy

    def landed(ref, recv):
        pltpu.make_async_remote_copy(
            src_ref=ref, dst_ref=ref, send_sem=recv, recv_sem=recv,
            device_id=(row, sibling), device_id_type=MESH,
        ).wait_recv()

    def left(ref, send):
        pltpu.make_async_remote_copy(
            src_ref=ref, dst_ref=ref, send_sem=send, recv_sem=send,
            device_id=(row, sibling), device_id_type=MESH,
        ).wait_send()

    loads = []
    for n, (source, target) in enumerate(
        ((emb_hbm, emb_ref), (queue_hbm, queue_ref), (proto_hbm, proto_ref))
    ):
        loads.append(pltpu.make_async_copy(source, target, in_sem.at[n]))
        loads[-1].start()
    barrier = pltpu.get_barrier_semaphore()
    count = 0
    for d in range(1, SIDE):
        for peer in (z * SIDE + y_peer(d), z_peer(d) * SIDE + y):
            pl.semaphore_signal(barrier, inc=1, device_id=(peer, me), device_id_type=MESH)
            count += 1
    for d in range(1, LANES):
        pl.semaphore_signal(barrier, inc=1, device_id=(row, p_peer(d)), device_id_type=MESH)
        count += 1

    image = image_ref[...].astype(F32)
    wide = jnp.broadcast_to(image, (B, B))
    rid, cid = iota((B, B), 0), iota((B, B), 1)
    tall = jnp.sum(jnp.where(rid == cid, wide, 0.0), axis=1, keepdims=True)
    same = jnp.where(wide == tall, 1.0, 0.0)
    base = (row * (B // CROPS)).astype(F32)
    place = jnp.sum(jnp.where(rid < cid, same, 0.0), axis=0, keepdims=True) * (B // CROPS) + (image - base)
    forward = jnp.where(rid.astype(F32) == place, 1.0, 0.0).astype(BF16)
    for copy in loads:
        copy.wait()
    exact, _ = unit_rows(emb_ref[...])
    ordered = jnp.dot(forward, exact.astype(BF16), preferred_element_type=F32).astype(BF16)
    rows[y, 0:B, :] = ordered
    rows[y, B:R, :] = unit_rows(queue_ref[...])[0].astype(BF16)
    dims = pl.ds(pl.multiple_of(row * 16, 16), 16)
    protos[dims, :] = proto_ref[:, pl.ds(pl.multiple_of(y * width, width), width)]

    pl.semaphore_wait(barrier, count)

    def from_y(k, d):
        return pltpu.make_async_remote_copy(
            src_ref=protos.at[dims, k * span:(k + 1) * span],
            dst_ref=protos.at[dims, k * span:(k + 1) * span],
            send_sem=a_send, recv_sem=a_recv.at[k, d], device_id=(row, sibling), device_id_type=MESH,
        )

    for k in range(chunks):
        for d in (1, 3, 2):
            remote(
                proto_ref.at[:, pl.ds(pl.multiple_of(y_peer(d) * width + k * span, span), span)],
                protos.at[dims, k * span:(k + 1) * span], a_send, a_recv.at[k, d],
                (z * SIDE + y_peer(d), me),
            )
    shared = pl.ds(pl.multiple_of(core * (R // 2), R // 2), R // 2)
    for d in (1, 3, 2):
        remote(
            rows.at[y, shared, :], rows.at[y, shared, :], r_send, r_recv.at[d],
            (z * SIDE + y_peer(d), me),
        )
    def to_z(k, source):
        slot = lax.rem(y + SIDE - source, SIDE)
        part = protos.at[pl.ds(pl.multiple_of((z * SIDE + slot) * 16, 16), 16), k * span:(k + 1) * span]
        for d in (1, 3, 2):
            remote(part, part, z_send, z_recv.at[k], (z_peer(d) * SIDE + y, me))

    for k in range(chunks):
        to_z(k, 0)
    for k in range(chunks):
        for source in (1, 3, 2):
            from_y(k, source).wait_recv()
            to_z(k, source)

    soft_acc[...] = jnp.zeros_like(soft_acc)
    col_acc[...] = jnp.zeros_like(col_acc)
    fill = fill_ref[0]
    for slot in range(SIDE):
        place = (z * SIDE + slot) * Q + iota((Q, 128), 0)
        alive[slot] = jnp.where(place < fill, 1.0, 0.0)
    place = jnp.sum(jnp.where(cid < rid, same, 0.0), axis=1, keepdims=True) * (B // CROPS) + (tall - base)
    back[...] = jnp.where(cid.astype(F32) == place, 1.0, 0.0).astype(BF16)
    exact, inverse = unit_rows(emb_ref[...])
    unit[...] = exact
    factor[...] = jnp.broadcast_to(inverse, (B, 128))

    def score_chunk(slot, k):
        for h in range(span // TILE):
            cols = pl.ds(pl.multiple_of(k * span + h * TILE, TILE), TILE)
            total = jnp.dot(rows[slot], protos[:, cols], preferred_element_type=F32)
            crop = total[0:B] * SCALE
            score[slot, :, cols] = crop
            soft = jnp.exp2(crop)
            soft_acc[slot] += soft[:, 0:128] + soft[:, 128:256]
            code = soft * soft
            massf[slot, 0:B, cols] = code
            rest = jnp.exp2(total[B:R] * (2.0 * SCALE))
            massf[slot, B:V, cols] = rest[0:V - B]
            massb[slot, :, cols] = rest[V - B:].astype(BF16)
            live = alive[slot]
            for g in range(TILE // 128):
                lanes = slice(g * 128, (g + 1) * 128)
                part = jnp.sum(code[:, lanes].reshape(B // 8, 8, 128), axis=0)
                part = part + jnp.sum((rest[:, lanes] * live).reshape(Q // 8, 8, 128), axis=0)
                at = pl.ds(pl.multiple_of(k * span + h * TILE + g * 128, 128), 128)
                col_acc[:, at] += part

    def score_many(first_slot, slots, first_chunk, many):
        def step(i, carry):
            n = first_slot + i // many
            score_chunk(lax.rem(y + n + n // 2, SIDE), first_chunk + lax.rem(i, many))
            return carry

        lax.fori_loop(0, slots * many, step, 0)

    def z_arrived(k):
        landed(protos.at[0:192, 0:span], z_recv.at[k])

    def score_far(first_chunk, many):
        def step(i, carry):
            score_chunk(y_peer(2), first_chunk + i)
            return carry

        lax.fori_loop(0, many, step, 0)

    def hand_over(d):
        landed(rows.at[0, 0:R // 2, :], r_recv.at[d])
        slot = lax.rem(y + SIDE - d, SIDE)
        part = rows.at[slot, shared, :]
        remote(part, part, f_send, f_recv.at[d], (row, sibling))

    z_arrived(0)
    score_chunk(y, 0)
    hand_over(1)
    hand_over(3)
    z_arrived(1)
    score_chunk(y, 1)
    landed(rows.at[0, 0:R // 2, :], f_recv.at[1])
    landed(rows.at[0, 0:R // 2, :], f_recv.at[3])
    score_many(1, 2, 0, 2)
    hand_over(2)
    z_arrived(2)
    score_many(0, 3, 2, 1)
    z_arrived(3)
    score_many(0, 3, 3, 1)
    landed(rows.at[0, 0:R // 2, :], f_recv.at[2])
    score_far(0, chunks)
    for j in range(tiles):
        col_part[0, j:j + 1, :] = jnp.sum(col_acc[:, j * TILE:(j + 1) * TILE], axis=0, keepdims=True)

    def column_exchange(t):
        for d in (2, 1, 3):
            remote(
                col_part.at[t], col_in.at[t, z], c_send, c_recv.at[t], (z_peer(d) * SIDE + y, me)
            )
        col_in[t, z] = col_part[t]
        landed(col_in.at[t, 0:SIDE - 1], c_recv.at[t])
        column = 1.0 / (col_in[t, 0] + col_in[t, 1] + col_in[t, 2] + col_in[t, 3])
        for j in range(tiles):
            col16[:, j * TILE:(j + 1) * TILE] = stack16(column[j:j + 1, :])
            colb[:, j * TILE:(j + 1) * TILE] = jnp.broadcast_to(column[j:j + 1, :], (8, TILE))

    def row_exchange(t):
        for d in (2, 1, 3):
            remote(
                row_part.at[t], rowx_in.at[t, me], x_send, x_recv.at[t],
                (row, lax.rem(chip + d, SIDE) * 2 + 1),
            )

        @pl.when(core == 0)
        def _():
            remote(row_part.at[t], rowx_in.at[t, me], x_send, x_recv.at[t], (row, sibling))
            landed(rowy_in.at[t], y_recv.at[t])

        @pl.when(core == 1)
        def _():
            rowx_in[t, me] = row_part[t]
            landed(rowx_in.at[t, 0:LANES - 1], x_recv.at[t])
            total = rowx_in[t, 0]
            for k in range(1, LANES):
                total = total + rowx_in[t, k]
            row_mid[t] = total
            for d, c in ((2, 0), (2, 1), (1, 0), (1, 1), (3, 0), (3, 1), (0, 0)):
                remote(
                    row_mid.at[t], rowy_in.at[t, y], y_send, y_recv.at[t],
                    (z * SIDE + y_peer(d), chip * 2 + c),
                )
            rowy_in[t, y] = total
            landed(rowy_in.at[t, 0:SIDE - 1], y_recv.at[t])

        return rowy_in[t, 0] + rowy_in[t, 1] + rowy_in[t, 2] + rowy_in[t, 3]

    def row_sums(slot, many):
        for g in range(many // 8):
            at = slice(g * 8, g * 8 + 8)
            sums = [None, None]
            for n in range(width // 128):
                lanes = slice(n * 128, (n + 1) * 128)
                term = massf[slot, at, lanes] * colb[:, lanes]
                sums[n % 2] = term if sums[n % 2] is None else sums[n % 2] + term
            row_acc[slot, at, :] = sums[0] + sums[1]

    def turn(slot, b):
        return jnp.sum(row_acc[slot, b * 128:(b + 1) * 128, :].T, axis=0, keepdims=True)

    half = R // 2
    rid8, lane8 = iota((8, half), 0), iota((8, half), 1)
    spot = lax.rem(rid8, 2) * half + lane8
    queue_row = (z * SIDE + rid8 // 2) * Q + spot - B
    live = jnp.where(jnp.logical_or(spot < B, queue_row < fill), 1.0, 0.0)

    for t in range(ITERS):
        column_exchange(t)
        if t + 1 == ITERS:
            break

        def row_block(slot, carry, t=t):
            row_sums(slot, V)
            rest = lax.dot_general(col16[...], massb[slot], NT, preferred_element_type=F32)
            rest = jnp.sum(rest, axis=0, keepdims=True)
            parts = [turn(slot, b) for b in range(V // 128)] + [rest[:, 0:128], rest[:, 128:256]]
            for h in range(2):
                row_part[t, pl.ds(2 * slot + h, 1), :] = jnp.concatenate(parts[3 * h:3 * h + 3], axis=1)
            return carry

        lax.fori_loop(0, SIDE, row_block, 0)
        weight = live / row_exchange(t)
        for slot in range(SIDE):
            row16[slot] = stack16(weight[2 * slot + 1:2 * slot + 2, 128:half])
            for b in range(V // 128):
                at = slice((b % 3) * 128, (b % 3 + 1) * 128)
                line = weight[2 * slot + b // 3:2 * slot + b // 3 + 1, at]
                row_wide[slot, b * 128:(b + 1) * 128, :] = jnp.broadcast_to(line, (128, 128)).T

        def column_block(slot, sums):
            rest = jnp.dot(row16[slot], massb[slot], preferred_element_type=F32)
            sums = list(sums)
            for g in range(V // 8):
                at = slice(g * 8, g * 8 + 8)
                scale = row_wide[slot, at, :]
                for n in range(width // 128):
                    sums[n] = sums[n] + massf[slot, at, n * 128:(n + 1) * 128] * scale
            return tuple(sums[n] + rest[0:8, n * 128:(n + 1) * 128] for n in range(width // 128))

        sums = lax.fori_loop(
            0, SIDE, column_block, tuple(jnp.zeros((8, 128), F32) for _ in range(width // 128))
        )
        for n in range(width // 128):
            at = slice((n % 2) * 128, (n % 2 + 1) * 128)
            col_part[t + 1, n // 2:n // 2 + 1, at] = jnp.sum(sums[n], axis=0, keepdims=True)

    last = ITERS - 1
    for slot in range(SIDE):
        row_sums(slot, B)
        for b in range(B // 128):
            row_part[last, 2 * slot:2 * slot + 1, b * 128:(b + 1) * 128] = turn(slot, b)
        row_part[last, 2 * slot + 1:2 * slot + 2, 0:B] = jnp.concatenate(
            [
                jnp.sum(soft_acc[slot, 0:128, :].T, axis=0, keepdims=True),
                jnp.sum(soft_acc[slot, 128:256, :].T, axis=0, keepdims=True),
            ],
            axis=1,
        )
        row_part[last, 2 * slot:2 * slot + 2, B:half] = jnp.ones((2, half - B), F32)
        eye = jnp.where(rid == cid, 1.0, 0.0).astype(BF16)
        turned[:, slot * B:(slot + 1) * B] = lax.dot_general(
            eye, rows[slot, 0:B, :], NT, preferred_element_type=F32
        ).astype(BF16)
    sums = row_exchange(last)
    for slot in range(SIDE):
        code = sums[2 * slot:2 * slot + 1, 0:B]
        soft = sums[2 * slot + 1:2 * slot + 2, 0:B]
        for target, value in ((row_code, (10.0 / (CROPS - 1)) / code), (row_soft, 10.0 / soft)):
            for h in range(2):
                target[slot, h * 128:(h + 1) * 128, :] = jnp.broadcast_to(
                    value[:, h * 128:(h + 1) * 128], (128, 128)
                ).T
    sublane = iota((8, B), 0)
    logs = jnp.log(sums[:, 0:B])
    mine = jnp.logical_and(sublane == 2 * y + 1, me == 0)
    logs = jnp.where(mine, logs, 0.0)
    logs = logs[:, 0:128] + logs[:, 128:256]

    images = B // CROPS
    slab = B // LANES

    def slope_chunk(slot, k, lost):
        for h in range(span // 128):
            lanes = pl.ds(pl.multiple_of(k * span + h * 128, 128), 128)
            column = colb[:, lanes]
            for i in range(images // 8):
                softs, parts, scores = [], [], []
                for c in range(CROPS):
                    at = slice(c * images + i * 8, c * images + i * 8 + 8)
                    s = score[slot, at, lanes]
                    e = jnp.exp2(s)
                    parts.append(e * e * column * row_code[slot, at, :])
                    softs.append(e * row_soft[slot, at, :])
                    scores.append(s)
                total = parts[0]
                for c in range(1, CROPS):
                    total = total + parts[c]
                for c in range(CROPS):
                    at = slice(c * images + i * 8, c * images + i * 8 + 8)
                    goal = total - parts[c]
                    lost = lost + goal * scores[c]
                    grad[slot, at, lanes] = (softs[c] - goal).astype(BF16)
        return lost

    def normed_chunk(slot, k):
        cols = pl.ds(pl.multiple_of(k * span, span), span)
        return lax.dot_general(grad[slot, :, cols], protos[:, cols], NT, preferred_element_type=F32)

    side = B // 2
    own_half = pl.ds(pl.multiple_of(core * side, side), side)
    other_half = pl.ds(pl.multiple_of((1 - core) * side, side), side)

    def to_sibling(n):
        remote(ng_out.at[n, other_half, :], ngc_in.at[n], e_send, e_recv.at[n], (row, sibling))

    def to_chips(n):
        landed(ngc_in.at[n], e_recv.at[n])
        ng_pair[n] = ng_out[n, own_half, :] + ngc_in[n]
        for d in (2, 1, 3):
            to_chip = lax.rem(chip + d, SIDE)
            remote(
                ng_pair.at[n, pl.ds(pl.multiple_of(to_chip * slab, slab), slab), :],
                ng_in.at[n, chip], n_send, n_recv.at[n], (row, to_chip * 2 + core),
            )
        ng_in[n, chip] = ng_pair[n, pl.ds(pl.multiple_of(chip * slab, slab), slab), :]

    def sum_normed(n):
        landed(ng_in.at[n, 0:SIDE - 1], n_recv.at[n])
        return ng_in[n, 0] + ng_in[n, 1] + ng_in[n, 2] + ng_in[n, 3]

    def send_protos(k):
        for h in range(span // TILE):
            cols = slice(k * span + h * TILE, k * span + (h + 1) * TILE)
            part = jnp.dot(turned[:, 0:B], grad[0, :, cols], preferred_element_type=F32)
            for other in range(1, SIDE):
                part = part + jnp.dot(
                    turned[:, other * B:(other + 1) * B], grad[other, :, cols],
                    preferred_element_type=F32,
                )
            gp_out[:, cols] = part.astype(BF16)
        for dz, dy in (
            (2, 2), (2, 1), (2, 3), (1, 2), (3, 2), (1, 1), (1, 3), (3, 1), (3, 3),
            (2, 0), (0, 2), (1, 0), (3, 0), (0, 1), (0, 3),
        ):
            peer = z_peer(dz) * SIDE + y_peer(dy)
            remote(
                gp_out.at[pl.ds(pl.multiple_of(peer * 16, 16), 16), k * span:(k + 1) * span],
                gp_in.at[z, y, k], g_send, g_recv, (peer, me),
            )

    def pass_normed(n):
        ng_sum[n] = sum_normed(n)
        d = order[n]
        remote(ng_sum.at[n], ngy_in.at[d], m_send, m_recv, (z * SIDE + y_peer(d), me))

    order = (2, 1, 3, 0)
    lost = jnp.zeros((8, 128), F32)
    for n in range(SIDE):
        slot = y_peer(order[n])
        if n:
            ng_out[n - 1] = jnp.zeros((B, D), F32)

        def block_chunk(k, lost, n=n, slot=slot):
            lost = slope_chunk(slot, k, lost)
            if n:
                ng_out[n - 1] += normed_chunk(y_peer(order[n - 1]), k)
            return lost

        lost = lax.fori_loop(0, chunks, block_chunk, lost)
        if n >= 1:
            to_sibling(n - 1)
        if n >= 2:
            to_chips(n - 2)
    lx_in[me] = logs - lost * (math.log(2.0) / 10.0)
    for d in range(1, LANES):
        remote(lx_in.at[me], lx_in.at[me], lx_send, lx_recv, (row, p_peer(d)))
    ng_out[SIDE - 1] = lax.dot_general(grad[y], protos[...], NT, preferred_element_type=F32)
    to_sibling(SIDE - 1)
    to_chips(SIDE - 2)
    send_protos(0)
    to_chips(SIDE - 1)
    send_protos(1)
    pass_normed(0)
    pass_normed(1)
    pass_normed(2)
    landed(lx_in.at[0:LANES - 1], lx_recv)
    lost = lx_in[0]
    for k in range(1, LANES):
        lost = lost + lx_in[k]
    lz_in[row] = lost
    for dz in range(SIDE):
        for dy in range(SIDE):
            if dz or dy:
                remote(
                    lz_in.at[row], lz_in.at[row], lz_send, lz_recv, (z_peer(dz) * SIDE + y_peer(dy), me)
                )
    send_protos(2)
    send_protos(3)
    total = sum_normed(3)
    landed(ngy_in.at[0:SIDE - 1], m_recv)
    mine_at = core * SIDE + chip
    ng_all[mine_at] = total + ngy_in[1] + ngy_in[2] + ngy_in[3]
    for d in (4, 3, 5, 2, 6, 1, 7):
        remote(ng_all.at[mine_at], ng_all.at[mine_at], h_send, h_recv, (row, p_peer(d)))

    landed(ng_all.at[0:LANES - 1], h_recv)
    gathered = ng_all[...].reshape(B, D)
    normed_grad = jnp.zeros((B, D), F32)
    for term in split3(gathered):
        normed_grad = normed_grad + jnp.dot(back[...], term.astype(BF16), preferred_element_type=F32)
    along = jnp.sum(unit[...] * normed_grad, axis=1, keepdims=True)
    rest = normed_grad - unit[...] * along
    for h in range(D // 128):
        ge_ref[:, h * 128:(h + 1) * 128] = factor[...] * rest[:, h * 128:(h + 1) * 128]

    landed(lz_in.at[0:SIDE * SIDE - 1], lz_recv)
    lost = lz_in[0]
    for k in range(1, SIDE * SIDE):
        lost = lost + lz_in[k]
    loss_ref[0] = jnp.sum(lost) * (1.0 / (B * SIDE * SIDE))

    for k in range(chunks):
        gp_in[z, y, k] = gp_out[dims, k * span:(k + 1) * span]
    landed(gp_out.at[0:240, :], g_recv)
    for n in range(SIDE):
        for k in range(chunks):
            start = n * width + k * span
            gp_ref[:, start:start + span] = (
                gp_in[0, n, k].astype(F32) + gp_in[1, n, k].astype(F32)
                + gp_in[2, n, k].astype(F32) + gp_in[3, n, k].astype(F32)
            )
    left(protos.at[0:192, 0:span], a_send)
    left(protos.at[0:192, :], z_send)
    left(rows.at[0:3, 0:R // 2, :], r_send)
    left(rows.at[0:3, 0:R // 2, :], f_send)
    left(col_in.at[:, 0:SIDE - 1], c_send)
    left(gp_out.at[0:240, :], g_send)
    left(ng_in.at[:, 0:SIDE - 1], n_send)
    left(ngc_in, e_send)
    left(ngy_in.at[0:SIDE - 1], m_send)
    left(ng_all.at[0:LANES - 1], h_send)
    left(lx_in.at[0:LANES - 1], lx_send)
    left(lz_in.at[0:SIDE * SIDE - 1], lz_send)

    @pl.when(core == 0)
    def _():
        left(rowx_in.at[:, 0:SIDE], x_send)

    @pl.when(core == 1)
    def _():
        left(rowx_in.at[:, 0:SIDE - 1], x_send)
        left(rowx_in.at[:, 0:LANES - 1], y_send)


def body(embeddings, queue_feats, prototypes, crop_image, fill_count):
    width = prototypes.shape[1] // SIDE
    half = R // 2
    chunks = 4
    vmem = pl.BlockSpec(memory_space=pltpu.VMEM)
    smem = pl.BlockSpec(memory_space=pltpu.SMEM)
    hbm = pl.BlockSpec(memory_space=pl.ANY)
    dma = pltpu.SemaphoreType.DMA
    slab = B // LANES

    def group(*shape):
        return [dma, dma(shape) if shape else dma]

    scratch = [
        pltpu.VMEM((B, D), BF16),
        pltpu.VMEM((Q, D), BF16),
        pltpu.VMEM(prototypes.shape, BF16),
        pltpu.VMEM((SIDE, R, D), BF16),
        pltpu.VMEM((D, width), BF16),
        pltpu.VMEM((SIDE, V, width), F32),
        pltpu.VMEM((SIDE, R - V, width), BF16),
        pltpu.VMEM((SIDE, V, 128), F32),
        pltpu.VMEM((SIDE, V, 128), F32),
        pltpu.VMEM((SIDE, B, width), F32),
        pltpu.VMEM((SIDE, B, width), BF16),
        pltpu.VMEM((D, SIDE * B), BF16),
        pltpu.VMEM((SIDE, B, 128), F32),
        pltpu.VMEM((8, width), F32),
        pltpu.VMEM((SIDE, Q, 128), F32),
        pltpu.VMEM((SIDE, 16, R - V), BF16),
        pltpu.VMEM((16, width), BF16),
        pltpu.VMEM((8, width), F32),
        pltpu.VMEM((ITERS, 8, width // 8), F32),
        pltpu.VMEM((ITERS, 8, half), F32),
        pltpu.VMEM((ITERS, 8, half), F32),
        pltpu.VMEM((ITERS, SIDE, 8, width // 8), F32),
        pltpu.VMEM((ITERS, LANES, 8, half), F32),
        pltpu.VMEM((ITERS, SIDE, 8, half), F32),
        pltpu.VMEM((SIDE, B, 128), F32),
        pltpu.VMEM((SIDE, B, 128), F32),
        pltpu.VMEM((B, D), F32),
        pltpu.VMEM((B, 128), F32),
        pltpu.VMEM((B, B), BF16),
        pltpu.VMEM((D, width), BF16),
        pltpu.VMEM((SIDE, SIDE, chunks, 16, width // chunks), BF16),
        pltpu.VMEM((SIDE, B, D), F32),
        pltpu.VMEM((SIDE, B // 2, D), F32),
        pltpu.VMEM((SIDE, B // 2, D), F32),
        pltpu.VMEM((SIDE, SIDE, slab, D), F32),
        pltpu.VMEM((SIDE, slab, D), F32),
        pltpu.VMEM((SIDE, slab, D), F32),
        pltpu.VMEM((LANES, slab, D), F32),
        pltpu.VMEM((LANES, 8, 128), F32),
        pltpu.VMEM((SIDE * SIDE, 8, 128), F32),
        *group(chunks, SIDE), *group(chunks), *group(SIDE), *group(SIDE),
        *group(ITERS), *group(ITERS), *group(ITERS),
        *group(), *group(SIDE), *group(SIDE), *group(), *group(), *group(), *group(), dma((3,)),
    ]
    return pl.pallas_call(
        kernel,
        name="swav",
        out_shape=(
            pltpu.VMEM((B, D), F32),
            pltpu.VMEM((prototypes.shape[0], prototypes.shape[1]), F32),
            jax.ShapeDtypeStruct((1,), F32),
        ),
        in_specs=[smem, hbm, hbm, hbm, vmem],
        out_specs=(vmem, vmem, smem),
        scratch_shapes=scratch,
        compiler_params=pltpu.CompilerParams(
            collective_id=0, has_side_effects=True, vmem_limit_bytes=60 * 1024 * 1024
        ),
    )(fill_count, embeddings, queue_feats, prototypes, crop_image.reshape(1, B))


def solution(mesh):
    placed = (P("row", None), P("row", None), P("row", "proto"), P("row"), P())
    return jax.shard_map(
        body,
        mesh=mesh,
        in_specs=placed,
        out_specs=(P("row", None), P("row", "proto"), P()),
        check_vma=False,
    )
```

```python
import functools
import math

import jax
import jax.numpy as jnp
from jax import lax
from jax.experimental import pallas as pl
from jax.experimental.pallas import tpu as pltpu
from jax.sharding import PartitionSpec as P

MESH = pl.DeviceIdType.MESH
F32 = jnp.float32
BF16 = jnp.bfloat16

CROPS = 8
ITERS = 3
SIDE = 4
LANES = 8
SCALE = 10.0 * math.log2(math.e)

B = 256
Q = 512
R = B + Q
V = 512
D = 256
TILE = 256
NT = (((1,), (1,)), ((), ()))


def iota(shape, dim):
    return lax.broadcasted_iota(jnp.int32, shape, dim)


def split3(v):
    hi = v.astype(BF16).astype(F32)
    rest = v - hi
    mid = rest.astype(BF16).astype(F32)
    return hi, mid, rest - mid


def stack16(v):
    hi, mid, low = split3(v)
    rid = iota((16, v.shape[1]), 0)
    out = jnp.where(rid == 0, hi, jnp.where(rid == 1, mid, jnp.where(rid == 2, low, 0.0)))
    return out.astype(BF16)


def unit_rows(raw):
    values = raw.astype(F32)
    inverse = lax.rsqrt(jnp.sum(values * values, axis=1, keepdims=True) + 1e-06)
    return values * inverse, inverse


def kernel(
    fill_ref, emb_hbm, queue_hbm, proto_hbm, image_ref,
    ge_ref, gp_ref, loss_ref,
    emb_ref, queue_ref, proto_ref, rows, protos, massf, massb, row_acc, row_wide, score, grad, turned, soft_acc, col_acc, alive, row16, col16, colb,
    col_part, row_part, row_mid, col_in, rowx_in, rowy_in,
    row_soft, row_code, unit, factor, back,
    upright, gp_out, gp_in, ng_out, ngc_in, ng_pair, ng_in, ng_sum, ngy_in, ng_all, lx_in, lz_in,
    a_send, a_recv, z_send, z_recv, r_send, r_recv, f_send, f_recv,
    c_send, c_recv, x_send, x_recv, y_send, y_recv,
    g_send, g_recv, e_send, e_recv, n_send, n_recv, m_send, m_recv, h_send, h_recv, lx_send, lx_recv, lz_send, lz_recv, in_sem,
):
    row = lax.axis_index("row")
    me = lax.axis_index("proto")
    z = row // SIDE
    y = lax.rem(row, SIDE)
    core = lax.rem(me, 2)
    chip = me // 2
    sibling = chip * 2 + (1 - core)
    width = protos.shape[1]
    tiles = width // TILE
    chunks = gp_in.shape[2]
    span = width // chunks

    def y_peer(d):
        return lax.rem(y + d, SIDE)

    def z_peer(d):
        return lax.rem(z + d, SIDE)

    def p_peer(d):
        return lax.rem(me + d, LANES)

    def remote(src, dst, send, recv, device):
        copy = pltpu.make_async_remote_copy(
            src_ref=src, dst_ref=dst, send_sem=send, recv_sem=recv,
            device_id=device, device_id_type=MESH,
        )
        copy.start()
        return copy

    def landed(ref, recv):
        pltpu.make_async_remote_copy(
            src_ref=ref, dst_ref=ref, send_sem=recv, recv_sem=recv,
            device_id=(row, sibling), device_id_type=MESH,
        ).wait_recv()

    def left(ref, send):
        pltpu.make_async_remote_copy(
            src_ref=ref, dst_ref=ref, send_sem=send, recv_sem=send,
            device_id=(row, sibling), device_id_type=MESH,
        ).wait_send()

    loads = []
    for n, (source, target) in enumerate(
        ((emb_hbm, emb_ref), (queue_hbm, queue_ref), (proto_hbm, proto_ref))
    ):
        loads.append(pltpu.make_async_copy(source, target, in_sem.at[n]))
        loads[-1].start()
    barrier = pltpu.get_barrier_semaphore()
    count = 0
    for d in range(1, SIDE):
        for peer in (z * SIDE + y_peer(d), z_peer(d) * SIDE + y):
            pl.semaphore_signal(barrier, inc=1, device_id=(peer, me), device_id_type=MESH)
            count += 1
    for d in range(1, LANES):
        pl.semaphore_signal(barrier, inc=1, device_id=(row, p_peer(d)), device_id_type=MESH)
        count += 1

    image = image_ref[...].astype(F32)
    wide = jnp.broadcast_to(image, (B, B))
    rid, cid = iota((B, B), 0), iota((B, B), 1)
    tall = jnp.sum(jnp.where(rid == cid, wide, 0.0), axis=1, keepdims=True)
    same = jnp.where(wide == tall, 1.0, 0.0)
    base = (row * (B // CROPS)).astype(F32)
    place = jnp.sum(jnp.where(rid < cid, same, 0.0), axis=0, keepdims=True) * (B // CROPS) + (image - base)
    forward = jnp.where(rid.astype(F32) == place, 1.0, 0.0).astype(BF16)
    for copy in loads:
        copy.wait()
    exact, _ = unit_rows(emb_ref[...])
    ordered = jnp.dot(forward, exact.astype(BF16), preferred_element_type=F32).astype(BF16)
    rows[y, 0:B, :] = ordered
    rows[y, B:R, :] = unit_rows(queue_ref[...])[0].astype(BF16)
    dims = pl.ds(pl.multiple_of(row * 16, 16), 16)
    protos[dims, :] = proto_ref[:, pl.ds(pl.multiple_of(y * width, width), width)]

    pl.semaphore_wait(barrier, count)

    def from_y(k, d):
        return pltpu.make_async_remote_copy(
            src_ref=protos.at[dims, k * span:(k + 1) * span],
            dst_ref=protos.at[dims, k * span:(k + 1) * span],
            send_sem=a_send, recv_sem=a_recv.at[k, d], device_id=(row, sibling), device_id_type=MESH,
        )

    for k in range(chunks):
        for d in (1, 3, 2):
            remote(
                proto_ref.at[:, pl.ds(pl.multiple_of(y_peer(d) * width + k * span, span), span)],
                protos.at[dims, k * span:(k + 1) * span], a_send, a_recv.at[k, d],
                (z * SIDE + y_peer(d), me),
            )
    shared = pl.ds(pl.multiple_of(core * (R // 2), R // 2), R // 2)
    for d in (1, 3, 2):
        remote(
            rows.at[y, shared, :], rows.at[y, shared, :], r_send, r_recv.at[d],
            (z * SIDE + y_peer(d), me),
        )
    def to_z(k, source):
        slot = lax.rem(y + SIDE - source, SIDE)
        part = protos.at[pl.ds(pl.multiple_of((z * SIDE + slot) * 16, 16), 16), k * span:(k + 1) * span]
        for d in (1, 3, 2):
            remote(part, part, z_send, z_recv.at[k], (z_peer(d) * SIDE + y, me))

    for k in range(chunks):
        to_z(k, 0)
    for k in range(chunks):
        for source in (1, 3, 2):
            from_y(k, source).wait_recv()
            to_z(k, source)

    soft_acc[...] = jnp.zeros_like(soft_acc)
    col_acc[...] = jnp.zeros_like(col_acc)
    fill = fill_ref[0]
    for slot in range(SIDE):
        place = (z * SIDE + slot) * Q + iota((Q, 128), 0)
        alive[slot] = jnp.where(place < fill, 1.0, 0.0)
    place = jnp.sum(jnp.where(cid < rid, same, 0.0), axis=1, keepdims=True) * (B // CROPS) + (tall - base)
    back[...] = jnp.where(cid.astype(F32) == place, 1.0, 0.0).astype(BF16)
    exact, inverse = unit_rows(emb_ref[...])
    unit[...] = exact
    factor[...] = jnp.broadcast_to(inverse, (B, 128))

    def score_chunk(slot, k):
        for h in range(span // TILE):
            cols = pl.ds(pl.multiple_of(k * span + h * TILE, TILE), TILE)
            total = jnp.dot(rows[slot], protos[:, cols], preferred_element_type=F32)
            crop = total[0:B] * SCALE
            score[slot, :, cols] = crop
            soft = jnp.exp2(crop)
            soft_acc[slot] += soft[:, 0:128] + soft[:, 128:256]
            code = soft * soft
            massf[slot, 0:B, cols] = code
            rest = jnp.exp2(total[B:R] * (2.0 * SCALE))
            massf[slot, B:V, cols] = rest[0:V - B]
            massb[slot, :, cols] = rest[V - B:].astype(BF16)
            live = alive[slot]
            for g in range(TILE // 128):
                lanes = slice(g * 128, (g + 1) * 128)
                part = jnp.sum(code[:, lanes].reshape(B // 8, 8, 128), axis=0)
                part = part + jnp.sum((rest[:, lanes] * live).reshape(Q // 8, 8, 128), axis=0)
                at = pl.ds(pl.multiple_of(k * span + h * TILE + g * 128, 128), 128)
                col_acc[:, at] += part

    def score_many(first_slot, slots, first_chunk, many):
        def step(i, carry):
            n = first_slot + i // many
            score_chunk(lax.rem(y + n + n // 2, SIDE), first_chunk + lax.rem(i, many))
            return carry

        lax.fori_loop(0, slots * many, step, 0)

    def z_arrived(k):
        landed(protos.at[0:192, 0:span], z_recv.at[k])

    def score_far(first_chunk, many):
        def step(i, carry):
            score_chunk(y_peer(2), first_chunk + i)
            return carry

        lax.fori_loop(0, many, step, 0)

    def hand_over(d):
        landed(rows.at[0, 0:R // 2, :], r_recv.at[d])
        slot = lax.rem(y + SIDE - d, SIDE)
        part = rows.at[slot, shared, :]
        remote(part, part, f_send, f_recv.at[d], (row, sibling))

    z_arrived(0)
    score_chunk(y, 0)
    hand_over(1)
    hand_over(3)
    z_arrived(1)
    score_chunk(y, 1)
    landed(rows.at[0, 0:R // 2, :], f_recv.at[1])
    landed(rows.at[0, 0:R // 2, :], f_recv.at[3])
    score_many(1, 2, 0, 2)
    hand_over(2)
    z_arrived(2)
    score_many(0, 3, 2, 1)
    z_arrived(3)
    score_many(0, 3, 3, 1)
    landed(rows.at[0, 0:R // 2, :], f_recv.at[2])
    score_far(0, chunks)
    for j in range(tiles):
        col_part[0, j:j + 1, :] = jnp.sum(col_acc[:, j * TILE:(j + 1) * TILE], axis=0, keepdims=True)

    def idle_work(t):
        eye = jnp.where(rid == cid, 1.0, 0.0).astype(BF16)
        if t == 0:
            for slot in range(SIDE):
                turned[:, slot * B:(slot + 1) * B] = lax.dot_general(
                    eye, rows[slot, 0:B, :], NT, preferred_element_type=F32
                ).astype(BF16)
                row_part[last, 2 * slot + 1:2 * slot + 2, 0:B] = jnp.concatenate(
                    [
                        jnp.sum(soft_acc[slot, 0:128, :].T, axis=0, keepdims=True),
                        jnp.sum(soft_acc[slot, 128:256, :].T, axis=0, keepdims=True),
                    ],
                    axis=1,
                )
                row_part[last, 2 * slot:2 * slot + 2, B:half] = jnp.ones((2, half - B), F32)
        elif t == 1:
            for j in range(tiles):
                at = slice(j * TILE, (j + 1) * TILE)
                upright[at, :] = lax.dot_general(
                    eye, protos[:, at], NT, preferred_element_type=F32
                ).astype(BF16)

    last = ITERS - 1
    half = R // 2

    def column_exchange(t):
        for d in (2, 1, 3):
            remote(
                col_part.at[t], col_in.at[t, z], c_send, c_recv.at[t], (z_peer(d) * SIDE + y, me)
            )
        col_in[t, z] = col_part[t]
        idle_work(t)
        landed(col_in.at[t, 0:SIDE - 1], c_recv.at[t])
        column = 1.0 / (col_in[t, 0] + col_in[t, 1] + col_in[t, 2] + col_in[t, 3])
        for j in range(tiles):
            col16[:, j * TILE:(j + 1) * TILE] = stack16(column[j:j + 1, :])
            colb[:, j * TILE:(j + 1) * TILE] = jnp.broadcast_to(column[j:j + 1, :], (8, TILE))

    def row_exchange(t):
        for d in (2, 1, 3):
            remote(
                row_part.at[t], rowx_in.at[t, me], x_send, x_recv.at[t],
                (row, lax.rem(chip + d, SIDE) * 2 + 1),
            )

        @pl.when(core == 0)
        def _():
            remote(row_part.at[t], rowx_in.at[t, me], x_send, x_recv.at[t], (row, sibling))
            landed(rowy_in.at[t], y_recv.at[t])

        @pl.when(core == 1)
        def _():
            rowx_in[t, me] = row_part[t]
            landed(rowx_in.at[t, 0:LANES - 1], x_recv.at[t])
            total = rowx_in[t, 0]
            for k in range(1, LANES):
                total = total + rowx_in[t, k]
            row_mid[t] = total
            for d, c in ((2, 0), (2, 1), (1, 0), (1, 1), (3, 0), (3, 1), (0, 0)):
                remote(
                    row_mid.at[t], rowy_in.at[t, y], y_send, y_recv.at[t],
                    (z * SIDE + y_peer(d), chip * 2 + c),
                )
            rowy_in[t, y] = total
            landed(rowy_in.at[t, 0:SIDE - 1], y_recv.at[t])

        return rowy_in[t, 0] + rowy_in[t, 1] + rowy_in[t, 2] + rowy_in[t, 3]

    def row_sums(slot, many):
        for g in range(many // 8):
            at = slice(g * 8, g * 8 + 8)
            sums = [None, None]
            for n in range(width // 128):
                lanes = slice(n * 128, (n + 1) * 128)
                term = massf[slot, at, lanes] * colb[:, lanes]
                sums[n % 2] = term if sums[n % 2] is None else sums[n % 2] + term
            row_acc[slot, at, :] = sums[0] + sums[1]

    def turn(slot, b):
        return jnp.sum(row_acc[slot, b * 128:(b + 1) * 128, :].T, axis=0, keepdims=True)

    rid8, lane8 = iota((8, half), 0), iota((8, half), 1)
    spot = lax.rem(rid8, 2) * half + lane8
    queue_row = (z * SIDE + rid8 // 2) * Q + spot - B
    live = jnp.where(jnp.logical_or(spot < B, queue_row < fill), 1.0, 0.0)

    for t in range(ITERS):
        column_exchange(t)
        if t + 1 == ITERS:
            break

        def row_block(slot, carry, t=t):
            row_sums(slot, V)
            rest = lax.dot_general(col16[...], massb[slot], NT, preferred_element_type=F32)
            rest = jnp.sum(rest, axis=0, keepdims=True)
            parts = [turn(slot, b) for b in range(V // 128)] + [rest[:, 0:128], rest[:, 128:256]]
            for h in range(2):
                row_part[t, pl.ds(2 * slot + h, 1), :] = jnp.concatenate(parts[3 * h:3 * h + 3], axis=1)
            return carry

        lax.fori_loop(0, SIDE, row_block, 0)
        weight = live / row_exchange(t)
        for slot in range(SIDE):
            row16[slot] = stack16(weight[2 * slot + 1:2 * slot + 2, 128:half])
            for b in range(V // 128):
                at = slice((b % 3) * 128, (b % 3 + 1) * 128)
                line = weight[2 * slot + b // 3:2 * slot + b // 3 + 1, at]
                row_wide[slot, b * 128:(b + 1) * 128, :] = jnp.broadcast_to(line, (128, 128)).T

        def column_block(slot, sums):
            rest = jnp.dot(row16[slot], massb[slot], preferred_element_type=F32)
            sums = list(sums)
            for g in range(V // 8):
                at = slice(g * 8, g * 8 + 8)
                scale = row_wide[slot, at, :]
                for n in range(width // 128):
                    sums[n] = sums[n] + massf[slot, at, n * 128:(n + 1) * 128] * scale
            return tuple(sums[n] + rest[0:8, n * 128:(n + 1) * 128] for n in range(width // 128))

        sums = lax.fori_loop(
            0, SIDE, column_block, tuple(jnp.zeros((8, 128), F32) for _ in range(width // 128))
        )
        for n in range(width // 128):
            at = slice((n % 2) * 128, (n % 2 + 1) * 128)
            col_part[t + 1, n // 2:n // 2 + 1, at] = jnp.sum(sums[n], axis=0, keepdims=True)

    for slot in range(SIDE):
        row_sums(slot, B)
        for b in range(B // 128):
            row_part[last, 2 * slot:2 * slot + 1, b * 128:(b + 1) * 128] = turn(slot, b)
    sums = row_exchange(last)
    for slot in range(SIDE):
        code = sums[2 * slot:2 * slot + 1, 0:B]
        soft = sums[2 * slot + 1:2 * slot + 2, 0:B]
        for target, value in ((row_code, (10.0 / (CROPS - 1)) / code), (row_soft, 10.0 / soft)):
            for h in range(2):
                target[slot, h * 128:(h + 1) * 128, :] = jnp.broadcast_to(
                    value[:, h * 128:(h + 1) * 128], (128, 128)
                ).T
    sublane = iota((8, B), 0)
    logs = jnp.log(sums[:, 0:B])
    mine = jnp.logical_and(sublane == 2 * y + 1, me == 0)
    logs = jnp.where(mine, logs, 0.0)
    logs = logs[:, 0:128] + logs[:, 128:256]

    images = B // CROPS
    slab = B // LANES

    def slope_chunk(slot, k, lost):
        for h in range(span // 128):
            lanes = pl.ds(pl.multiple_of(k * span + h * 128, 128), 128)
            column = colb[:, lanes]
            for i in range(images // 8):
                softs, parts, scores = [], [], []
                for c in range(CROPS):
                    at = slice(c * images + i * 8, c * images + i * 8 + 8)
                    s = score[slot, at, lanes]
                    e = jnp.exp2(s)
                    parts.append(e * e * column * row_code[slot, at, :])
                    softs.append(e * row_soft[slot, at, :])
                    scores.append(s)
                total = parts[0]
                for c in range(1, CROPS):
                    total = total + parts[c]
                for c in range(CROPS):
                    at = slice(c * images + i * 8, c * images + i * 8 + 8)
                    goal = total - parts[c]
                    lost = lost + goal * scores[c]
                    grad[slot, at, lanes] = (softs[c] - goal).astype(BF16)
        return lost

    side = B // 2
    own_half = pl.ds(pl.multiple_of(core * side, side), side)
    other_half = pl.ds(pl.multiple_of((1 - core) * side, side), side)

    def to_sibling(n):
        remote(ng_out.at[n, other_half, :], ngc_in.at[n], e_send, e_recv.at[n], (row, sibling))

    def to_chips(n):
        landed(ngc_in.at[n], e_recv.at[n])
        ng_pair[n] = ng_out[n, own_half, :] + ngc_in[n]
        for d in (2, 1, 3):
            to_chip = lax.rem(chip + d, SIDE)
            remote(
                ng_pair.at[n, pl.ds(pl.multiple_of(to_chip * slab, slab), slab), :],
                ng_in.at[n, chip], n_send, n_recv.at[n], (row, to_chip * 2 + core),
            )
        ng_in[n, chip] = ng_pair[n, pl.ds(pl.multiple_of(chip * slab, slab), slab), :]

    def sum_normed(n):
        landed(ng_in.at[n, 0:SIDE - 1], n_recv.at[n])
        return ng_in[n, 0] + ng_in[n, 1] + ng_in[n, 2] + ng_in[n, 3]

    def make_protos(k):
        for h in range(span // TILE):
            cols = slice(k * span + h * TILE, k * span + (h + 1) * TILE)
            part = jnp.dot(turned[:, 0:B], grad[0, :, cols], preferred_element_type=F32)
            for other in range(1, SIDE):
                part = part + jnp.dot(
                    turned[:, other * B:(other + 1) * B], grad[other, :, cols],
                    preferred_element_type=F32,
                )
            gp_out[:, cols] = part.astype(BF16)

    def send_protos(k):
        for dz, dy in (
            (2, 2), (2, 1), (2, 3), (1, 2), (3, 2), (1, 1), (1, 3), (3, 1), (3, 3),
            (2, 0), (0, 2), (1, 0), (3, 0), (0, 1), (0, 3),
        ):
            peer = z_peer(dz) * SIDE + y_peer(dy)
            remote(
                gp_out.at[pl.ds(pl.multiple_of(peer * 16, 16), 16), k * span:(k + 1) * span],
                gp_in.at[z, y, k], g_send, g_recv, (peer, me),
            )

    def pass_normed(n):
        ng_sum[n] = sum_normed(n)
        d = order[n]
        remote(ng_sum.at[n], ngy_in.at[d], m_send, m_recv, (z * SIDE + y_peer(d), me))

    order = (2, 1, 3, 0)
    lost = jnp.zeros((8, 128), F32)
    for k in range(chunks):
        lost = lax.fori_loop(0, SIDE, lambda slot, lost, k=k: slope_chunk(slot, k, lost), lost)
        if k + 1 < chunks:
            make_protos(k)
            send_protos(k)
    lx_in[me] = logs - lost * (math.log(2.0) / 10.0)
    for d in range(1, LANES):
        remote(lx_in.at[me], lx_in.at[me], lx_send, lx_recv, (row, p_peer(d)))
    for n in range(SIDE):
        ng_out[n] = jnp.dot(grad[y_peer(order[n])], upright[...], preferred_element_type=F32)
        to_sibling(n)
        if n:
            to_chips(n - 1)
    make_protos(chunks - 1)
    to_chips(SIDE - 1)
    pass_normed(0)
    pass_normed(1)
    pass_normed(2)
    send_protos(chunks - 1)
    landed(lx_in.at[0:LANES - 1], lx_recv)
    lost = lx_in[0]
    for k in range(1, LANES):
        lost = lost + lx_in[k]
    lz_in[row] = lost
    for dz in range(SIDE):
        for dy in range(SIDE):
            if dz or dy:
                remote(
                    lz_in.at[row], lz_in.at[row], lz_send, lz_recv, (z_peer(dz) * SIDE + y_peer(dy), me)
                )
    total = sum_normed(3)
    landed(ngy_in.at[0:SIDE - 1], m_recv)
    mine_at = core * SIDE + chip
    ng_all[mine_at] = total + ngy_in[1] + ngy_in[2] + ngy_in[3]
    for d in (4, 3, 5, 2, 6, 1, 7):
        remote(ng_all.at[mine_at], ng_all.at[mine_at], h_send, h_recv, (row, p_peer(d)))

    landed(ng_all.at[0:LANES - 1], h_recv)
    gathered = ng_all[...].reshape(B, D)
    normed_grad = jnp.zeros((B, D), F32)
    for term in split3(gathered):
        normed_grad = normed_grad + jnp.dot(back[...], term.astype(BF16), preferred_element_type=F32)
    along = jnp.sum(unit[...] * normed_grad, axis=1, keepdims=True)
    rest = normed_grad - unit[...] * along
    for h in range(D // 128):
        ge_ref[:, h * 128:(h + 1) * 128] = factor[...] * rest[:, h * 128:(h + 1) * 128]

    landed(lz_in.at[0:SIDE * SIDE - 1], lz_recv)
    lost = lz_in[0]
    for k in range(1, SIDE * SIDE):
        lost = lost + lz_in[k]
    loss_ref[0] = jnp.sum(lost) * (1.0 / (B * SIDE * SIDE))

    for k in range(chunks):
        gp_in[z, y, k] = gp_out[dims, k * span:(k + 1) * span]
    landed(gp_out.at[0:240, :], g_recv)
    for n in range(SIDE):
        for k in range(chunks):
            start = n * width + k * span
            gp_ref[:, start:start + span] = (
                gp_in[0, n, k].astype(F32) + gp_in[1, n, k].astype(F32)
                + gp_in[2, n, k].astype(F32) + gp_in[3, n, k].astype(F32)
            )
    left(protos.at[0:192, 0:span], a_send)
    left(protos.at[0:192, :], z_send)
    left(rows.at[0:3, 0:R // 2, :], r_send)
    left(rows.at[0:3, 0:R // 2, :], f_send)
    left(col_in.at[:, 0:SIDE - 1], c_send)
    left(gp_out.at[0:240, :], g_send)
    left(ng_in.at[:, 0:SIDE - 1], n_send)
    left(ngc_in, e_send)
    left(ngy_in.at[0:SIDE - 1], m_send)
    left(ng_all.at[0:LANES - 1], h_send)
    left(lx_in.at[0:LANES - 1], lx_send)
    left(lz_in.at[0:SIDE * SIDE - 1], lz_send)

    @pl.when(core == 0)
    def _():
        left(rowx_in.at[:, 0:SIDE], x_send)

    @pl.when(core == 1)
    def _():
        left(rowx_in.at[:, 0:SIDE - 1], x_send)
        left(rowx_in.at[:, 0:LANES - 1], y_send)


def body(embeddings, queue_feats, prototypes, crop_image, fill_count):
    width = prototypes.shape[1] // SIDE
    half = R // 2
    chunks = 4
    vmem = pl.BlockSpec(memory_space=pltpu.VMEM)
    smem = pl.BlockSpec(memory_space=pltpu.SMEM)
    hbm = pl.BlockSpec(memory_space=pl.ANY)
    dma = pltpu.SemaphoreType.DMA
    slab = B // LANES

    def group(*shape):
        return [dma, dma(shape) if shape else dma]

    scratch = [
        pltpu.VMEM((B, D), BF16),
        pltpu.VMEM((Q, D), BF16),
        pltpu.VMEM(prototypes.shape, BF16),
        pltpu.VMEM((SIDE, R, D), BF16),
        pltpu.VMEM((D, width), BF16),
        pltpu.VMEM((SIDE, V, width), F32),
        pltpu.VMEM((SIDE, R - V, width), BF16),
        pltpu.VMEM((SIDE, V, 128), F32),
        pltpu.VMEM((SIDE, V, 128), F32),
        pltpu.VMEM((SIDE, B, width), F32),
        pltpu.VMEM((SIDE, B, width), BF16),
        pltpu.VMEM((D, SIDE * B), BF16),
        pltpu.VMEM((SIDE, B, 128), F32),
        pltpu.VMEM((8, width), F32),
        pltpu.VMEM((SIDE, Q, 128), F32),
        pltpu.VMEM((SIDE, 16, R - V), BF16),
        pltpu.VMEM((16, width), BF16),
        pltpu.VMEM((8, width), F32),
        pltpu.VMEM((ITERS, 8, width // 8), F32),
        pltpu.VMEM((ITERS, 8, half), F32),
        pltpu.VMEM((ITERS, 8, half), F32),
        pltpu.VMEM((ITERS, SIDE, 8, width // 8), F32),
        pltpu.VMEM((ITERS, LANES, 8, half), F32),
        pltpu.VMEM((ITERS, SIDE, 8, half), F32),
        pltpu.VMEM((SIDE, B, 128), F32),
        pltpu.VMEM((SIDE, B, 128), F32),
        pltpu.VMEM((B, D), F32),
        pltpu.VMEM((B, 128), F32),
        pltpu.VMEM((B, B), BF16),
        pltpu.VMEM((width, D), BF16),
        pltpu.VMEM((D, width), BF16),
        pltpu.VMEM((SIDE, SIDE, chunks, 16, width // chunks), BF16),
        pltpu.VMEM((SIDE, B, D), F32),
        pltpu.VMEM((SIDE, B // 2, D), F32),
        pltpu.VMEM((SIDE, B // 2, D), F32),
        pltpu.VMEM((SIDE, SIDE, slab, D), F32),
        pltpu.VMEM((SIDE, slab, D), F32),
        pltpu.VMEM((SIDE, slab, D), F32),
        pltpu.VMEM((LANES, slab, D), F32),
        pltpu.VMEM((LANES, 8, 128), F32),
        pltpu.VMEM((SIDE * SIDE, 8, 128), F32),
        *group(chunks, SIDE), *group(chunks), *group(SIDE), *group(SIDE),
        *group(ITERS), *group(ITERS), *group(ITERS),
        *group(), *group(SIDE), *group(SIDE), *group(), *group(), *group(), *group(), dma((3,)),
    ]
    return pl.pallas_call(
        kernel,
        name="swav",
        out_shape=(
            pltpu.VMEM((B, D), F32),
            pltpu.VMEM((prototypes.shape[0], prototypes.shape[1]), F32),
            jax.ShapeDtypeStruct((1,), F32),
        ),
        in_specs=[smem, hbm, hbm, hbm, vmem],
        out_specs=(vmem, vmem, smem),
        scratch_shapes=scratch,
        compiler_params=pltpu.CompilerParams(
            collective_id=0, has_side_effects=True, vmem_limit_bytes=60 * 1024 * 1024
        ),
    )(fill_count, embeddings, queue_feats, prototypes, crop_image.reshape(1, B))


def solution(mesh):
    placed = (P("row", None), P("row", None), P("row", "proto"), P("row"), P())
    return jax.shard_map(
        body,
        mesh=mesh,
        in_specs=placed,
        out_specs=(P("row", None), P("row", "proto"), P()),
        check_vma=False,
    )
```

```python
import functools
import math

import jax
import jax.numpy as jnp
from jax import lax
from jax.experimental import pallas as pl
from jax.experimental.pallas import tpu as pltpu
from jax.sharding import PartitionSpec as P

MESH = pl.DeviceIdType.MESH
F32 = jnp.float32
BF16 = jnp.bfloat16

CROPS = 8
ITERS = 3
SIDE = 4
LANES = 8
SCALE = 10.0 * math.log2(math.e)

B = 256
Q = 512
R = B + Q
V = 384
D = 256
TILE = 256
NT = (((1,), (1,)), ((), ()))


def iota(shape, dim):
    return lax.broadcasted_iota(jnp.int32, shape, dim)


def split3(v):
    hi = v.astype(BF16).astype(F32)
    rest = v - hi
    mid = rest.astype(BF16).astype(F32)
    return hi, mid, rest - mid


def stack16(v):
    hi, mid, low = split3(v)
    rid = iota((16, v.shape[1]), 0)
    out = jnp.where(rid == 0, hi, jnp.where(rid == 1, mid, jnp.where(rid == 2, low, 0.0)))
    return out.astype(BF16)


def unit_rows(raw):
    values = raw.astype(F32)
    inverse = lax.rsqrt(jnp.sum(values * values, axis=1, keepdims=True) + 1e-06)
    return values * inverse, inverse


def kernel(
    fill_ref, emb_hbm, queue_hbm, proto_hbm, image_hbm,
    ge_ref, gp_ref, loss_ref,
    emb_ref, queue_ref, proto_ref, image_ref, rows, protos, massf, massb, row_acc, row_wide, score, grad, turned, soft_acc, col_acc, alive, row16, col16, colb,
    col_part, row_part, row_mid, col_in, rowx_in, rowy_in,
    row_soft, row_code, unit, factor, back,
    upright, gp_out, gp_in, ng_out, ngc_in, ng_pair, ng_in, ng_sum, ngy_in, ng_all, lx_in, lz_in,
    a_send, a_recv, z_send, z_recv, r_send, r_recv, f_send, f_recv,
    c_send, c_recv, x_send, x_recv, y_send, y_recv,
    g_send, g_recv, e_send, e_recv, n_send, n_recv, m_send, m_recv, h_send, h_recv, lx_send, lx_recv, lz_send, lz_recv, in_sem,
):
    row = lax.axis_index("row")
    me = lax.axis_index("proto")
    z = row // SIDE
    y = lax.rem(row, SIDE)
    core = lax.rem(me, 2)
    chip = me // 2
    sibling = chip * 2 + (1 - core)
    width = protos.shape[1]
    tiles = width // TILE
    chunks = gp_in.shape[2]
    span = width // chunks

    def y_peer(d):
        return lax.rem(y + d, SIDE)

    def z_peer(d):
        return lax.rem(z + d, SIDE)

    def p_peer(d):
        return lax.rem(me + d, LANES)

    def remote(src, dst, send, recv, device):
        copy = pltpu.make_async_remote_copy(
            src_ref=src, dst_ref=dst, send_sem=send, recv_sem=recv,
            device_id=device, device_id_type=MESH,
        )
        copy.start()
        return copy

    def landed(ref, recv):
        pltpu.make_async_remote_copy(
            src_ref=ref, dst_ref=ref, send_sem=recv, recv_sem=recv,
            device_id=(row, sibling), device_id_type=MESH,
        ).wait_recv()

    def left(ref, send):
        pltpu.make_async_remote_copy(
            src_ref=ref, dst_ref=ref, send_sem=send, recv_sem=send,
            device_id=(row, sibling), device_id_type=MESH,
        ).wait_send()

    loads = []
    for n, (source, target) in enumerate(
        ((image_hbm, image_ref), (emb_hbm, emb_ref), (queue_hbm, queue_ref), (proto_hbm, proto_ref))
    ):
        loads.append(pltpu.make_async_copy(source, target, in_sem.at[n]))
        loads[-1].start()
    barrier = pltpu.get_barrier_semaphore()
    count = 0
    for d in range(1, SIDE):
        for peer in (z * SIDE + y_peer(d), z_peer(d) * SIDE + y):
            pl.semaphore_signal(barrier, inc=1, device_id=(peer, me), device_id_type=MESH)
            count += 1
    for d in range(1, LANES):
        pl.semaphore_signal(barrier, inc=1, device_id=(row, p_peer(d)), device_id_type=MESH)
        count += 1

    for copy in loads:
        copy.wait()
    image = image_ref[...].astype(F32)
    wide = jnp.broadcast_to(image, (B, B))
    rid, cid = iota((B, B), 0), iota((B, B), 1)
    tall = jnp.sum(jnp.where(rid == cid, wide, 0.0), axis=1, keepdims=True)
    same = jnp.where(wide == tall, 1.0, 0.0)
    base = (row * (B // CROPS)).astype(F32)
    place = jnp.sum(jnp.where(rid < cid, same, 0.0), axis=0, keepdims=True) * (B // CROPS) + (image - base)
    forward = jnp.where(rid.astype(F32) == place, 1.0, 0.0).astype(BF16)
    exact, _ = unit_rows(emb_ref[...])
    ordered = jnp.dot(forward, exact.astype(BF16), preferred_element_type=F32).astype(BF16)
    rows[y, 0:B, :] = ordered
    rows[y, B:R, :] = unit_rows(queue_ref[...])[0].astype(BF16)
    dims = pl.ds(pl.multiple_of(row * 16, 16), 16)
    protos[dims, :] = proto_ref[:, pl.ds(pl.multiple_of(y * width, width), width)]

    pl.semaphore_wait(barrier, count)

    def from_y(k, d):
        return pltpu.make_async_remote_copy(
            src_ref=protos.at[dims, k * span:(k + 1) * span],
            dst_ref=protos.at[dims, k * span:(k + 1) * span],
            send_sem=a_send, recv_sem=a_recv.at[k, d], device_id=(row, sibling), device_id_type=MESH,
        )

    for k in range(chunks):
        for d in (1, 3, 2):
            remote(
                proto_ref.at[:, pl.ds(pl.multiple_of(y_peer(d) * width + k * span, span), span)],
                protos.at[dims, k * span:(k + 1) * span], a_send, a_recv.at[k, d],
                (z * SIDE + y_peer(d), me),
            )
    shared = pl.ds(pl.multiple_of(core * (R // 2), R // 2), R // 2)
    for d in (1, 3, 2):
        remote(
            rows.at[y, shared, :], rows.at[y, shared, :], r_send, r_recv.at[d],
            (z * SIDE + y_peer(d), me),
        )
    def to_z(k, source):
        slot = lax.rem(y + SIDE - source, SIDE)
        part = protos.at[pl.ds(pl.multiple_of((z * SIDE + slot) * 16, 16), 16), k * span:(k + 1) * span]
        for d in (1, 3, 2):
            remote(part, part, z_send, z_recv.at[k], (z_peer(d) * SIDE + y, me))

    for k in range(chunks):
        to_z(k, 0)
    for k in range(chunks):
        for source in (1, 3, 2):
            from_y(k, source).wait_recv()
            to_z(k, source)

    soft_acc[...] = jnp.zeros_like(soft_acc)
    col_acc[...] = jnp.zeros_like(col_acc)
    fill = fill_ref[0]
    for slot in range(SIDE):
        place = (z * SIDE + slot) * Q + iota((Q, 128), 0)
        alive[slot] = jnp.where(place < fill, 1.0, 0.0)
    place = jnp.sum(jnp.where(cid < rid, same, 0.0), axis=1, keepdims=True) * (B // CROPS) + (tall - base)
    back[...] = jnp.where(cid.astype(F32) == place, 1.0, 0.0).astype(BF16)
    exact, inverse = unit_rows(emb_ref[...])
    unit[...] = exact
    factor[...] = jnp.broadcast_to(inverse, (B, 128))

    def score_chunk(slot, k):
        for h in range(span // TILE):
            cols = pl.ds(pl.multiple_of(k * span + h * TILE, TILE), TILE)
            total = jnp.dot(rows[slot], protos[:, cols], preferred_element_type=F32)
            crop = total[0:B] * SCALE
            score[slot, :, cols] = crop
            soft = jnp.exp2(crop)
            soft_acc[slot] += soft[:, 0:128] + soft[:, 128:256]
            code = soft * soft
            massf[slot, 0:B, cols] = code
            rest = jnp.exp2(total[B:R] * (2.0 * SCALE))
            massf[slot, B:V, cols] = rest[0:V - B]
            massb[slot, :, cols] = rest[V - B:].astype(BF16)
            live = alive[slot]
            for g in range(TILE // 128):
                lanes = slice(g * 128, (g + 1) * 128)
                part = jnp.sum(code[:, lanes].reshape(B // 8, 8, 128), axis=0)
                part = part + jnp.sum((rest[:, lanes] * live).reshape(Q // 8, 8, 128), axis=0)
                at = pl.ds(pl.multiple_of(k * span + h * TILE + g * 128, 128), 128)
                col_acc[:, at] += part

    def score_many(first_slot, slots, first_chunk, many):
        def step(i, carry):
            n = first_slot + i // many
            score_chunk(lax.rem(y + n + n // 2, SIDE), first_chunk + lax.rem(i, many))
            return carry

        lax.fori_loop(0, slots * many, step, 0)

    def z_arrived(k):
        landed(protos.at[0:192, 0:span], z_recv.at[k])

    def score_far(first_chunk, many):
        def step(i, carry):
            score_chunk(y_peer(2), first_chunk + i)
            return carry

        lax.fori_loop(0, many, step, 0)

    def hand_over(d):
        landed(rows.at[0, 0:R // 2, :], r_recv.at[d])
        slot = lax.rem(y + SIDE - d, SIDE)
        part = rows.at[slot, shared, :]
        remote(part, part, f_send, f_recv.at[d], (row, sibling))

    z_arrived(0)
    score_chunk(y, 0)
    hand_over(1)
    hand_over(3)
    z_arrived(1)
    score_chunk(y, 1)
    landed(rows.at[0, 0:R // 2, :], f_recv.at[1])
    landed(rows.at[0, 0:R // 2, :], f_recv.at[3])
    score_many(1, 2, 0, 2)
    hand_over(2)
    z_arrived(2)
    score_many(0, 3, 2, 1)
    z_arrived(3)
    score_many(0, 3, 3, 1)
    landed(rows.at[0, 0:R // 2, :], f_recv.at[2])
    score_far(0, chunks)
    for j in range(tiles):
        col_part[0, j:j + 1, :] = jnp.sum(col_acc[:, j * TILE:(j + 1) * TILE], axis=0, keepdims=True)

    def idle_work(t):
        eye = jnp.where(rid == cid, 1.0, 0.0).astype(BF16)
        if t == 0:
            for slot in range(SIDE):
                turned[:, slot * B:(slot + 1) * B] = lax.dot_general(
                    eye, rows[slot, 0:B, :], NT, preferred_element_type=F32
                ).astype(BF16)
                row_part[last, 2 * slot + 1:2 * slot + 2, 0:B] = jnp.concatenate(
                    [
                        jnp.sum(soft_acc[slot, 0:128, :].T, axis=0, keepdims=True),
                        jnp.sum(soft_acc[slot, 128:256, :].T, axis=0, keepdims=True),
                    ],
                    axis=1,
                )
                row_part[last, 2 * slot:2 * slot + 2, B:half] = jnp.ones((2, half - B), F32)
        elif t == 1:
            for j in range(tiles):
                at = slice(j * TILE, (j + 1) * TILE)
                upright[at, :] = lax.dot_general(
                    eye, protos[:, at], NT, preferred_element_type=F32
                ).astype(BF16)

    last = ITERS - 1
    half = R // 2

    def column_exchange(t):
        for d in (2, 1, 3):
            remote(
                col_part.at[t], col_in.at[t, z], c_send, c_recv.at[t], (z_peer(d) * SIDE + y, me)
            )
        col_in[t, z] = col_part[t]
        idle_work(t)
        landed(col_in.at[t, 0:SIDE - 1], c_recv.at[t])
        column = 1.0 / (col_in[t, 0] + col_in[t, 1] + col_in[t, 2] + col_in[t, 3])
        for j in range(tiles):
            col16[:, j * TILE:(j + 1) * TILE] = stack16(column[j:j + 1, :])
            colb[:, j * TILE:(j + 1) * TILE] = jnp.broadcast_to(column[j:j + 1, :], (8, TILE))

    def row_exchange(t):
        for d in (2, 1, 3):
            remote(
                row_part.at[t], rowx_in.at[t, me], x_send, x_recv.at[t],
                (row, lax.rem(chip + d, SIDE) * 2 + 1),
            )

        @pl.when(core == 0)
        def _():
            remote(row_part.at[t], rowx_in.at[t, me], x_send, x_recv.at[t], (row, sibling))
            landed(rowy_in.at[t], y_recv.at[t])

        @pl.when(core == 1)
        def _():
            rowx_in[t, me] = row_part[t]
            landed(rowx_in.at[t, 0:LANES - 1], x_recv.at[t])
            total = rowx_in[t, 0]
            for k in range(1, LANES):
                total = total + rowx_in[t, k]
            row_mid[t] = total
            for d, c in ((2, 0), (2, 1), (1, 0), (1, 1), (3, 0), (3, 1), (0, 0)):
                remote(
                    row_mid.at[t], rowy_in.at[t, y], y_send, y_recv.at[t],
                    (z * SIDE + y_peer(d), chip * 2 + c),
                )
            rowy_in[t, y] = total
            landed(rowy_in.at[t, 0:SIDE - 1], y_recv.at[t])

        return rowy_in[t, 0] + rowy_in[t, 1] + rowy_in[t, 2] + rowy_in[t, 3]

    def row_sums(slot, many):
        for g in range(many // 8):
            at = slice(g * 8, g * 8 + 8)
            sums = [None, None]
            for n in range(width // 128):
                lanes = slice(n * 128, (n + 1) * 128)
                term = massf[slot, at, lanes] * colb[:, lanes]
                sums[n % 2] = term if sums[n % 2] is None else sums[n % 2] + term
            row_acc[slot, at, :] = sums[0] + sums[1]

    def turn(slot, b):
        return jnp.sum(row_acc[slot, b * 128:(b + 1) * 128, :].T, axis=0, keepdims=True)

    rid8, lane8 = iota((8, half), 0), iota((8, half), 1)
    spot = lax.rem(rid8, 2) * half + lane8
    queue_row = (z * SIDE + rid8 // 2) * Q + spot - B
    live = jnp.where(jnp.logical_or(spot < B, queue_row < fill), 1.0, 0.0)

    for t in range(ITERS):
        column_exchange(t)
        if t + 1 == ITERS:
            break

        def row_block(slot, carry, t=t):
            row_sums(slot, V)
            rest = lax.dot_general(col16[...], massb[slot], NT, preferred_element_type=F32)
            rest = jnp.sum(rest, axis=0, keepdims=True)
            parts = [turn(slot, b) for b in range(V // 128)]
            parts += [rest[:, b * 128:(b + 1) * 128] for b in range((R - V) // 128)]
            for h in range(2):
                row_part[t, pl.ds(2 * slot + h, 1), :] = jnp.concatenate(parts[3 * h:3 * h + 3], axis=1)
            return carry

        lax.fori_loop(0, SIDE, row_block, 0)
        weight = live / row_exchange(t)
        for slot in range(SIDE):
            row16[slot] = stack16(weight[2 * slot + 1:2 * slot + 2, V - half:half])
            for b in range(V // 128):
                at = slice((b % 3) * 128, (b % 3 + 1) * 128)
                line = weight[2 * slot + b // 3:2 * slot + b // 3 + 1, at]
                row_wide[slot, b * 128:(b + 1) * 128, :] = jnp.broadcast_to(line, (128, 128)).T

        def column_block(slot, sums):
            rest = jnp.dot(row16[slot], massb[slot], preferred_element_type=F32)
            sums = list(sums)
            for g in range(V // 8):
                at = slice(g * 8, g * 8 + 8)
                scale = row_wide[slot, at, :]
                for n in range(width // 128):
                    sums[n] = sums[n] + massf[slot, at, n * 128:(n + 1) * 128] * scale
            return tuple(sums[n] + rest[0:8, n * 128:(n + 1) * 128] for n in range(width // 128))

        sums = lax.fori_loop(
            0, SIDE, column_block, tuple(jnp.zeros((8, 128), F32) for _ in range(width // 128))
        )
        for n in range(width // 128):
            at = slice((n % 2) * 128, (n % 2 + 1) * 128)
            col_part[t + 1, n // 2:n // 2 + 1, at] = jnp.sum(sums[n], axis=0, keepdims=True)

    for slot in range(SIDE):
        row_sums(slot, B)
        for b in range(B // 128):
            row_part[last, 2 * slot:2 * slot + 1, b * 128:(b + 1) * 128] = turn(slot, b)
    sums = row_exchange(last)
    for slot in range(SIDE):
        code = sums[2 * slot:2 * slot + 1, 0:B]
        soft = sums[2 * slot + 1:2 * slot + 2, 0:B]
        for target, value in ((row_code, (10.0 / (CROPS - 1)) / code), (row_soft, 10.0 / soft)):
            for h in range(2):
                target[slot, h * 128:(h + 1) * 128, :] = jnp.broadcast_to(
                    value[:, h * 128:(h + 1) * 128], (128, 128)
                ).T
    sublane = iota((8, B), 0)
    logs = jnp.log(sums[:, 0:B])
    mine = jnp.logical_and(sublane == 2 * y + 1, me == 0)
    logs = jnp.where(mine, logs, 0.0)
    logs = logs[:, 0:128] + logs[:, 128:256]

    images = B // CROPS
    slab = B // LANES

    def slope_chunk(slot, k, lost):
        for h in range(span // 128):
            lanes = pl.ds(pl.multiple_of(k * span + h * 128, 128), 128)
            column = colb[:, lanes]
            for i in range(images // 8):
                softs, parts, scores = [], [], []
                for c in range(CROPS):
                    at = slice(c * images + i * 8, c * images + i * 8 + 8)
                    s = score[slot, at, lanes]
                    e = jnp.exp2(s)
                    parts.append(e * e * column * row_code[slot, at, :])
                    softs.append(e * row_soft[slot, at, :])
                    scores.append(s)
                total = parts[0]
                for c in range(1, CROPS):
                    total = total + parts[c]
                for c in range(CROPS):
                    at = slice(c * images + i * 8, c * images + i * 8 + 8)
                    goal = total - parts[c]
                    lost = lost + goal * scores[c]
                    grad[slot, at, lanes] = (softs[c] - goal).astype(BF16)
        return lost

    side = B // 2
    own_half = pl.ds(pl.multiple_of(core * side, side), side)
    other_half = pl.ds(pl.multiple_of((1 - core) * side, side), side)

    def to_sibling(n):
        remote(ng_out.at[n, other_half, :], ngc_in.at[n], e_send, e_recv.at[n], (row, sibling))

    def to_chips(n):
        landed(ngc_in.at[n], e_recv.at[n])
        ng_pair[n] = ng_out[n, own_half, :] + ngc_in[n]
        for d in (2, 1, 3):
            to_chip = lax.rem(chip + d, SIDE)
            remote(
                ng_pair.at[n, pl.ds(pl.multiple_of(to_chip * slab, slab), slab), :],
                ng_in.at[n, chip], n_send, n_recv.at[n], (row, to_chip * 2 + core),
            )
        ng_in[n, chip] = ng_pair[n, pl.ds(pl.multiple_of(chip * slab, slab), slab), :]

    def sum_normed(n):
        landed(ng_in.at[n, 0:SIDE - 1], n_recv.at[n])
        return ng_in[n, 0] + ng_in[n, 1] + ng_in[n, 2] + ng_in[n, 3]

    def make_protos(k):
        for h in range(span // TILE):
            cols = slice(k * span + h * TILE, k * span + (h + 1) * TILE)
            part = jnp.dot(turned[:, 0:B], grad[0, :, cols], preferred_element_type=F32)
            for other in range(1, SIDE):
                part = part + jnp.dot(
                    turned[:, other * B:(other + 1) * B], grad[other, :, cols],
                    preferred_element_type=F32,
                )
            gp_out[:, cols] = part.astype(BF16)

    def send_protos(k):
        for dz, dy in (
            (2, 2), (2, 1), (2, 3), (1, 2), (3, 2), (1, 1), (1, 3), (3, 1), (3, 3),
            (2, 0), (0, 2), (1, 0), (3, 0), (0, 1), (0, 3),
        ):
            peer = z_peer(dz) * SIDE + y_peer(dy)
            remote(
                gp_out.at[pl.ds(pl.multiple_of(peer * 16, 16), 16), k * span:(k + 1) * span],
                gp_in.at[z, y, k], g_send, g_recv, (peer, me),
            )

    def pass_normed(n):
        ng_sum[n] = sum_normed(n)
        d = order[n]
        remote(ng_sum.at[n], ngy_in.at[d], m_send, m_recv, (z * SIDE + y_peer(d), me))

    order = (2, 1, 3, 0)
    lost = jnp.zeros((8, 128), F32)
    for k in range(chunks):
        lost = lax.fori_loop(0, SIDE, lambda slot, lost, k=k: slope_chunk(slot, k, lost), lost)
        if k + 2 < chunks:
            make_protos(k)
            send_protos(k)
    lx_in[me] = logs - lost * (math.log(2.0) / 10.0)
    for d in range(1, LANES):
        remote(lx_in.at[me], lx_in.at[me], lx_send, lx_recv, (row, p_peer(d)))
    for n in range(SIDE):
        ng_out[n] = jnp.dot(grad[y_peer(order[n])], upright[...], preferred_element_type=F32)
        to_sibling(n)
        if n:
            to_chips(n - 1)
        if n == 1:
            make_protos(chunks - 2)
            send_protos(chunks - 2)
    make_protos(chunks - 1)
    to_chips(SIDE - 1)
    pass_normed(0)
    pass_normed(1)
    pass_normed(2)
    send_protos(chunks - 1)
    landed(lx_in.at[0:LANES - 1], lx_recv)
    lost = lx_in[0]
    for k in range(1, LANES):
        lost = lost + lx_in[k]
    lz_in[row] = lost
    for dz in range(SIDE):
        for dy in range(SIDE):
            if dz or dy:
                remote(
                    lz_in.at[row], lz_in.at[row], lz_send, lz_recv, (z_peer(dz) * SIDE + y_peer(dy), me)
                )
    total = sum_normed(3)
    landed(ngy_in.at[0:SIDE - 1], m_recv)
    mine_at = core * SIDE + chip
    ng_all[mine_at] = total + ngy_in[1] + ngy_in[2] + ngy_in[3]
    for d in (4, 3, 5, 2, 6, 1, 7):
        remote(ng_all.at[mine_at], ng_all.at[mine_at], h_send, h_recv, (row, p_peer(d)))

    landed(ng_all.at[0:LANES - 1], h_recv)
    gathered = ng_all[...].reshape(B, D)
    normed_grad = jnp.zeros((B, D), F32)
    for term in split3(gathered):
        normed_grad = normed_grad + jnp.dot(back[...], term.astype(BF16), preferred_element_type=F32)
    along = jnp.sum(unit[...] * normed_grad, axis=1, keepdims=True)
    rest = normed_grad - unit[...] * along
    for h in range(D // 128):
        ge_ref[:, h * 128:(h + 1) * 128] = factor[...] * rest[:, h * 128:(h + 1) * 128]

    landed(lz_in.at[0:SIDE * SIDE - 1], lz_recv)
    lost = lz_in[0]
    for k in range(1, SIDE * SIDE):
        lost = lost + lz_in[k]
    loss_ref[0] = jnp.sum(lost) * (1.0 / (B * SIDE * SIDE))

    for k in range(chunks):
        gp_in[z, y, k] = gp_out[dims, k * span:(k + 1) * span]
    landed(gp_out.at[0:240, :], g_recv)
    for n in range(SIDE):
        for k in range(chunks):
            start = n * width + k * span
            gp_ref[:, start:start + span] = (
                gp_in[0, n, k].astype(F32) + gp_in[1, n, k].astype(F32)
                + gp_in[2, n, k].astype(F32) + gp_in[3, n, k].astype(F32)
            )
    left(protos.at[0:192, 0:span], a_send)
    left(protos.at[0:192, :], z_send)
    left(rows.at[0:3, 0:R // 2, :], r_send)
    left(rows.at[0:3, 0:R // 2, :], f_send)
    left(col_in.at[:, 0:SIDE - 1], c_send)
    left(gp_out.at[0:240, :], g_send)
    left(ng_in.at[:, 0:SIDE - 1], n_send)
    left(ngc_in, e_send)
    left(ngy_in.at[0:SIDE - 1], m_send)
    left(ng_all.at[0:LANES - 1], h_send)
    left(lx_in.at[0:LANES - 1], lx_send)
    left(lz_in.at[0:SIDE * SIDE - 1], lz_send)

    @pl.when(core == 0)
    def _():
        left(rowx_in.at[:, 0:SIDE], x_send)

    @pl.when(core == 1)
    def _():
        left(rowx_in.at[:, 0:SIDE - 1], x_send)
        left(rowx_in.at[:, 0:LANES - 1], y_send)


def body(embeddings, queue_feats, prototypes, crop_image, fill_count):
    width = prototypes.shape[1] // SIDE
    half = R // 2
    chunks = 4
    vmem = pl.BlockSpec(memory_space=pltpu.VMEM)
    smem = pl.BlockSpec(memory_space=pltpu.SMEM)
    hbm = pl.BlockSpec(memory_space=pl.ANY)
    dma = pltpu.SemaphoreType.DMA
    slab = B // LANES

    def group(*shape):
        return [dma, dma(shape) if shape else dma]

    scratch = [
        pltpu.VMEM((B, D), BF16),
        pltpu.VMEM((Q, D), BF16),
        pltpu.VMEM(prototypes.shape, BF16),
        pltpu.VMEM((1, B), jnp.int32),
        pltpu.VMEM((SIDE, R, D), BF16),
        pltpu.VMEM((D, width), BF16),
        pltpu.VMEM((SIDE, V, width), F32),
        pltpu.VMEM((SIDE, R - V, width), BF16),
        pltpu.VMEM((SIDE, V, 128), F32),
        pltpu.VMEM((SIDE, V, 128), F32),
        pltpu.VMEM((SIDE, B, width), F32),
        pltpu.VMEM((SIDE, B, width), BF16),
        pltpu.VMEM((D, SIDE * B), BF16),
        pltpu.VMEM((SIDE, B, 128), F32),
        pltpu.VMEM((8, width), F32),
        pltpu.VMEM((SIDE, Q, 128), F32),
        pltpu.VMEM((SIDE, 16, R - V), BF16),
        pltpu.VMEM((16, width), BF16),
        pltpu.VMEM((8, width), F32),
        pltpu.VMEM((ITERS, 8, width // 8), F32),
        pltpu.VMEM((ITERS, 8, half), F32),
        pltpu.VMEM((ITERS, 8, half), F32),
        pltpu.VMEM((ITERS, SIDE, 8, width // 8), F32),
        pltpu.VMEM((ITERS, LANES, 8, half), F32),
        pltpu.VMEM((ITERS, SIDE, 8, half), F32),
        pltpu.VMEM((SIDE, B, 128), F32),
        pltpu.VMEM((SIDE, B, 128), F32),
        pltpu.VMEM((B, D), F32),
        pltpu.VMEM((B, 128), F32),
        pltpu.VMEM((B, B), BF16),
        pltpu.VMEM((width, D), BF16),
        pltpu.VMEM((D, width), BF16),
        pltpu.VMEM((SIDE, SIDE, chunks, 16, width // chunks), BF16),
        pltpu.VMEM((SIDE, B, D), F32),
        pltpu.VMEM((SIDE, B // 2, D), F32),
        pltpu.VMEM((SIDE, B // 2, D), F32),
        pltpu.VMEM((SIDE, SIDE, slab, D), F32),
        pltpu.VMEM((SIDE, slab, D), F32),
        pltpu.VMEM((SIDE, slab, D), F32),
        pltpu.VMEM((LANES, slab, D), F32),
        pltpu.VMEM((LANES, 8, 128), F32),
        pltpu.VMEM((SIDE * SIDE, 8, 128), F32),
        *group(chunks, SIDE), *group(chunks), *group(SIDE), *group(SIDE),
        *group(ITERS), *group(ITERS), *group(ITERS),
        *group(), *group(SIDE), *group(SIDE), *group(), *group(), *group(), *group(), dma((4,)),
    ]
    return pl.pallas_call(
        kernel,
        name="swav",
        out_shape=(
            pltpu.VMEM((B, D), F32),
            pltpu.VMEM((prototypes.shape[0], prototypes.shape[1]), F32),
            jax.ShapeDtypeStruct((1,), F32),
        ),
        in_specs=[smem, hbm, hbm, hbm, hbm],
        out_specs=(vmem, vmem, smem),
        scratch_shapes=scratch,
        compiler_params=pltpu.CompilerParams(
            collective_id=0, has_side_effects=True, vmem_limit_bytes=60 * 1024 * 1024
        ),
    )(fill_count, embeddings, queue_feats, prototypes, crop_image.reshape(1, B))


def solution(mesh):
    placed = (P("row", None), P("row", None), P("row", "proto"), P("row"), P())
    return jax.shard_map(
        body,
        mesh=mesh,
        in_specs=placed,
        out_specs=(P("row", None), P("row", "proto"), P()),
        check_vma=False,
    )
```

```python
import functools
import math

import jax
import jax.numpy as jnp
from jax import lax
from jax.experimental import pallas as pl
from jax.experimental.pallas import tpu as pltpu
from jax.sharding import PartitionSpec as P

MESH = pl.DeviceIdType.MESH
F32 = jnp.float32
BF16 = jnp.bfloat16

CROPS = 8
ITERS = 3
SIDE = 4
LANES = 8
SCALE = 10.0 * math.log2(math.e)

B = 256
Q = 512
R = B + Q
V = 384
D = 256
TILE = 256
NT = (((1,), (1,)), ((), ()))


def iota(shape, dim):
    return lax.broadcasted_iota(jnp.int32, shape, dim)


def split3(v):
    hi = v.astype(BF16).astype(F32)
    rest = v - hi
    mid = rest.astype(BF16).astype(F32)
    return hi, mid, rest - mid


def stack16(v):
    hi, mid, low = split3(v)
    rid = iota((16, v.shape[1]), 0)
    out = jnp.where(rid == 0, hi, jnp.where(rid == 1, mid, jnp.where(rid == 2, low, 0.0)))
    return out.astype(BF16)


def unit_rows(raw):
    values = raw.astype(F32)
    inverse = lax.rsqrt(jnp.sum(values * values, axis=1, keepdims=True) + 1e-06)
    return values * inverse, inverse


def kernel(
    fill_ref, emb_hbm, queue_hbm, proto_hbm, image_hbm,
    ge_ref, gp_ref, loss_ref,
    emb_ref, queue_ref, proto_ref, image_ref, rows, protos, massf, massb, row_acc, row_wide, score, grad, turned, soft_acc, col_acc, alive, row16, col16, colb,
    col_part, row_part, row_mid, col_in, rowx_in, rowy_in,
    row_soft, row_code, unit, factor, back,
    upright, gp_out, gp_in, ng_out, ngc_in, ng_pair, ng_in, ng_sum, ngy_in, ng_all, lx_in, lz_in,
    a_send, a_recv, z_send, z_recv, r_send, r_recv, f_send, f_recv,
    c_send, c_recv, x_send, x_recv, y_send, y_recv,
    g_send, g_recv, e_send, e_recv, n_send, n_recv, m_send, m_recv, h_send, h_recv, lx_send, lx_recv, lz_send, lz_recv, in_sem,
):
    row = lax.axis_index("row")
    me = lax.axis_index("proto")
    z = row // SIDE
    y = lax.rem(row, SIDE)
    core = lax.rem(me, 2)
    chip = me // 2
    sibling = chip * 2 + (1 - core)
    width = protos.shape[1]
    tiles = width // TILE
    chunks = gp_in.shape[2]
    span = width // chunks

    def y_peer(d):
        return lax.rem(y + d, SIDE)

    def z_peer(d):
        return lax.rem(z + d, SIDE)

    def p_peer(d):
        return lax.rem(me + d, LANES)

    def remote(src, dst, send, recv, device):
        copy = pltpu.make_async_remote_copy(
            src_ref=src, dst_ref=dst, send_sem=send, recv_sem=recv,
            device_id=device, device_id_type=MESH,
        )
        copy.start()
        return copy

    def landed(ref, recv):
        pltpu.make_async_remote_copy(
            src_ref=ref, dst_ref=ref, send_sem=recv, recv_sem=recv,
            device_id=(row, sibling), device_id_type=MESH,
        ).wait_recv()

    def left(ref, send):
        pltpu.make_async_remote_copy(
            src_ref=ref, dst_ref=ref, send_sem=send, recv_sem=send,
            device_id=(row, sibling), device_id_type=MESH,
        ).wait_send()

    loads = []
    for n, (source, target) in enumerate(
        ((image_hbm, image_ref), (emb_hbm, emb_ref), (queue_hbm, queue_ref), (proto_hbm, proto_ref))
    ):
        loads.append(pltpu.make_async_copy(source, target, in_sem.at[n]))
        loads[-1].start()
    barrier = pltpu.get_barrier_semaphore()
    count = 0
    for d in range(1, SIDE):
        for peer in (z * SIDE + y_peer(d), z_peer(d) * SIDE + y):
            pl.semaphore_signal(barrier, inc=1, device_id=(peer, me), device_id_type=MESH)
            count += 1
    for d in range(1, LANES):
        pl.semaphore_signal(barrier, inc=1, device_id=(row, p_peer(d)), device_id_type=MESH)
        count += 1

    for copy in loads:
        copy.wait()
    image = image_ref[...].astype(F32)
    wide = jnp.broadcast_to(image, (B, B))
    rid, cid = iota((B, B), 0), iota((B, B), 1)
    tall = jnp.sum(jnp.where(rid == cid, wide, 0.0), axis=1, keepdims=True)
    same = jnp.where(wide == tall, 1.0, 0.0)
    base = (row * (B // CROPS)).astype(F32)
    place = jnp.sum(jnp.where(rid < cid, same, 0.0), axis=0, keepdims=True) * (B // CROPS) + (image - base)
    forward = jnp.where(rid.astype(F32) == place, 1.0, 0.0).astype(BF16)
    exact, _ = unit_rows(emb_ref[...])
    ordered = jnp.dot(forward, exact.astype(BF16), preferred_element_type=F32).astype(BF16)
    rows[y, 0:B, :] = ordered
    rows[y, B:R, :] = unit_rows(queue_ref[...])[0].astype(BF16)
    dims = pl.ds(pl.multiple_of(row * 16, 16), 16)
    protos[dims, :] = proto_ref[:, pl.ds(pl.multiple_of(y * width, width), width)]

    pl.semaphore_wait(barrier, count)

    def from_y(k, d):
        return pltpu.make_async_remote_copy(
            src_ref=protos.at[dims, k * span:(k + 1) * span],
            dst_ref=protos.at[dims, k * span:(k + 1) * span],
            send_sem=a_send, recv_sem=a_recv.at[k, d], device_id=(row, sibling), device_id_type=MESH,
        )

    for k in range(chunks):
        for d in (1, 3, 2):
            remote(
                proto_ref.at[:, pl.ds(pl.multiple_of(y_peer(d) * width + k * span, span), span)],
                protos.at[dims, k * span:(k + 1) * span], a_send, a_recv.at[k, d],
                (z * SIDE + y_peer(d), me),
            )
    shared = pl.ds(pl.multiple_of(core * (R // 2), R // 2), R // 2)
    for d in (1, 3, 2):
        remote(
            rows.at[y, shared, :], rows.at[y, shared, :], r_send, r_recv.at[d],
            (z * SIDE + y_peer(d), me),
        )
    def to_z(k, source):
        slot = lax.rem(y + SIDE - source, SIDE)
        part = protos.at[pl.ds(pl.multiple_of((z * SIDE + slot) * 16, 16), 16), k * span:(k + 1) * span]
        for d in (1, 3, 2):
            remote(part, part, z_send, z_recv.at[k], (z_peer(d) * SIDE + y, me))

    for k in range(chunks):
        to_z(k, 0)
    for k in range(chunks):
        for source in (1, 3, 2):
            from_y(k, source).wait_recv()
            to_z(k, source)

    soft_acc[...] = jnp.zeros_like(soft_acc)
    col_acc[...] = jnp.zeros_like(col_acc)
    fill = fill_ref[0]
    for slot in range(SIDE):
        place = (z * SIDE + slot) * Q + iota((Q, 128), 0)
        alive[slot] = jnp.where(place < fill, 1.0, 0.0)
    place = jnp.sum(jnp.where(cid < rid, same, 0.0), axis=1, keepdims=True) * (B // CROPS) + (tall - base)
    back[...] = jnp.where(cid.astype(F32) == place, 1.0, 0.0).astype(BF16)
    exact, inverse = unit_rows(emb_ref[...])
    unit[...] = exact
    factor[...] = jnp.broadcast_to(inverse, (B, 128))

    def score_chunk(slot, k):
        for h in range(span // TILE):
            cols = pl.ds(pl.multiple_of(k * span + h * TILE, TILE), TILE)
            total = jnp.dot(rows[slot], protos[:, cols], preferred_element_type=F32)
            crop = total[0:B] * SCALE
            score[slot, :, cols] = crop
            soft = jnp.exp2(crop)
            soft_acc[slot] += soft[:, 0:128] + soft[:, 128:256]
            code = soft * soft
            massf[slot, 0:B, cols] = code
            rest = jnp.exp2(total[B:R] * (2.0 * SCALE))
            massf[slot, B:V, cols] = rest[0:V - B]
            massb[slot, :, cols] = rest[V - B:].astype(BF16)
            live = alive[slot]
            for g in range(TILE // 128):
                lanes = slice(g * 128, (g + 1) * 128)
                part = jnp.sum(code[:, lanes].reshape(B // 8, 8, 128), axis=0)
                part = part + jnp.sum((rest[:, lanes] * live).reshape(Q // 8, 8, 128), axis=0)
                at = pl.ds(pl.multiple_of(k * span + h * TILE + g * 128, 128), 128)
                col_acc[:, at] += part

    def score_many(first_slot, slots, first_chunk, many):
        def step(i, carry):
            n = first_slot + i // many
            score_chunk(lax.rem(y + n + n // 2, SIDE), first_chunk + lax.rem(i, many))
            return carry

        lax.fori_loop(0, slots * many, step, 0)

    def z_arrived(k):
        landed(protos.at[0:192, 0:span], z_recv.at[k])

    def score_far(first_chunk, many):
        def step(i, carry):
            score_chunk(y_peer(2), first_chunk + i)
            return carry

        lax.fori_loop(0, many, step, 0)

    def hand_over(d):
        landed(rows.at[0, 0:R // 2, :], r_recv.at[d])
        slot = lax.rem(y + SIDE - d, SIDE)
        part = rows.at[slot, shared, :]
        remote(part, part, f_send, f_recv.at[d], (row, sibling))

    z_arrived(0)
    score_chunk(y, 0)
    hand_over(1)
    hand_over(3)
    z_arrived(1)
    score_chunk(y, 1)
    landed(rows.at[0, 0:R // 2, :], f_recv.at[1])
    landed(rows.at[0, 0:R // 2, :], f_recv.at[3])
    score_many(1, 2, 0, 2)
    hand_over(2)
    z_arrived(2)
    score_many(0, 3, 2, 1)
    z_arrived(3)
    score_many(0, 3, 3, 1)
    landed(rows.at[0, 0:R // 2, :], f_recv.at[2])
    score_far(0, chunks)
    for j in range(tiles):
        col_part[0, j:j + 1, :] = jnp.sum(col_acc[:, j * TILE:(j + 1) * TILE], axis=0, keepdims=True)

    def idle_work(t):
        eye = jnp.where(rid == cid, 1.0, 0.0).astype(BF16)
        if t == 0:
            for slot in range(SIDE):
                turned[:, slot * B:(slot + 1) * B] = lax.dot_general(
                    eye, rows[slot, 0:B, :], NT, preferred_element_type=F32
                ).astype(BF16)
                row_part[last, 2 * slot + 1:2 * slot + 2, 0:B] = jnp.concatenate(
                    [
                        jnp.sum(soft_acc[slot, 0:128, :].T, axis=0, keepdims=True),
                        jnp.sum(soft_acc[slot, 128:256, :].T, axis=0, keepdims=True),
                    ],
                    axis=1,
                )
                row_part[last, 2 * slot:2 * slot + 2, B:half] = jnp.ones((2, half - B), F32)
        elif t == 1:
            for j in range(tiles):
                at = slice(j * TILE, (j + 1) * TILE)
                upright[at, :] = lax.dot_general(
                    eye, protos[:, at], NT, preferred_element_type=F32
                ).astype(BF16)

    last = ITERS - 1
    half = R // 2

    def column_exchange(t):
        for d in (2, 1, 3):
            remote(
                col_part.at[t], col_in.at[t, z], c_send, c_recv.at[t], (z_peer(d) * SIDE + y, me)
            )
        col_in[t, z] = col_part[t]
        idle_work(t)
        landed(col_in.at[t, 0:SIDE - 1], c_recv.at[t])
        column = 1.0 / (col_in[t, 0] + col_in[t, 1] + col_in[t, 2] + col_in[t, 3])
        for j in range(tiles):
            col16[:, j * TILE:(j + 1) * TILE] = stack16(column[j:j + 1, :])
            colb[:, j * TILE:(j + 1) * TILE] = jnp.broadcast_to(column[j:j + 1, :], (8, TILE))

    def row_exchange(t):
        for d in (2, 1, 3):
            remote(
                row_part.at[t], rowx_in.at[t, me], x_send, x_recv.at[t],
                (row, lax.rem(chip + d, SIDE) * 2 + 1),
            )

        @pl.when(core == 0)
        def _():
            remote(row_part.at[t], rowx_in.at[t, me], x_send, x_recv.at[t], (row, sibling))
            landed(rowy_in.at[t], y_recv.at[t])

        @pl.when(core == 1)
        def _():
            rowx_in[t, me] = row_part[t]
            landed(rowx_in.at[t, 0:LANES - 1], x_recv.at[t])
            total = rowx_in[t, 0]
            for k in range(1, LANES):
                total = total + rowx_in[t, k]
            row_mid[t] = total
            for d, c in ((2, 0), (2, 1), (1, 0), (1, 1), (3, 0), (3, 1), (0, 0)):
                remote(
                    row_mid.at[t], rowy_in.at[t, y], y_send, y_recv.at[t],
                    (z * SIDE + y_peer(d), chip * 2 + c),
                )
            rowy_in[t, y] = total
            landed(rowy_in.at[t, 0:SIDE - 1], y_recv.at[t])

        return rowy_in[t, 0] + rowy_in[t, 1] + rowy_in[t, 2] + rowy_in[t, 3]

    def row_sums(slot, many):
        for g in range(many // 8):
            at = slice(g * 8, g * 8 + 8)
            sums = [None, None]
            for n in range(width // 128):
                lanes = slice(n * 128, (n + 1) * 128)
                term = massf[slot, at, lanes] * colb[:, lanes]
                sums[n % 2] = term if sums[n % 2] is None else sums[n % 2] + term
            row_acc[slot, at, :] = sums[0] + sums[1]

    def turn(slot, b):
        return jnp.sum(row_acc[slot, b * 128:(b + 1) * 128, :].T, axis=0, keepdims=True)

    rid8, lane8 = iota((8, half), 0), iota((8, half), 1)
    spot = lax.rem(rid8, 2) * half + lane8
    queue_row = (z * SIDE + rid8 // 2) * Q + spot - B
    live = jnp.where(jnp.logical_or(spot < B, queue_row < fill), 1.0, 0.0)

    for t in range(ITERS):
        column_exchange(t)
        if t + 1 == ITERS:
            break

        def row_block(slot, carry, t=t):
            row_sums(slot, V)
            rest = lax.dot_general(col16[...], massb[slot], NT, preferred_element_type=F32)
            rest = jnp.sum(rest, axis=0, keepdims=True)
            parts = [turn(slot, b) for b in range(V // 128)]
            parts += [rest[:, b * 128:(b + 1) * 128] for b in range((R - V) // 128)]
            for h in range(2):
                row_part[t, pl.ds(2 * slot + h, 1), :] = jnp.concatenate(parts[3 * h:3 * h + 3], axis=1)
            return carry

        lax.fori_loop(0, SIDE, row_block, 0)
        weight = live / row_exchange(t)
        for slot in range(SIDE):
            row16[slot] = stack16(weight[2 * slot + 1:2 * slot + 2, V - half:half])
            for b in range(V // 128):
                at = slice((b % 3) * 128, (b % 3 + 1) * 128)
                line = weight[2 * slot + b // 3:2 * slot + b // 3 + 1, at]
                row_wide[slot, b * 128:(b + 1) * 128, :] = jnp.broadcast_to(line, (128, 128)).T

        def column_block(slot, sums):
            rest = jnp.dot(row16[slot], massb[slot], preferred_element_type=F32)
            sums = list(sums)
            for g in range(V // 8):
                at = slice(g * 8, g * 8 + 8)
                scale = row_wide[slot, at, :]
                for n in range(width // 128):
                    sums[n] = sums[n] + massf[slot, at, n * 128:(n + 1) * 128] * scale
            return tuple(sums[n] + rest[0:8, n * 128:(n + 1) * 128] for n in range(width // 128))

        sums = lax.fori_loop(
            0, SIDE, column_block, tuple(jnp.zeros((8, 128), F32) for _ in range(width // 128))
        )
        for n in range(width // 128):
            at = slice((n % 2) * 128, (n % 2 + 1) * 128)
            col_part[t + 1, n // 2:n // 2 + 1, at] = jnp.sum(sums[n], axis=0, keepdims=True)

    for slot in range(SIDE):
        row_sums(slot, B)
        for b in range(B // 128):
            row_part[last, 2 * slot:2 * slot + 1, b * 128:(b + 1) * 128] = turn(slot, b)
    sums = row_exchange(last)
    for slot in range(SIDE):
        code = sums[2 * slot:2 * slot + 1, 0:B]
        soft = sums[2 * slot + 1:2 * slot + 2, 0:B]
        for target, value in ((row_code, (10.0 / (CROPS - 1)) / code), (row_soft, 10.0 / soft)):
            for h in range(2):
                target[slot, h * 128:(h + 1) * 128, :] = jnp.broadcast_to(
                    value[:, h * 128:(h + 1) * 128], (128, 128)
                ).T
    sublane = iota((8, B), 0)
    logs = jnp.log(sums[:, 0:B])
    mine = jnp.logical_and(sublane == 2 * y + 1, me == 0)
    logs = jnp.where(mine, logs, 0.0)
    logs = logs[:, 0:128] + logs[:, 128:256]

    images = B // CROPS
    slab = B // LANES

    def slope_chunk(slot, k, lost):
        for h in range(span // 128):
            lanes = pl.ds(pl.multiple_of(k * span + h * 128, 128), 128)
            column = colb[:, lanes]
            for i in range(images // 8):
                softs, parts, scores = [], [], []
                for c in range(CROPS):
                    at = slice(c * images + i * 8, c * images + i * 8 + 8)
                    s = score[slot, at, lanes]
                    e = jnp.exp2(s)
                    parts.append(e * e * column * row_code[slot, at, :])
                    softs.append(e * row_soft[slot, at, :])
                    scores.append(s)
                total = parts[0]
                for c in range(1, CROPS):
                    total = total + parts[c]
                for c in range(CROPS):
                    at = slice(c * images + i * 8, c * images + i * 8 + 8)
                    goal = total - parts[c]
                    lost = lost + goal * scores[c]
                    grad[slot, at, lanes] = (softs[c] - goal).astype(BF16)
        return lost

    side = B // 2
    own_half = pl.ds(pl.multiple_of(core * side, side), side)
    other_half = pl.ds(pl.multiple_of((1 - core) * side, side), side)

    def to_sibling(n):
        remote(ng_out.at[n, other_half, :], ngc_in.at[n], e_send, e_recv.at[n], (row, sibling))

    def to_chips(n):
        landed(ngc_in.at[n], e_recv.at[n])
        ng_pair[n] = ng_out[n, own_half, :] + ngc_in[n]
        for d in (2, 1, 3):
            to_chip = lax.rem(chip + d, SIDE)
            remote(
                ng_pair.at[n, pl.ds(pl.multiple_of(to_chip * slab, slab), slab), :],
                ng_in.at[n, chip], n_send, n_recv.at[n], (row, to_chip * 2 + core),
            )
        ng_in[n, chip] = ng_pair[n, pl.ds(pl.multiple_of(chip * slab, slab), slab), :]

    def sum_normed(n):
        landed(ng_in.at[n, 0:SIDE - 1], n_recv.at[n])
        return ng_in[n, 0] + ng_in[n, 1] + ng_in[n, 2] + ng_in[n, 3]

    def make_protos(k):
        for h in range(span // TILE):
            cols = slice(k * span + h * TILE, k * span + (h + 1) * TILE)
            part = jnp.dot(turned[:, 0:B], grad[0, :, cols], preferred_element_type=F32)
            for other in range(1, SIDE):
                part = part + jnp.dot(
                    turned[:, other * B:(other + 1) * B], grad[other, :, cols],
                    preferred_element_type=F32,
                )
            gp_out[:, cols] = part.astype(BF16)

    def send_protos(k):
        for dz, dy in (
            (2, 2), (2, 1), (2, 3), (1, 2), (3, 2), (1, 1), (1, 3), (3, 1), (3, 3),
            (2, 0), (0, 2), (1, 0), (3, 0), (0, 1), (0, 3),
        ):
            peer = z_peer(dz) * SIDE + y_peer(dy)
            remote(
                gp_out.at[pl.ds(pl.multiple_of(peer * 16, 16), 16), k * span:(k + 1) * span],
                gp_in.at[z, y, k], g_send, g_recv, (peer, me),
            )

    def pass_normed(n):
        ng_sum[n] = sum_normed(n)
        d = order[n]
        remote(ng_sum.at[n], ngy_in.at[d], m_send, m_recv, (z * SIDE + y_peer(d), me))

    order = (2, 1, 3, 0)
    lost = jnp.zeros((8, 128), F32)
    for k in range(chunks):
        lost = lax.fori_loop(0, SIDE, lambda slot, lost, k=k: slope_chunk(slot, k, lost), lost)
        if k + 2 < chunks:
            make_protos(k)
            send_protos(k)
    lx_in[me] = logs - lost * (math.log(2.0) / 10.0)
    for d in range(1, LANES):
        remote(lx_in.at[me], lx_in.at[me], lx_send, lx_recv, (row, p_peer(d)))
    for n in range(SIDE):
        ng_out[n] = jnp.dot(grad[y_peer(order[n])], upright[...], preferred_element_type=F32)
        to_sibling(n)
        if n:
            to_chips(n - 1)
        if n == 1:
            make_protos(chunks - 2)
            send_protos(chunks - 2)
    make_protos(chunks - 1)
    to_chips(SIDE - 1)
    pass_normed(0)
    pass_normed(1)
    pass_normed(2)
    send_protos(chunks - 1)
    landed(lx_in.at[0:LANES - 1], lx_recv)
    lost = lx_in[0]
    for k in range(1, LANES):
        lost = lost + lx_in[k]
    lz_in[row] = lost
    for dz in range(SIDE):
        for dy in range(SIDE):
            if dz or dy:
                remote(
                    lz_in.at[row], lz_in.at[row], lz_send, lz_recv, (z_peer(dz) * SIDE + y_peer(dy), me)
                )
    total = sum_normed(3)
    landed(ngy_in.at[0:SIDE - 1], m_recv)
    mine_at = core * SIDE + chip
    ng_all[mine_at] = total + ngy_in[1] + ngy_in[2] + ngy_in[3]
    for d in (4, 3, 5, 2, 6, 1, 7):
        remote(ng_all.at[mine_at], ng_all.at[mine_at], h_send, h_recv, (row, p_peer(d)))

    landed(ng_all.at[0:LANES - 1], h_recv)
    gathered = ng_all[...].reshape(B, D)
    normed_grad = jnp.zeros((B, D), F32)
    for term in split3(gathered):
        normed_grad = normed_grad + jnp.dot(back[...], term.astype(BF16), preferred_element_type=F32)
    along = jnp.sum(unit[...] * normed_grad, axis=1, keepdims=True)
    rest = normed_grad - unit[...] * along
    for h in range(D // 128):
        ge_ref[:, h * 128:(h + 1) * 128] = factor[...] * rest[:, h * 128:(h + 1) * 128]

    landed(lz_in.at[0:SIDE * SIDE - 1], lz_recv)
    lost = lz_in[0]
    for k in range(1, SIDE * SIDE):
        lost = lost + lz_in[k]
    loss_ref[0] = jnp.sum(lost) * (1.0 / (B * SIDE * SIDE))

    for k in range(chunks):
        gp_in[z, y, k] = gp_out[dims, k * span:(k + 1) * span]
    landed(gp_out.at[0:240, :], g_recv)
    for n in range(SIDE):
        for k in range(chunks):
            start = n * width + k * span
            gp_ref[:, start:start + span] = (
                gp_in[0, n, k].astype(F32) + gp_in[1, n, k].astype(F32)
                + gp_in[2, n, k].astype(F32) + gp_in[3, n, k].astype(F32)
            )
    left(protos.at[0:192, 0:span], a_send)
    left(protos.at[0:192, :], z_send)
    left(rows.at[0:3, 0:R // 2, :], r_send)
    left(rows.at[0:3, 0:R // 2, :], f_send)
    left(col_in.at[:, 0:SIDE - 1], c_send)
    left(gp_out.at[0:240, :], g_send)
    left(ng_in.at[:, 0:SIDE - 1], n_send)
    left(ngc_in, e_send)
    left(ngy_in.at[0:SIDE - 1], m_send)
    left(ng_all.at[0:LANES - 1], h_send)
    left(lx_in.at[0:LANES - 1], lx_send)
    left(lz_in.at[0:SIDE * SIDE - 1], lz_send)

    @pl.when(core == 0)
    def _():
        left(rowx_in.at[:, 0:SIDE], x_send)

    @pl.when(core == 1)
    def _():
        left(rowx_in.at[:, 0:SIDE - 1], x_send)
        left(rowx_in.at[:, 0:LANES - 1], y_send)


def body(embeddings, queue_feats, prototypes, crop_image, fill_count):
    width = prototypes.shape[1] // SIDE
    half = R // 2
    chunks = 4
    vmem = pl.BlockSpec(memory_space=pltpu.VMEM)
    smem = pl.BlockSpec(memory_space=pltpu.SMEM)
    hbm = pl.BlockSpec(memory_space=pl.ANY)
    dma = pltpu.SemaphoreType.DMA
    slab = B // LANES

    def group(*shape):
        return [dma, dma(shape) if shape else dma]

    scratch = [
        pltpu.VMEM((B, D), BF16),
        pltpu.VMEM((Q, D), BF16),
        pltpu.VMEM(prototypes.shape, BF16),
        pltpu.VMEM((1, B), jnp.int32),
        pltpu.VMEM((SIDE, R, D), BF16),
        pltpu.VMEM((D, width), BF16),
        pltpu.VMEM((SIDE, V, width), F32),
        pltpu.VMEM((SIDE, R - V, width), BF16),
        pltpu.VMEM((SIDE, V, 128), F32),
        pltpu.VMEM((SIDE, V, 128), F32),
        pltpu.VMEM((SIDE, B, width), F32),
        pltpu.VMEM((SIDE, B, width), BF16),
        pltpu.VMEM((D, SIDE * B), BF16),
        pltpu.VMEM((SIDE, B, 128), F32),
        pltpu.VMEM((8, width), F32),
        pltpu.VMEM((SIDE, Q, 128), F32),
        pltpu.VMEM((SIDE, 16, R - V), BF16),
        pltpu.VMEM((16, width), BF16),
        pltpu.VMEM((8, width), F32),
        pltpu.VMEM((ITERS, 8, width // 8), F32),
        pltpu.VMEM((ITERS, 8, half), F32),
        pltpu.VMEM((ITERS, 8, half), F32),
        pltpu.VMEM((ITERS, SIDE, 8, width // 8), F32),
        pltpu.VMEM((ITERS, LANES, 8, half), F32),
        pltpu.VMEM((ITERS, SIDE, 8, half), F32),
        pltpu.VMEM((SIDE, B, 128), F32),
        pltpu.VMEM((SIDE, B, 128), F32),
        pltpu.VMEM((B, D), F32),
        pltpu.VMEM((B, 128), F32),
        pltpu.VMEM((B, B), BF16),
        pltpu.VMEM((width, D), BF16),
        pltpu.VMEM((D, width), BF16),
        pltpu.VMEM((SIDE, SIDE, chunks, 16, width // chunks), BF16),
        pltpu.VMEM((SIDE, B, D), F32),
        pltpu.VMEM((SIDE, B // 2, D), F32),
        pltpu.VMEM((SIDE, B // 2, D), F32),
        pltpu.VMEM((SIDE, SIDE, slab, D), F32),
        pltpu.VMEM((SIDE, slab, D), F32),
        pltpu.VMEM((SIDE, slab, D), F32),
        pltpu.VMEM((LANES, slab, D), F32),
        pltpu.VMEM((LANES, 8, 128), F32),
        pltpu.VMEM((SIDE * SIDE, 8, 128), F32),
        *group(chunks, SIDE), *group(chunks), *group(SIDE), *group(SIDE),
        *group(ITERS), *group(ITERS), *group(ITERS),
        *group(), *group(SIDE), *group(SIDE), *group(), *group(), *group(), *group(), dma((4,)),
    ]
    return pl.pallas_call(
        kernel,
        name="swav",
        out_shape=(
            pltpu.VMEM((B, D), F32),
            pltpu.VMEM((prototypes.shape[0], prototypes.shape[1]), F32),
            pltpu.SMEM((1,), F32),
        ),
        in_specs=[smem, hbm, hbm, hbm, hbm],
        out_specs=(vmem, vmem, smem),
        scratch_shapes=scratch,
        compiler_params=pltpu.CompilerParams(
            collective_id=0, has_side_effects=True, vmem_limit_bytes=60 * 1024 * 1024
        ),
    )(fill_count, embeddings, queue_feats, prototypes, crop_image.reshape(1, B))


def solution(mesh):
    placed = (P("row", None), P("row", None), P("row", "proto"), P("row"), P())
    return jax.shard_map(
        body,
        mesh=mesh,
        in_specs=placed,
        out_specs=(P("row", None), P("row", "proto"), P()),
        check_vma=False,
    )
```
